256 devices in a mesh: row: 32 (over z_lo, x, core), col: 8 (over z_hi, y).
Axes of the slice: x: 4, y: 4, z: 8 (z_hi: 2, z_lo: 4; z = z_hi * 4 + z_lo), core: 2. Of those that a mesh axis runs over, the one named last changes fastest.
Arguments:
- sequence_embedding: float32 [128, 512, 256], P('row', 'col'), may hold values from -6 to 6
- standardize_scale: float32 [256], replicated, may hold values from 0.25 to 1.75
- standardize_offset: float32 [256], replicated, may hold values from -0.5 to 0.5
- first_operand_matrix: float32 [256, 32], replicated, may hold values from -0.375 to 0.375
- first_operand_intercept: float32 [32], replicated, may hold values from -0.5 to 0.5
- second_operand_matrix: float32 [256, 32], replicated, may hold values from -0.375 to 0.375
- second_operand_intercept: float32 [32], replicated, may hold values from -0.5 to 0.5
- result_matrix: float32 [1024, 128], replicated, may hold values from -2 to 2
- result_intercept: float32 [128], replicated, may hold values from -0.5 to 0.5
- edge_incoming_sensitivity: float32 [512, 512, 128], P('row', 'col'), may hold values from -6 to 6
Outputs:
- pair_output_update: float32 [512, 512, 128], P('row', 'col')
- alignment_gradient: float32 [128, 512, 256], P('row', 'col')
- projection_gradient: float32 [1024, 128], P(('row', 'col'))
The draws below stay inside these ranges and needn't reach their ends.
All inputs are finite; a program needn't handle non-finite values.
Results may differ from the reference program's by a relative error of at most 0.0001.
Values sent between devices are 32-bit elements; how exact they have to be, the bound alone decides.
No kernel may reach another device: no remote copies, remote signals or barrier semaphores. Data moves between devices by JAX's collectives and lax.ppermute only.
A program may use at most 64 MiB of HBM per device.

```python
import math
import jax
import jax.numpy as jnp
from jax import lax

SEQUENCE_FEATS = 256
HIDDEN_WIDTH = 32
EDGE_FEATURES = 128
SEQUENCE_COUNT = 128
SEQUENCE_SPAN = 512


def block_scale(key, extent, pieces, smallest, high):
    def one(axis_at, blocks):
        heights = jax.random.uniform(jax.random.fold_in(jax.random.fold_in(key, 6), axis_at), (blocks,), jnp.float32, smallest / len(pieces), high / len(pieces))
        return jnp.repeat(jnp.exp(heights), extent[axis_at] // blocks).reshape((-1,) + (1,) * (len(extent) - axis_at - 1))

    loudness = one(*pieces[0])
    for cut in pieces[1:]:
        loudness = loudness * one(*cut)
    return loudness


def bell_draw(stream_key, shape, width, bound, shards=(), held_as=jnp.bfloat16):
    drawn = jax.random.normal(stream_key, shape, jnp.float32) * width
    if len(shards) > 0:
        drawn = block_scale(stream_key, shape, shards, -0.22, 0.18) * drawn
    return jnp.clip(drawn, min=-bound, max=bound).astype(held_as)


def setup_inputs(seed: int = 0) -> dict:
    splits = jax.random.split(jax.random.key(seed), 11)
    sequence_embedding = bell_draw(splits[0], (SEQUENCE_COUNT, SEQUENCE_SPAN, SEQUENCE_FEATS), 1.0, 6.0, ((0, 32), (1, 8)), jnp.float32)
    standardize_scale = jnp.clip(1.0 + 0.15 * jax.random.normal(splits[1], (SEQUENCE_FEATS,), jnp.float32), 0.25, 1.75)
    standardize_offset = jnp.clip(jax.random.uniform(splits[2], (SEQUENCE_FEATS,), jnp.float32, -0.5, 0.5), -0.5, 0.5)
    first_operand_matrix = bell_draw(splits[3], (SEQUENCE_FEATS, HIDDEN_WIDTH), SEQUENCE_FEATS ** -0.5, 0.375, (), jnp.float32)
    first_operand_intercept = jnp.clip(jax.random.uniform(splits[4], (HIDDEN_WIDTH,), jnp.float32, -0.5, 0.5), -0.5, 0.5)
    second_operand_matrix = bell_draw(splits[5], (SEQUENCE_FEATS, HIDDEN_WIDTH), SEQUENCE_FEATS ** -0.5, 0.375, (), jnp.float32)
    second_operand_intercept = jnp.clip(jax.random.uniform(splits[6], (HIDDEN_WIDTH,), jnp.float32, -0.5, 0.5), -0.5, 0.5)
    result_matrix = bell_draw(splits[7], (HIDDEN_WIDTH * HIDDEN_WIDTH, EDGE_FEATURES), (HIDDEN_WIDTH * HIDDEN_WIDTH // SEQUENCE_COUNT) ** -0.5, 2.0, (), jnp.float32)
    result_intercept = jnp.clip(jax.random.uniform(splits[8], (EDGE_FEATURES,), jnp.float32, -0.5, 0.5), -0.5, 0.5)
    edge_incoming_sensitivity = bell_draw(splits[9], (SEQUENCE_SPAN, SEQUENCE_SPAN, EDGE_FEATURES), 1.0, 6.0, ((0, 32), (1, 8)), jnp.float32)
    return dict(sequence_embedding=sequence_embedding, standardize_scale=standardize_scale, standardize_offset=standardize_offset, first_operand_matrix=first_operand_matrix, first_operand_intercept=first_operand_intercept, second_operand_matrix=second_operand_matrix, second_operand_intercept=second_operand_intercept, result_matrix=result_matrix, result_intercept=result_intercept, edge_incoming_sensitivity=edge_incoming_sensitivity)


precise = lax.Precision.HIGHEST

def linear_transform(sequence_embedding, standardize_scale, standardize_offset, first_operand_matrix, first_operand_intercept, second_operand_matrix, second_operand_intercept):
    average_feature = lax.optimization_barrier(jnp.mean(sequence_embedding, axis=-1, keepdims=True))
    demeaned_features = sequence_embedding - average_feature
    variance = lax.optimization_barrier(jnp.mean(demeaned_features * demeaned_features, axis=-1, keepdims=True))
    normed = demeaned_features * lax.rsqrt(variance + 1e-05) * standardize_scale + standardize_offset
    first_operand_entries = jnp.einsum('src,cd->srd', normed, first_operand_matrix, precision=precise) + first_operand_intercept
    second_operand_entries = jnp.einsum('src,cd->srd', normed, second_operand_matrix, precision=precise) + second_operand_intercept
    return (first_operand_entries, second_operand_entries)

def tile_work(left_all, right_all, result_matrix, result_intercept, edge_incoming_sensitivity):
    rows_all, tile_i, chans = left_all.shape
    tile_j = right_all.shape[1]
    pair_ch = result_matrix.shape[1]
    block_rows = math.gcd(tile_i, 8)
    num_blocks = tile_i // block_rows
    left_blocks = left_all.reshape(rows_all, num_blocks, block_rows, chans).transpose(1, 0, 2, 3)
    cot_blocks = edge_incoming_sensitivity.reshape(num_blocks, block_rows, tile_j, pair_ch)

    def tile_step(carry, inputs):
        summed_weight, right_sum = carry
        left_blk, cot_blk = inputs
        products = jnp.einsum('sic,sje->ijce', left_blk, right_all, precision=precise)
        products = products.reshape(block_rows, tile_j, chans * chans)
        pair_blk = jnp.einsum('ijk,kh->ijh', products, result_matrix, precision=precise) / rows_all + result_intercept
        grad_outer = jnp.einsum('ijh,kh->ijk', cot_blk, result_matrix, precision=precise) / rows_all
        grad_outer = grad_outer.reshape(block_rows, tile_j, chans, chans)
        summed_weight = summed_weight + jnp.einsum('ijk,ijh->kh', products, cot_blk, precision=precise)
        left_factor_gradient = jnp.einsum('ijce,sje->sic', grad_outer, right_all, precision=precise)
        right_sum = right_sum + jnp.einsum('sic,ijce->sje', left_blk, grad_outer, precision=precise)
        return ((summed_weight, right_sum), (pair_blk, left_factor_gradient))
    initial = (jnp.zeros((chans * chans, pair_ch), jnp.float32), jnp.zeros(right_all.shape, jnp.float32))
    (summed_weight, right_sum), (pair_blocks, left_grads) = lax.scan(tile_step, initial, (left_blocks, cot_blocks))
    pair_tile = pair_blocks.reshape(tile_i, tile_j, pair_ch)
    left_factor_gradient = left_grads.transpose(1, 0, 2, 3).reshape(rows_all, tile_i, chans)
    return (pair_tile, left_factor_gradient, summed_weight, right_sum)

def reference(sequence_embedding, standardize_scale, standardize_offset, first_operand_matrix, first_operand_intercept, second_operand_matrix, second_operand_intercept, result_matrix, result_intercept, edge_incoming_sensitivity):

    def device_portion(values):
        return linear_transform(values, standardize_scale, standardize_offset, first_operand_matrix, first_operand_intercept, second_operand_matrix, second_operand_intercept)
    (first_operand_entries, second_operand_entries), reverse_derivative = jax.vjp(device_portion, sequence_embedding)
    pair_output_update, left_factor_gradient, summed_weight, right_factor_gradient = tile_work(first_operand_entries, second_operand_entries, result_matrix, result_intercept, edge_incoming_sensitivity)
    alignment_gradient = reverse_derivative((left_factor_gradient, right_factor_gradient))[0]
    return (pair_output_update, alignment_gradient, summed_weight / SEQUENCE_SPAN)
```

```python
import math

import jax
import jax.numpy as jnp
from jax import lax
from jax.sharding import PartitionSpec as P

precise = lax.Precision.HIGHEST
fast = lax.Precision.HIGH


def laid_out(pieces, dim):
    pieces = jnp.moveaxis(pieces, 0, dim)
    dims = pieces.shape
    return pieces.reshape(*dims[:dim], dims[dim] * dims[dim + 1], *dims[dim + 2 :])


def copy_for_each(array, axis):
    peers = lax.axis_size(axis)
    return lax.all_to_all(
        jnp.broadcast_to(array[None], (peers, *array.shape)), axis, 0, 0, tiled=True
    )


def gathered_copies(array, axis, dim):
    return laid_out(copy_for_each(array, axis), dim)


def in_blocks(array, dim, peers):
    before, after = (array.shape[:dim], array.shape[dim + 1 :])
    return jnp.moveaxis(array.reshape(*before, peers, -1, *after), dim, 0)


def sum_at_owner(array, axis, dim):
    pieces = in_blocks(array, dim, lax.axis_size(axis))
    arrived = lax.all_to_all(pieces, axis, split_axis=0, concat_axis=0, tiled=True)
    return arrived.sum(axis=0)


def linear_transform(
    sequence_embedding,
    standardize_scale,
    standardize_offset,
    first_operand_matrix,
    first_operand_intercept,
    second_operand_matrix,
    second_operand_intercept,
):
    average_feature = jnp.mean(sequence_embedding, axis=-1, keepdims=True)
    demeaned_features = sequence_embedding - average_feature
    variance = jnp.mean(demeaned_features * demeaned_features, axis=-1, keepdims=True)
    normed = (
        demeaned_features * lax.rsqrt(variance + 1e-05) * standardize_scale + standardize_offset
    )
    first_operand_entries = (
        jnp.einsum("src,cd->srd", normed, first_operand_matrix, precision=precise)
        + first_operand_intercept
    )
    second_operand_entries = (
        jnp.einsum("src,cd->srd", normed, second_operand_matrix, precision=precise)
        + second_operand_intercept
    )
    return (first_operand_entries, second_operand_entries)


def tile_work(left_all, right_all, result_matrix, result_intercept, edge_incoming_sensitivity):
    rows_all, tile_i, chans = left_all.shape
    tile_j = right_all.shape[1]
    pair_ch = result_matrix.shape[1]
    block_rows = math.gcd(tile_i, 8)
    num_blocks = tile_i // block_rows
    left_blocks = left_all.reshape(rows_all, num_blocks, block_rows, chans).transpose(1, 0, 2, 3)
    cot_blocks = edge_incoming_sensitivity.reshape(num_blocks, block_rows, tile_j, pair_ch)

    def tile_step(carry, inputs):
        summed_weight, right_sum = carry
        left_blk, cot_blk = inputs
        products = jnp.einsum("sic,sje->ijce", left_blk, right_all, precision=fast)
        products = products.reshape(block_rows, tile_j, chans * chans)
        pair_blk = (
            jnp.einsum("ijk,kh->ijh", products, result_matrix, precision=fast) / rows_all
            + result_intercept
        )
        grad_outer = jnp.einsum("ijh,kh->ijk", cot_blk, result_matrix, precision=fast) / rows_all
        grad_outer = grad_outer.reshape(block_rows, tile_j, chans, chans)
        summed_weight = summed_weight + jnp.einsum(
            "ijk,ijh->kh", products, cot_blk, precision=fast
        )
        left_factor_gradient = jnp.einsum("ijce,sje->sic", grad_outer, right_all, precision=fast)
        right_sum = right_sum + jnp.einsum("sic,ijce->sje", left_blk, grad_outer, precision=fast)
        return ((summed_weight, right_sum), (pair_blk, left_factor_gradient))

    initial = (
        jnp.zeros((chans * chans, pair_ch), jnp.float32),
        jnp.zeros(right_all.shape, jnp.float32),
    )
    (summed_weight, right_sum), (pair_blocks, left_grads) = lax.scan(
        tile_step, initial, (left_blocks, cot_blocks)
    )
    pair_tile = pair_blocks.reshape(tile_i, tile_j, pair_ch)
    left_factor_gradient = left_grads.transpose(1, 0, 2, 3).reshape(rows_all, tile_i, chans)
    return (pair_tile, left_factor_gradient, summed_weight, right_sum)


def local(
    sequence_embedding,
    standardize_scale,
    standardize_offset,
    first_operand_matrix,
    first_operand_intercept,
    second_operand_matrix,
    second_operand_intercept,
    result_matrix,
    result_intercept,
    edge_incoming_sensitivity,
):

    def device_portion(values):
        return linear_transform(
            values,
            standardize_scale,
            standardize_offset,
            first_operand_matrix,
            first_operand_intercept,
            second_operand_matrix,
            second_operand_intercept,
        )

    (first_operand_portion, second_operand_portion), reverse_derivative = jax.vjp(
        device_portion, sequence_embedding
    )
    col_count = lax.axis_size("col")
    right_all = gathered_copies(second_operand_portion, "row", 0)
    widened = gathered_copies(first_operand_portion, "col", 1)
    left_all = lax.all_to_all(widened, "row", split_axis=1, concat_axis=0, tiled=True)
    pair_output_update, left_factor_gradient, summed_weight, right_sum = tile_work(
        left_all, right_all, result_matrix, result_intercept, edge_incoming_sensitivity
    )
    swapped = lax.all_to_all(left_factor_gradient, "row", split_axis=0, concat_axis=1, tiled=True)
    left_backprop = sum_at_owner(swapped, "col", 1)
    right_backprop = sum_at_owner(right_sum, "row", 0)
    alignment_gradient = reverse_derivative((left_backprop, right_backprop))[0]
    res_total = right_all.shape[1] * col_count
    projection_gradient = (
        sum_at_owner(sum_at_owner(summed_weight, "row", 0), "col", 0) / res_total
    )
    return (pair_output_update, alignment_gradient, projection_gradient)


def solution(mesh):
    return jax.shard_map(
        local,
        mesh=mesh,
        in_specs=(
            P("row", "col", None),
            P(),
            P(),
            P(),
            P(),
            P(),
            P(),
            P(),
            P(),
            P("row", "col", None),
        ),
        out_specs=(P("row", "col", None), P("row", "col", None), P(("row", "col"), None)),
        check_vma=False,
    )
```

```python
import functools

import jax
import jax.numpy as jnp
from jax import lax
from jax.experimental import pallas as pl
from jax.experimental.pallas import tpu as pltpu
from jax.sharding import Mesh, PartitionSpec as P

exact = lax.Precision.HIGHEST
f32 = jnp.float32
bf16 = jnp.bfloat16

SIZES = (4, 4, 2, 2, 4)
NAMES = ("zl", "x", "core", "zh", "y")
CHIP = ("zl", "x")
ROW = ("zl", "x", "core")
COL = ("zh", "y")
VMEM = pl.BlockSpec(memory_space=pltpu.VMEM)

FWD = 96
BWD = 112


def contract(a, b, dims):
    return lax.dot_general(a, b, (dims, ((), ())), precision=exact, preferred_element_type=f32)


def matmul(a, b):
    return lax.dot_general(a, b, (((1,), (0,)), ((), ())), preferred_element_type=f32)


def halves(v):
    high = v.astype(bf16)
    return high, (v - high.astype(f32)).astype(bf16)


def standardized(x):
    demeaned = x - jnp.mean(x, axis=-1, keepdims=True)
    variance = jnp.mean(demeaned * demeaned, axis=-1, keepdims=True)
    inverse = lax.rsqrt(variance + 1e-05)
    return demeaned * inverse, inverse


def project_kernel(x_ref, scale_ref, offset_ref, w1_ref, b1_ref, w2_ref, b2_ref, left_ref, right_ref, tmp):
    core = lax.axis_index("core")
    normed = standardized(x_ref[...])[0] * scale_ref[...] + offset_ref[...]
    tmp[:, 0:32] = contract(normed, w1_ref[...], ((1,), (1,))) + b1_ref[...]
    wide = jnp.concatenate([tmp[pl.ds(u, 64, stride=4), :][:, 0:32] for u in range(4)], axis=1)
    for s in range(4):
        for q in range(4):
            left_ref[q // 2, lax.rem(q % 2 + core, 2), s * 4 : s * 4 + 4, :] = wide[
                s * 16 + q * 4 : s * 16 + q * 4 + 4
            ]
    right = contract(w2_ref[...], normed, ((1,), (1,))) + b2_ref[...]
    for s in range(4):
        cols = right[:, s * 64 : s * 64 + 64]
        right_ref[s * 16 : s * 16 + 16, :] = jnp.concatenate([cols[0:16], cols[16:32]], axis=1)


def pick(parts, chunk):
    low = jnp.where(chunk == 0, parts[0], parts[1])
    return jnp.where(chunk < 2, low, jnp.where(chunk == 2, parts[2], parts[3]))


def tile_kernel(
    own_ref, other_ref, w_ref, bias_ref, cot_ref,
    pair_ref, own_out, other_out,
    l_ref, lcat, lt, r_hl, rt, wide_t, a_hi, a_lo, w_hl, w_cat, cot_cat, cot_t, g_hi, g_lo, dw,
):
    core = lax.axis_index("core")
    chunk = lax.broadcasted_iota(jnp.int32, (64, 128), 1) // 32
    sides = ((own_ref, FWD, 32), (other_ref, FWD - 16, 16))

    def rows(row, right):
        got = []
        for ref, pitch, base in sides:
            for s in range(4):
                at = base + s * 16 + row if right else s * 4 + row
                got.append(ref[pl.ds(at, 16, stride=pitch), :])
        return jnp.concatenate(got, axis=0)

    for e in range(32):
        hi, lo = halves(w_ref[pl.ds(e, 32, stride=32), :])
        for d in range(4):
            at = (e // 4) * 128 + ((e % 4 + d) % 4) * 32
            w_hl[d, at : at + 32, 0:128] = hi
            w_hl[d, at : at + 32, 128:256] = lo
    for d in range(4):
        for quad in range(4):
            v = cot_ref[quad * 4 + d]
            hi, lo = halves(v)
            cot_cat[d, quad * 64 : quad * 64 + 64, 0:128] = hi
            cot_cat[d, quad * 64 : quad * 64 + 64, 128:256] = hi
            cot_cat[d, quad * 64 : quad * 64 + 64, 256:384] = lo
    for d in range(4):
        v = jnp.concatenate([cot_ref[quad * 4 + d] for quad in range(4)], axis=0).T
        hi, lo = halves(v)
        cot_t[d, 0:128, :] = hi
        cot_t[d, 128:256, :] = lo
    for d in range(4):
        w_cat[:, 0:256] = w_hl[d]
        w_cat[:, 256:384] = w_hl[d, :, 0:128]
        wide_t[d] = lax.dot_general(
            cot_cat[d], w_cat[...], (((1,), (1,)), ((), ())), preferred_element_type=f32
        )
    for block in range(8):
        h, g = block // 4, block % 4
        for quad in range(4):
            parts = [
                wide_t[d, quad * 64 : quad * 64 + 64, block * 128 : block * 128 + 128]
                for d in range(4)
            ]
            for m in range(4):
                hi, lo = halves(pick([parts[(p - m) % 4] for p in range(4)], chunk))
                at = g * 128 + h * 64
                g_hi[m, at : at + 64, quad * 128 : quad * 128 + 128] = hi
                g_lo[m, at : at + 64, quad * 128 : quad * 128 + 128] = lo
    for quad in range(4):
        v = rows(quad, False)
        for m in range(4):
            hi, lo = halves(pltpu.roll(v, 32 * m, axis=1) if m else v)
            lcat[m, 0:128, quad * 128 : quad * 128 + 128] = hi
            lcat[m, 128:256, quad * 128 : quad * 128 + 128] = lo
            lcat[m, 256:384, quad * 128 : quad * 128 + 128] = hi
        hi, lo = halves(v.T)
        for p in range(4):
            for m in range(4):
                at = quad * 128 + ((p + m) % 4) * 32
                lt[m, at : at + 32, 0:128] = hi[p * 32 : p * 32 + 32]
                lt[m, at : at + 32, 128:256] = lo[p * 32 : p * 32 + 32]
    for e in range(16):
        g, m = e // 4, e % 4
        v = rows(e, True)
        hi, lo = halves(v)
        r_hl[m, 0:128, g * 128 : g * 128 + 128] = hi
        r_hl[m, 128:256, g * 128 : g * 128 + 128] = lo
        hi, lo = halves(v.T)
        rt[m, g * 128 : g * 128 + 128, 0:128] = hi
        rt[m, g * 128 : g * 128 + 128, 128:256] = hi
        rt[m, g * 128 : g * 128 + 128, 256:384] = lo
    for m in range(4):
        at = m * 512
        l_ref[at : at + 512, :] = matmul(rt[m], lcat[m])
    for block in range(8):
        h, g = block // 4, block % 4
        for quad in range(4):
            at = g * 128 + h * 64
            parts = [
                l_ref[m * 512 + at : m * 512 + at + 64, quad * 128 : quad * 128 + 128]
                for m in range(4)
            ]
            for d in range(4):
                hi, lo = halves(pick([parts[(p - d) % 4] for p in range(4)], chunk))
                a_hi[d, quad * 64 : quad * 64 + 64, block * 128 : block * 128 + 128] = hi
                a_lo[d, quad * 64 : quad * 64 + 64, block * 128 : block * 128 + 128] = lo
    for d in range(4):
        both = matmul(a_hi[d], w_hl[d])
        pair = both[:, 0:128] + both[:, 128:256] + matmul(a_lo[d], w_hl[d, :, 0:128])
        pair = pair * (1.0 / 128) + bias_ref[...]
        for quad in range(4):
            pair_ref[quad * 4 + d] = pair[quad * 64 : quad * 64 + 64]
    for d in range(4):
        both = matmul(cot_t[d], a_hi[d])
        part = both[0:128] + both[128:256] + matmul(cot_t[d, 0:128, :], a_lo[d])
        for block in range(8):
            v = part[:, block * 128 : block * 128 + 128]
            if d == 0:
                dw[block] = v
            else:
                dw[block] += pltpu.roll(v, 128 - 32 * d, axis=1)
    for block in range(8):
        dw[block] = dw[block].T
    for block in range(8):
        for p in range(4):
            for out, side in ((own_out, core), (other_out, 1 - core)):
                out[pl.ds(64 + p * 8 + block, 16, stride=BWD), :] = dw[
                    block, pl.ds(p * 32 + side, 16, stride=2), :
                ]
    for m in range(4):
        both = matmul(g_hi[m], lt[m])
        v = both[:, 0:128] + both[:, 128:256] + matmul(g_lo[m], lt[m, :, 0:128])
        for g in range(4):
            t = v[g * 128 : g * 128 + 128].T * (1.0 / 128)
            e = g * 4 + m
            for half, out in ((0, own_out), (1, other_out)):
                for s in range(4):
                    at = (half * 4 + s) * 16
                    out[pl.ds(s * 16 + e, 16, stride=BWD), :] = t[at : at + 16]
    total = [None] * 4
    for m in range(4):
        both = matmul(r_hl[m], g_hi[m])
        v = both[0:128] + both[128:256] + matmul(r_hl[m, 0:128, :], g_lo[m])
        for quad in range(4):
            part = v[:, quad * 128 : quad * 128 + 128]
            if m:
                part = pltpu.roll(part, 128 - 32 * m, axis=1)
            total[quad] = part if total[quad] is None else total[quad] + part
    for quad in range(4):
        t = total[quad] * (1.0 / 128)
        for half, out in ((0, own_out), (1, other_out)):
            for s in range(4):
                at = (half * 4 + s) * 16
                out[pl.ds(96 + s * 4 + quad, 16, stride=BWD), :] = t[at : at + 16]


def finish_kernel(x_ref, scale_ref, w1_ref, w2_ref, right_ref, col_ref, out_ref, weight_ref, tmp):
    core = lax.axis_index("core")
    left = col_ref[0]
    for c in range(1, 8):
        left = left + col_ref[c]
    weight_ref[...] = left[64:68] * (1.0 / 512)
    for u in range(4):
        part = contract(left[0:64, u * 32 : u * 32 + 32], w1_ref[...], ((1,), (0,)))
        for q in range(4):
            side = lax.rem(q % 2 + core, 2)
            for s in range(4):
                at = s * 64 + 32 * (q // 2) + 16 * side + u
                block = (q * 4 + s) * 4
                for k in range(2):
                    tmp[k, pl.ds(at, 4, stride=4), :] = part[block : block + 4, k * 128 : k * 128 + 128]
    grads = []
    for s in range(4):
        rows = right_ref[s * 16 : s * 16 + 16, :]
        entries = jnp.concatenate([rows[:, 0:64], rows[:, 64:128]], axis=0)
        grads.append(contract(entries, w2_ref[...], ((0,), (0,))))
    grad = jnp.concatenate(grads, axis=0) + jnp.concatenate([tmp[0], tmp[1]], axis=1)
    unit, inverse = standardized(x_ref[...])
    grad = grad * scale_ref[...]
    mean = jnp.mean(grad, axis=-1, keepdims=True)
    along = jnp.mean(grad * unit, axis=-1, keepdims=True)
    out_ref[...] = inverse * (grad - mean - unit * along)


def cost(flops, moved):
    return pl.CostEstimate(flops=flops, bytes_accessed=moved, transcendentals=0)


def swap_cores(array):
    return lax.ppermute(array, "core", [(0, 1), (1, 0)])


def exchange(array, axes):
    return lax.all_to_all(array, axes, 0, 0, tiled=True)


def local(
    sequence_embedding,
    standardize_scale,
    standardize_offset,
    first_operand_matrix,
    first_operand_intercept,
    second_operand_matrix,
    second_operand_intercept,
    result_matrix,
    result_intercept,
    edge_incoming_sensitivity,
):
    x = sequence_embedding.reshape(256, 256)
    scale = standardize_scale.reshape(1, 256)
    w1 = first_operand_matrix.T
    w2 = second_operand_matrix.T
    left, right = pl.pallas_call(
        project_kernel,
        out_shape=(
            jax.ShapeDtypeStruct((2, 2, 16, 128), f32),
            jax.ShapeDtypeStruct((64, 128), f32),
        ),
        in_specs=[VMEM] * 7,
        out_specs=(VMEM, VMEM),
        scratch_shapes=[pltpu.VMEM((256, 128), f32)],
        cost_estimate=cost(2 * 256 * 256 * 64 * 6, 400000),
        name="project",
    )(
        x,
        scale,
        standardize_offset.reshape(1, 256),
        w1,
        first_operand_intercept.reshape(1, 32),
        w2,
        second_operand_intercept.reshape(32, 1),
    )
    left = exchange(jnp.broadcast_to(left.reshape(1, 64, 128), (8, 64, 128)), COL)
    sent = jnp.concatenate(
        [left.reshape(16, 32, 128), jnp.broadcast_to(right[None], (16, 64, 128))], axis=1
    )
    own = exchange(sent, CHIP)
    other = swap_cores(own[:, 16:])
    pair, own_grads, other_grads = pl.pallas_call(
        tile_kernel,
        out_shape=(
            jax.ShapeDtypeStruct((16, 64, 128), f32),
            jax.ShapeDtypeStruct((16 * BWD, 128), f32),
            jax.ShapeDtypeStruct((16 * BWD, 128), f32),
        ),
        in_specs=[VMEM] * 5,
        out_specs=(VMEM, VMEM, VMEM),
        scratch_shapes=[
            pltpu.VMEM((2048, 512), f32),
            pltpu.VMEM((4, 384, 512), bf16),
            pltpu.VMEM((4, 512, 256), bf16),
            pltpu.VMEM((4, 256, 512), bf16),
            pltpu.VMEM((4, 512, 384), bf16),
            pltpu.VMEM((4, 256, 1024), f32),
            pltpu.VMEM((4, 256, 1024), bf16),
            pltpu.VMEM((4, 256, 1024), bf16),
            pltpu.VMEM((4, 1024, 256), bf16),
            pltpu.VMEM((1024, 384), bf16),
            pltpu.VMEM((4, 256, 384), bf16),
            pltpu.VMEM((4, 256, 256), bf16),
            pltpu.VMEM((4, 512, 512), bf16),
            pltpu.VMEM((4, 512, 512), bf16),
            pltpu.VMEM((8, 128, 128), f32),
        ],
        compiler_params=pltpu.CompilerParams(vmem_limit_bytes=48 * 1024 * 1024),
        cost_estimate=cost(1610612736 * 3, 5000000),
        name="tile",
    )(
        own.reshape(16 * FWD, 128),
        other.reshape(16 * (FWD - 16), 128),
        result_matrix,
        result_intercept.reshape(1, 128),
        edge_incoming_sensitivity,
    )
    own_grads = own_grads.reshape(16, BWD, 128)
    got = swap_cores(other_grads.reshape(16, BWD, 128))
    sent = jnp.concatenate(
        [own_grads[:, :96] + got[:, :96], own_grads[:, 96:], got[:, 96:]], axis=1
    )
    back = exchange(sent, CHIP)
    right_grad = back[:, :64].sum(axis=0)
    weight = back[:, 64:96].sum(axis=0).reshape(4, 8, 128).transpose(1, 0, 2)
    sent = jnp.concatenate(
        [back[:, 96:].reshape(8, 64, 128), jnp.pad(weight, ((0, 0), (0, 4), (0, 0)))], axis=1
    )
    cols = exchange(sent, COL)
    grad, weight = pl.pallas_call(
        finish_kernel,
        out_shape=(
            jax.ShapeDtypeStruct((256, 256), f32),
            jax.ShapeDtypeStruct((4, 128), f32),
        ),
        in_specs=[VMEM] * 6,
        out_specs=(VMEM, VMEM),
        scratch_shapes=[pltpu.VMEM((2, 256, 128), f32)],
        cost_estimate=cost(2 * 256 * 256 * 64 * 6, 900000),
        name="finish",
    )(x, scale, w1, w2, right_grad, cols)
    return pair, grad.reshape(4, 64, 256), weight


def solution(mesh):
    fine = Mesh(mesh.devices.reshape(SIZES), NAMES)
    tile = P(ROW, COL, None)
    return jax.shard_map(
        local,
        mesh=fine,
        in_specs=(tile, P(), P(), P(), P(), P(), P(), P(), P(), tile),
        out_specs=(tile, tile, P(ROW + COL, None)),
        check_vma=False,
    )
```

```python
import jax
import jax.numpy as jnp
from jax import lax
from jax.experimental import pallas as pl
from jax.experimental.pallas import tpu as pltpu
from jax.sharding import Mesh, PartitionSpec as P

exact = lax.Precision.HIGHEST
f32 = jnp.float32
bf16 = jnp.bfloat16

SIZES = (4, 4, 2, 2, 4)
NAMES = ("zl", "x", "core", "zh", "y")
CHIP = ("zl", "x")
ROW = ("zl", "x", "core")
COL = ("zh", "y")
VMEM = pl.BlockSpec(memory_space=pltpu.VMEM)

FWD = 96
BWD = 112


def contract(a, b, dims):
    return lax.dot_general(a, b, (dims, ((), ())), precision=exact, preferred_element_type=f32)


def matmul(a, b):
    return lax.dot_general(a, b, (((1,), (0,)), ((), ())), preferred_element_type=f32)


def halves(v):
    high = v.astype(bf16)
    return high, (v - high.astype(f32)).astype(bf16)


def standardized(x):
    demeaned = x - jnp.mean(x, axis=-1, keepdims=True)
    variance = jnp.mean(demeaned * demeaned, axis=-1, keepdims=True)
    inverse = lax.rsqrt(variance + 1e-05)
    return demeaned * inverse, inverse


def project_kernel(x_ref, scale_ref, offset_ref, w1_ref, b1_ref, w2_ref, b2_ref, left_ref, right_ref, tmp):
    core = lax.axis_index("core")
    normed = standardized(x_ref[...])[0] * scale_ref[...] + offset_ref[...]
    tmp[:, 0:32] = contract(normed, w1_ref[...], ((1,), (1,))) + b1_ref[...]
    wide = jnp.concatenate([tmp[pl.ds(u, 64, stride=4), :][:, 0:32] for u in range(4)], axis=1)
    for q in range(4):
        part = jnp.concatenate([wide[s * 16 + q * 4 : s * 16 + q * 4 + 4] for s in range(4)], axis=0)
        at = pl.multiple_of((q // 2 * 2 + lax.rem(q % 2 + core, 2)) * 16, 16)
        for copy in range(8):
            left_ref[copy, pl.ds(at, 16), :] = part
    on = lax.broadcasted_iota(jnp.int32, (32, 32), 0) == lax.broadcasted_iota(jnp.int32, (32, 32), 1)
    b2 = jnp.sum(jnp.where(on, b2_ref[...], 0.0), axis=1, keepdims=True)
    right = contract(w2_ref[...], normed, ((1,), (1,))) + b2
    for s in range(4):
        cols = right[:, s * 64 : s * 64 + 64]
        right_ref[s * 16 : s * 16 + 16, :] = jnp.concatenate([cols[0:16], cols[16:32]], axis=1)


def pick(parts):
    chunk = lax.broadcasted_iota(jnp.int32, (64, 128), 1) // 32
    low = jnp.where(chunk == 0, parts[0], parts[1])
    return jnp.where(chunk < 2, low, jnp.where(chunk == 2, parts[2], parts[3]))


def rows(own_ref, other_ref, row, right):
    got = []
    for ref, pitch, base in ((own_ref, FWD, 32), (other_ref, FWD - 16, 16)):
        for s in range(4):
            at = base + s * 16 + row if right else s * 4 + row
            got.append(ref[pl.ds(at, 16, stride=pitch), :])
    return jnp.concatenate(got, axis=0)


def weights_by_class(w_ref, w_hl):
    for e in range(32):
        hi, lo = halves(w_ref[pl.ds(e, 32, stride=32), :])
        for d in range(4):
            at = (e // 4) * 128 + ((e % 4 + d) % 4) * 32
            w_hl[d, at : at + 32, 0:128] = hi
            w_hl[d, at : at + 32, 128:256] = lo


def cotangent_kernel(w_ref, cot_ref, g_hi, g_lo, cot_t, wide_t, w_hl, w_cat, cot_cat):
    weights_by_class(w_ref, w_hl)
    for d in range(4):
        for quad in range(4):
            hi, lo = halves(cot_ref[quad * 4 + d])
            cot_cat[d, quad * 64 : quad * 64 + 64, 0:128] = hi
            cot_cat[d, quad * 64 : quad * 64 + 64, 128:256] = hi
            cot_cat[d, quad * 64 : quad * 64 + 64, 256:384] = lo
    for d in range(4):
        hi, lo = halves(jnp.concatenate([cot_ref[quad * 4 + d] for quad in range(4)], axis=0).T)
        cot_t[d, 0:128, :] = hi
        cot_t[d, 128:256, :] = lo
    for d in range(4):
        w_cat[:, 0:256] = w_hl[d]
        w_cat[:, 256:384] = w_hl[d, :, 0:128]
        wide_t[d] = lax.dot_general(
            cot_cat[d], w_cat[...], (((1,), (1,)), ((), ())), preferred_element_type=f32
        )
    for block in range(8):
        h, g = block // 4, block % 4
        at = g * 128 + h * 64
        for quad in range(4):
            parts = [
                wide_t[d, quad * 64 : quad * 64 + 64, block * 128 : block * 128 + 128]
                for d in range(4)
            ]
            for m in range(4):
                hi, lo = halves(pick([parts[(p - m) % 4] for p in range(4)]))
                g_hi[m, at : at + 64, quad * 128 : quad * 128 + 128] = hi
                g_lo[m, at : at + 64, quad * 128 : quad * 128 + 128] = lo


def outer_product(own_ref, other_ref, outer, lcat, rt, a_hi, a_lo, lt=None, r_hl=None):
    for quad in range(4):
        v = rows(own_ref, other_ref, quad, False)
        for m in range(4):
            hi, lo = halves(pltpu.roll(v, 32 * m, axis=1) if m else v)
            lcat[m, 0:128, quad * 128 : quad * 128 + 128] = hi
            lcat[m, 128:256, quad * 128 : quad * 128 + 128] = lo
            lcat[m, 256:384, quad * 128 : quad * 128 + 128] = hi
        if lt is None:
            continue
        hi, lo = halves(v.T)
        for p in range(4):
            for m in range(4):
                at = quad * 128 + ((p + m) % 4) * 32
                lt[m, at : at + 32, 0:128] = hi[p * 32 : p * 32 + 32]
                lt[m, at : at + 32, 128:256] = lo[p * 32 : p * 32 + 32]
    for e in range(16):
        g, m = e // 4, e % 4
        v = rows(own_ref, other_ref, e, True)
        if r_hl is not None:
            hi, lo = halves(v)
            r_hl[m, 0:128, g * 128 : g * 128 + 128] = hi
            r_hl[m, 128:256, g * 128 : g * 128 + 128] = lo
        hi, lo = halves(v.T)
        rt[m, g * 128 : g * 128 + 128, 0:128] = hi
        rt[m, g * 128 : g * 128 + 128, 128:256] = hi
        rt[m, g * 128 : g * 128 + 128, 256:384] = lo
    for m in range(4):
        outer[m] = matmul(rt[m], lcat[m])
    for block in range(8):
        h, g = block // 4, block % 4
        at = g * 128 + h * 64
        for quad in range(4):
            parts = [outer[m, at : at + 64, quad * 128 : quad * 128 + 128] for m in range(4)]
            for d in range(4):
                hi, lo = halves(pick([parts[(p - d) % 4] for p in range(4)]))
                a_hi[d, quad * 64 : quad * 64 + 64, block * 128 : block * 128 + 128] = hi
                a_lo[d, quad * 64 : quad * 64 + 64, block * 128 : block * 128 + 128] = lo


def pair_kernel(own_ref, other_ref, w_ref, bias_ref, pair_ref, outer, lcat, rt, a_hi, a_lo, w_hl):
    weights_by_class(w_ref, w_hl)
    outer_product(own_ref, other_ref, outer, lcat, rt, a_hi, a_lo)
    for d in range(4):
        both = matmul(a_hi[d], w_hl[d])
        pair = both[:, 0:128] + both[:, 128:256] + matmul(a_lo[d], w_hl[d, :, 0:128])
        pair = pair * (1.0 / 128) + bias_ref[...]
        for quad in range(4):
            pair_ref[quad * 4 + d] = pair[quad * 64 : quad * 64 + 64]


def tile_kernel(
    own_ref, other_ref, g_hi, g_lo, cot_t, own_out, other_out,
    outer, lcat, rt, a_hi, a_lo, lt, r_hl, dw,
):
    core = lax.axis_index("core")
    outer_product(own_ref, other_ref, outer, lcat, rt, a_hi, a_lo, lt, r_hl)
    for d in range(4):
        both = matmul(cot_t[d], a_hi[d])
        part = both[0:128] + both[128:256] + matmul(cot_t[d, 0:128, :], a_lo[d])
        for block in range(8):
            v = part[:, block * 128 : block * 128 + 128]
            if d == 0:
                dw[block] = v
            else:
                dw[block] += pltpu.roll(v, 128 - 32 * d, axis=1)
    for block in range(8):
        dw[block] = dw[block].T
    for block in range(8):
        for p in range(4):
            for out, side in ((own_out, core), (other_out, 1 - core)):
                out[pl.ds(64 + p * 8 + block, 16, stride=BWD), :] = dw[
                    block, pl.ds(p * 32 + side, 16, stride=2), :
                ]
    for m in range(4):
        both = matmul(g_hi[m], lt[m])
        v = both[:, 0:128] + both[:, 128:256] + matmul(g_lo[m], lt[m, :, 0:128])
        for g in range(4):
            t = v[g * 128 : g * 128 + 128].T * (1.0 / 128)
            e = g * 4 + m
            for half, out in ((0, own_out), (1, other_out)):
                for s in range(4):
                    at = (half * 4 + s) * 16
                    out[pl.ds(s * 16 + e, 16, stride=BWD), :] = t[at : at + 16]
    total = [None] * 4
    for m in range(4):
        both = matmul(r_hl[m], g_hi[m])
        v = both[0:128] + both[128:256] + matmul(r_hl[m, 0:128, :], g_lo[m])
        for quad in range(4):
            part = v[:, quad * 128 : quad * 128 + 128]
            if m:
                part = pltpu.roll(part, 128 - 32 * m, axis=1)
            total[quad] = part if total[quad] is None else total[quad] + part
    for quad in range(4):
        t = total[quad] * (1.0 / 128)
        for half, out in ((0, own_out), (1, other_out)):
            for s in range(4):
                at = (half * 4 + s) * 16
                out[pl.ds(96 + s * 4 + quad, 16, stride=BWD), :] = t[at : at + 16]


def right_kernel(w2_ref, right_ref, out_ref):
    total = right_ref[0, 0:64]
    for chip in range(1, 16):
        total = total + right_ref[chip, 0:64]
    for s in range(4):
        part = total[s * 16 : s * 16 + 16, :]
        entries = jnp.concatenate([part[:, 0:64], part[:, 64:128]], axis=0)
        out_ref[s * 64 : s * 64 + 64, :] = contract(entries, w2_ref[...], ((0,), (0,)))


def finish_kernel(x_ref, scale_ref, w1_ref, part_ref, col_ref, out_ref, weight_ref, tmp):
    core = lax.axis_index("core")
    left = col_ref[0]
    for c in range(1, 8):
        left = left + col_ref[c]
    weight_ref[...] = left[64:68] * (1.0 / 512)
    for u in range(4):
        part = contract(left[0:64, u * 32 : u * 32 + 32], w1_ref[...], ((1,), (0,)))
        for q in range(4):
            side = lax.rem(q % 2 + core, 2)
            for s in range(4):
                at = s * 64 + 32 * (q // 2) + 16 * side + u
                block = (q * 4 + s) * 4
                for k in range(2):
                    tmp[k, pl.ds(at, 4, stride=4), :] = part[block : block + 4, k * 128 : k * 128 + 128]
    unit, inverse = standardized(x_ref[...])
    grad = (part_ref[...] + jnp.concatenate([tmp[0], tmp[1]], axis=1)) * scale_ref[...]
    mean = jnp.mean(grad, axis=-1, keepdims=True)
    along = jnp.mean(grad * unit, axis=-1, keepdims=True)
    out_ref[...] = inverse * (grad - mean - unit * along)


def call(kernel, name, outs, scratch, mib, flops, *args):
    shapes = tuple(jax.ShapeDtypeStruct(*out) for out in outs)
    moved = sum(a.size * a.dtype.itemsize for a in args + shapes)
    return pl.pallas_call(
        kernel,
        out_shape=shapes,
        in_specs=[VMEM] * len(args),
        out_specs=(VMEM,) * len(outs),
        scratch_shapes=[pltpu.VMEM(*s) for s in scratch],
        compiler_params=pltpu.CompilerParams(vmem_limit_bytes=mib * 1024 * 1024),
        cost_estimate=pl.CostEstimate(flops=flops, bytes_accessed=moved, transcendentals=0),
        name=name,
    )(*args)


def swap_cores(array):
    return lax.ppermute(array, "core", [(0, 1), (1, 0)])


def exchange(array, axes):
    return lax.all_to_all(array, axes, 0, 0, tiled=True)


def local(
    sequence_embedding,
    standardize_scale,
    standardize_offset,
    first_operand_matrix,
    first_operand_intercept,
    second_operand_matrix,
    second_operand_intercept,
    result_matrix,
    result_intercept,
    edge_incoming_sensitivity,
):
    x = sequence_embedding.reshape(256, 256)
    scale = standardize_scale.reshape(1, 256)
    w1 = first_operand_matrix.T
    w2 = second_operand_matrix.T
    small = 2 * 256 * 256 * 32 * 6
    step = 2 * 1024 * 1024 * 128 * 3
    left, right = call(
        project_kernel,
        "project",
        [((8, 64, 128), f32), ((64, 128), f32)],
        [((256, 128), f32)],
        8,
        2 * small,
        x,
        scale,
        standardize_offset.reshape(1, 256),
        w1,
        first_operand_intercept.reshape(1, 32),
        w2,
        second_operand_intercept.reshape(1, 32),
    )
    g_hi, g_lo, cot_t = call(
        cotangent_kernel,
        "cotangent",
        [((4, 512, 512), bf16), ((4, 512, 512), bf16), ((4, 256, 256), bf16)],
        [
            ((4, 256, 1024), f32),
            ((4, 1024, 256), bf16),
            ((1024, 384), bf16),
            ((4, 256, 384), bf16),
        ],
        24,
        step,
        result_matrix,
        edge_incoming_sensitivity,
    )
    left = exchange(left, COL)
    sent = jnp.concatenate(
        [left.reshape(16, 32, 128), jnp.broadcast_to(right[None], (16, 64, 128))], axis=1
    )
    sent, g_hi, g_lo, cot_t = lax.optimization_barrier((sent, g_hi, g_lo, cot_t))
    own = exchange(sent, CHIP)
    other = swap_cores(own[:, 16:]).reshape(16 * (FWD - 16), 128)
    own = own.reshape(16 * FWD, 128)
    working = [
        ((4, 512, 512), f32),
        ((4, 384, 512), bf16),
        ((4, 512, 384), bf16),
        ((4, 256, 1024), bf16),
        ((4, 256, 1024), bf16),
    ]
    own_grads, other_grads = call(
        tile_kernel,
        "tile",
        [((16 * BWD, 128), f32), ((16 * BWD, 128), f32)],
        working + [((4, 512, 256), bf16), ((4, 256, 512), bf16), ((8, 128, 128), f32)],
        32,
        4 * step,
        own,
        other,
        g_hi,
        g_lo,
        cot_t,
    )
    (pair,) = call(
        pair_kernel,
        "pair",
        [((16, 64, 128), f32)],
        working + [((4, 1024, 256), bf16)],
        28,
        2 * step,
        own,
        other,
        result_matrix,
        result_intercept.reshape(1, 128),
    )
    own_grads = own_grads.reshape(16, BWD, 128)
    got = swap_cores(other_grads.reshape(16, BWD, 128))
    sent = jnp.concatenate(
        [own_grads[:, :96] + got[:, :96], own_grads[:, 96:], got[:, 96:]], axis=1
    )
    back = exchange(sent, CHIP)
    weight = back[:, 64:96].sum(axis=0).reshape(4, 8, 128).transpose(1, 0, 2)
    sent = jnp.concatenate(
        [back[:, 96:].reshape(8, 64, 128), jnp.pad(weight, ((0, 0), (0, 4), (0, 0)))], axis=1
    )
    cols = exchange(sent, COL)
    (part,) = call(right_kernel, "right", [((256, 256), f32)], [], 8, small, w2, back)
    grad, weight = call(
        finish_kernel,
        "finish",
        [((256, 256), f32), ((4, 128), f32)],
        [((2, 256, 128), f32)],
        8,
        small,
        x,
        scale,
        w1,
        part,
        cols,
    )
    return pair, grad.reshape(4, 64, 256), weight


def solution(mesh):
    fine = Mesh(mesh.devices.reshape(SIZES), NAMES)
    tile = P(ROW, COL, None)
    return jax.shard_map(
        local,
        mesh=fine,
        in_specs=(tile, P(), P(), P(), P(), P(), P(), P(), P(), tile),
        out_specs=(tile, tile, P(ROW + COL, None)),
        check_vma=False,
    )
```

```python
import jax
import jax.numpy as jnp
from jax import lax
from jax.experimental import pallas as pl
from jax.experimental.pallas import tpu as pltpu
from jax.sharding import Mesh, PartitionSpec as P

exact = lax.Precision.HIGHEST
f32 = jnp.float32
bf16 = jnp.bfloat16

SIZES = (4, 4, 2, 2, 4)
NAMES = ("zl", "x", "core", "zh", "y")
CHIP = ("zl", "x")
ROW = ("zl", "x", "core")
COL = ("zh", "y")
VMEM = pl.BlockSpec(memory_space=pltpu.VMEM)

BWD = 48


def contract(a, b, dims):
    return lax.dot_general(a, b, (dims, ((), ())), precision=exact, preferred_element_type=f32)


def matmul(a, b):
    return lax.dot_general(a, b, (((1,), (0,)), ((), ())), preferred_element_type=f32)


def halves(v):
    high = v.astype(bf16)
    return high, (v - high.astype(f32)).astype(bf16)


def standardized(x):
    demeaned = x - jnp.mean(x, axis=-1, keepdims=True)
    variance = jnp.mean(demeaned * demeaned, axis=-1, keepdims=True)
    inverse = lax.rsqrt(variance + 1e-05)
    return demeaned * inverse, inverse


def project_kernel(x_ref, scale_ref, offset_ref, w1_ref, b1_ref, w2_ref, b2_ref, left_ref, right_ref, tmp):
    normed = standardized(x_ref[...])[0] * scale_ref[...] + offset_ref[...]
    tmp[:, 0:32] = contract(normed, w1_ref[...], ((1,), (1,))) + b1_ref[...]
    wide = jnp.concatenate([tmp[pl.ds(u, 64, stride=4), :][:, 0:32] for u in range(4)], axis=1)
    for q in range(4):
        part = jnp.concatenate([wide[s * 16 + q * 4 : s * 16 + q * 4 + 4] for s in range(4)], axis=0)
        for copy in range(8):
            left_ref[copy, q * 16 : q * 16 + 16, :] = part
    on = lax.broadcasted_iota(jnp.int32, (32, 32), 0) == lax.broadcasted_iota(jnp.int32, (32, 32), 1)
    b2 = jnp.sum(jnp.where(on, b2_ref[...], 0.0), axis=1, keepdims=True)
    right = contract(w2_ref[...], normed, ((1,), (1,))) + b2
    for s in range(4):
        cols = right[:, s * 64 : s * 64 + 64]
        right_ref[s * 16 : s * 16 + 16, :] = jnp.concatenate([cols[0:16], cols[16:32]], axis=1)


def pick(parts):
    chunk = lax.broadcasted_iota(jnp.int32, (64, 128), 1) // 32
    low = jnp.where(chunk == 0, parts[0], parts[1])
    return jnp.where(chunk < 2, low, jnp.where(chunk == 2, parts[2], parts[3]))


def chip_of(dz, dx):
    return jnp.bitwise_xor(lax.axis_index("zl"), dz) * 4 + jnp.bitwise_xor(lax.axis_index("x"), dx)


def left_rows(left_ref, quad):
    core = lax.axis_index("core")
    got = []
    for side in (core, 1 - core):
        for s in range(4):
            got.append(left_ref[pl.ds(side * 16 + s * 4 + quad, 16, stride=32), :])
    return jnp.concatenate(got, axis=0)


def gather_right(parts, right_all):
    for at, ref in enumerate(parts):
        for dz in range(4):
            start = (at // 4) * 1024 + chip_of(dz, at % 4) * 64
            right_all[pl.ds(pl.multiple_of(start, 64), 64), :] = ref[dz]


def right_rows(right_all, e):
    got = []
    for half in range(2):
        for s in range(4):
            got.append(right_all[pl.ds(half * 1024 + s * 16 + e, 16, stride=64), :])
    return jnp.concatenate(got, axis=0)


def left_turned(left_ref, lt):
    for quad in range(4):
        hi, lo = halves(left_rows(left_ref, quad).T)
        for p in range(4):
            for m in range(4):
                at = quad * 128 + ((p + m) % 4) * 32
                lt[m, at : at + 32, 0:128] = hi[p * 32 : p * 32 + 32]
                lt[m, at : at + 32, 128:256] = lo[p * 32 : p * 32 + 32]


def weights_by_class(w_ref, w_hl):
    for e in range(32):
        hi, lo = halves(w_ref[pl.ds(e, 32, stride=32), :])
        for d in range(4):
            at = (e // 4) * 128 + ((e % 4 + d) % 4) * 32
            w_hl[d, at : at + 32, 0:128] = hi
            w_hl[d, at : at + 32, 128:256] = lo


def cotangent_kernel(w_ref, cot_ref, g_hi, g_lo, cot_t, wide_t, w_hl, w_cat, cot_cat):
    weights_by_class(w_ref, w_hl)
    for d in range(4):
        for quad in range(4):
            hi, lo = halves(cot_ref[quad * 4 + d])
            cot_cat[d, quad * 64 : quad * 64 + 64, 0:128] = hi
            cot_cat[d, quad * 64 : quad * 64 + 64, 128:256] = hi
            cot_cat[d, quad * 64 : quad * 64 + 64, 256:384] = lo
    for d in range(4):
        hi, lo = halves(jnp.concatenate([cot_ref[quad * 4 + d] for quad in range(4)], axis=0).T)
        cot_t[d, 0:128, :] = hi
        cot_t[d, 128:256, :] = lo
    for d in range(4):
        w_cat[:, 0:256] = w_hl[d]
        w_cat[:, 256:384] = w_hl[d, :, 0:128]
        wide_t[d] = lax.dot_general(
            cot_cat[d], w_cat[...], (((1,), (1,)), ((), ())), preferred_element_type=f32
        )
    for block in range(8):
        h, g = block // 4, block % 4
        at = g * 128 + h * 64
        for quad in range(4):
            parts = [
                wide_t[d, quad * 64 : quad * 64 + 64, block * 128 : block * 128 + 128]
                for d in range(4)
            ]
            for m in range(4):
                hi, lo = halves(pick([parts[(p - m) % 4] for p in range(4)]))
                g_hi[m, at : at + 64, quad * 128 : quad * 128 + 128] = hi
                g_lo[m, at : at + 64, quad * 128 : quad * 128 + 128] = lo


def outer_product(left_ref, parts, right_all, outer, lcat, rt, a_hi, a_lo, r_hl=None):
    gather_right(parts, right_all)
    for quad in range(4):
        v = left_rows(left_ref, quad)
        for m in range(4):
            hi, lo = halves(pltpu.roll(v, 32 * m, axis=1) if m else v)
            lcat[m, 0:128, quad * 128 : quad * 128 + 128] = hi
            lcat[m, 128:256, quad * 128 : quad * 128 + 128] = lo
            lcat[m, 256:384, quad * 128 : quad * 128 + 128] = hi
    for e in range(16):
        g, m = e // 4, e % 4
        v = right_rows(right_all, e)
        if r_hl is not None:
            hi, lo = halves(v)
            r_hl[m, 0:128, g * 128 : g * 128 + 128] = hi
            r_hl[m, 128:256, g * 128 : g * 128 + 128] = lo
        hi, lo = halves(v.T)
        rt[m, g * 128 : g * 128 + 128, 0:128] = hi
        rt[m, g * 128 : g * 128 + 128, 128:256] = hi
        rt[m, g * 128 : g * 128 + 128, 256:384] = lo
    for m in range(4):
        outer[m] = matmul(rt[m], lcat[m])
    for block in range(8):
        h, g = block // 4, block % 4
        at = g * 128 + h * 64
        for quad in range(4):
            parts = [outer[m, at : at + 64, quad * 128 : quad * 128 + 128] for m in range(4)]
            for d in range(4):
                hi, lo = halves(pick([parts[(p - d) % 4] for p in range(4)]))
                a_hi[d, quad * 64 : quad * 64 + 64, block * 128 : block * 128 + 128] = hi
                a_lo[d, quad * 64 : quad * 64 + 64, block * 128 : block * 128 + 128] = lo


def pair_kernel(left_ref, *refs):
    parts, (w_ref, bias_ref, pair_ref, right_all, outer, lcat, rt, a_hi, a_lo, w_hl) = refs[:8], refs[8:]
    weights_by_class(w_ref, w_hl)
    outer_product(left_ref, parts, right_all, outer, lcat, rt, a_hi, a_lo)
    for d in range(4):
        both = matmul(a_hi[d], w_hl[d])
        pair = both[:, 0:128] + both[:, 128:256] + matmul(a_lo[d], w_hl[d, :, 0:128])
        pair = pair * (1.0 / 128) + bias_ref[...]
        for quad in range(4):
            pair_ref[quad * 4 + d] = pair[quad * 64 : quad * 64 + 64]


def tile_kernel(left_ref, *refs):
    parts, (g_hi, g_lo, cot_t, own_out, other_out) = refs[:8], refs[8:13]
    right_all, outer, lcat, rt, a_hi, a_lo, r_hl, dw = refs[13:]
    core = lax.axis_index("core")
    outer_product(left_ref, parts, right_all, outer, lcat, rt, a_hi, a_lo, r_hl)
    for d in range(4):
        both = matmul(cot_t[d], a_hi[d])
        part = both[0:128] + both[128:256] + matmul(cot_t[d, 0:128, :], a_lo[d])
        for block in range(8):
            v = part[:, block * 128 : block * 128 + 128]
            if d == 0:
                dw[block] = v
            else:
                dw[block] += pltpu.roll(v, 128 - 32 * d, axis=1)
    for block in range(8):
        dw[block] = dw[block].T
    for block in range(8):
        for p in range(4):
            for out, side in ((own_out, core), (other_out, 1 - core)):
                out[pl.ds(p * 8 + block, 16, stride=BWD), :] = dw[
                    block, pl.ds(p * 32 + side, 16, stride=2), :
                ]
    total = [None] * 4
    for m in range(4):
        both = matmul(r_hl[m], g_hi[m])
        v = both[0:128] + both[128:256] + matmul(r_hl[m, 0:128, :], g_lo[m])
        for quad in range(4):
            part = v[:, quad * 128 : quad * 128 + 128]
            if m:
                part = pltpu.roll(part, 128 - 32 * m, axis=1)
            total[quad] = part if total[quad] is None else total[quad] + part
    for quad in range(4):
        t = total[quad] * (1.0 / 128)
        for half, out in ((0, own_out), (1, other_out)):
            for s in range(4):
                at = (half * 4 + s) * 16
                out[pl.ds(32 + s * 4 + quad, 16, stride=BWD), :] = t[at : at + 16]


def right_gradient_kernel(left_ref, g_hi, g_lo, *refs):
    outs, (lt, total) = refs[:8], refs[8:]
    left_turned(left_ref, lt)
    for m in range(4):
        both = matmul(g_hi[m], lt[m])
        v = both[:, 0:128] + both[:, 128:256] + matmul(g_lo[m], lt[m, :, 0:128])
        for g in range(4):
            t = v[g * 128 : g * 128 + 128].T * (1.0 / 128)
            for half in range(2):
                for s in range(4):
                    at = (half * 4 + s) * 16
                    row = half * 1024 + s * 16 + g * 4 + m
                    total[pl.ds(row, 16, stride=64), :] = t[at : at + 16]
    for at, ref in enumerate(outs):
        for dz in range(4):
            start = (at // 4) * 1024 + chip_of(dz, at % 4) * 64
            ref[dz] = total[pl.ds(pl.multiple_of(start, 64), 64), :]


def right_kernel(w2_ref, a_ref, b_ref, c_ref, d_ref, out_ref):
    total = (a_ref[...] + b_ref[...]) + (c_ref[...] + d_ref[...])
    for s in range(4):
        part = total[s * 16 : s * 16 + 16, :]
        entries = jnp.concatenate([part[:, 0:64], part[:, 64:128]], axis=0)
        out_ref[s * 64 : s * 64 + 64, :] = contract(entries, w2_ref[...], ((0,), (0,)))


def finish_kernel(x_ref, scale_ref, w1_ref, part_ref, col_ref, out_ref, weight_ref, tmp):
    core = lax.axis_index("core")
    left = col_ref[0]
    for c in range(1, 8):
        left = left + col_ref[c]
    weight_ref[...] = left[64:68] * (1.0 / 512)
    for u in range(4):
        part = contract(left[0:64, u * 32 : u * 32 + 32], w1_ref[...], ((1,), (0,)))
        for q in range(4):
            side = lax.rem(q % 2 + core, 2)
            for s in range(4):
                at = s * 64 + 32 * (q // 2) + 16 * side + u
                block = (q * 4 + s) * 4
                for k in range(2):
                    tmp[k, pl.ds(at, 4, stride=4), :] = part[block : block + 4, k * 128 : k * 128 + 128]
    unit, inverse = standardized(x_ref[...])
    grad = (part_ref[...] + jnp.concatenate([tmp[0], tmp[1]], axis=1)) * scale_ref[...]
    mean = jnp.mean(grad, axis=-1, keepdims=True)
    along = jnp.mean(grad * unit, axis=-1, keepdims=True)
    out_ref[...] = inverse * (grad - mean - unit * along)


def call(kernel, name, outs, scratch, mib, flops, *args):
    shapes = tuple(jax.ShapeDtypeStruct(*out) for out in outs)
    moved = sum(a.size * a.dtype.itemsize for a in args + shapes)
    return pl.pallas_call(
        kernel,
        out_shape=shapes,
        in_specs=[VMEM] * len(args),
        out_specs=(VMEM,) * len(outs),
        scratch_shapes=[pltpu.VMEM(*s) for s in scratch],
        compiler_params=pltpu.CompilerParams(
            vmem_limit_bytes=mib * 1024 * 1024 if mib else None
        ),
        cost_estimate=pl.CostEstimate(flops=flops, bytes_accessed=moved, transcendentals=0),
        name=name,
    )(*args)


def swap_cores(array):
    return lax.ppermute(array, "core", [(0, 1), (1, 0)])


def from_peer(array, axis, apart):
    return lax.ppermute(array, axis, [(i, i ^ apart) for i in range(4)])


def exchange(array, axes):
    return lax.all_to_all(array, axes, 0, 0, tiled=True)


def local(
    sequence_embedding,
    standardize_scale,
    standardize_offset,
    first_operand_matrix,
    first_operand_intercept,
    second_operand_matrix,
    second_operand_intercept,
    result_matrix,
    result_intercept,
    edge_incoming_sensitivity,
):
    x = sequence_embedding.reshape(256, 256)
    scale = standardize_scale.reshape(1, 256)
    w1 = first_operand_matrix.T
    w2 = second_operand_matrix.T
    small = 2 * 256 * 256 * 32 * 6
    step = 2 * 1024 * 1024 * 128 * 3
    left, right = call(
        project_kernel,
        "project",
        [((8, 64, 128), f32), ((64, 128), f32)],
        [((256, 128), f32)],
        None,
        2 * small,
        x,
        scale,
        standardize_offset.reshape(1, 256),
        w1,
        first_operand_intercept.reshape(1, 32),
        w2,
        second_operand_intercept.reshape(1, 32),
    )
    g_hi, g_lo, cot_t = call(
        cotangent_kernel,
        "cotangent",
        [((4, 512, 512), bf16), ((4, 512, 512), bf16), ((4, 256, 256), bf16)],
        [
            ((4, 256, 1024), f32),
            ((4, 1024, 256), bf16),
            ((1024, 384), bf16),
            ((4, 256, 384), bf16),
        ],
        24,
        step,
        result_matrix,
        edge_incoming_sensitivity,
    )
    left = exchange(left, COL).reshape(32, 16, 128)
    right = jnp.stack([right] + [from_peer(right, "zl", dz) for dz in (1, 2, 3)])
    left, right, g_hi, g_lo, cot_t = lax.optimization_barrier((left, right, g_hi, g_lo, cot_t))
    left = exchange(left, ROW).reshape(512, 128)
    parts = [right] + [from_peer(right, "x", dx) for dx in (1, 2, 3)]
    parts = parts + [swap_cores(part) for part in parts]
    working = [
        ((2048, 128), f32),
        ((4, 512, 512), f32),
        ((4, 384, 512), bf16),
        ((4, 512, 384), bf16),
        ((4, 256, 1024), bf16),
        ((4, 256, 1024), bf16),
    ]
    own, other = call(
        tile_kernel,
        "tile",
        [((16 * BWD, 128), f32), ((16 * BWD, 128), f32)],
        working + [((4, 256, 512), bf16), ((8, 128, 128), f32)],
        28,
        3 * step,
        left,
        *parts,
        g_hi,
        g_lo,
        cot_t,
    )
    own = own.reshape(16, BWD, 128)
    got = swap_cores(other.reshape(16, BWD, 128))
    sent = jnp.concatenate([own[:, :32] + got[:, :32], own[:, 32:], got[:, 32:]], axis=1)
    back = exchange(sent, CHIP)
    sums = call(
        right_gradient_kernel,
        "right_gradient",
        [((4, 64, 128), f32)] * 8,
        [((4, 512, 256), bf16), ((2048, 128), f32)],
        16,
        step,
        left,
        g_hi,
        g_lo,
    )
    sums = [a + swap_cores(b) for a, b in zip(sums[:4], sums[4:])]
    right = sums[0] + sum(from_peer(sums[dx], "x", dx) for dx in (1, 2, 3))
    (pair,) = call(
        pair_kernel,
        "pair",
        [((16, 64, 128), f32)],
        working + [((4, 1024, 256), bf16)],
        28,
        2 * step,
        left,
        *parts,
        result_matrix,
        result_intercept.reshape(1, 128),
    )
    weight = back[:, :32].sum(axis=0).reshape(4, 8, 128).transpose(1, 0, 2)
    sent = jnp.concatenate(
        [back[:, 32:].reshape(8, 64, 128), jnp.pad(weight, ((0, 0), (0, 4), (0, 0)))], axis=1
    )
    sent, right, pair = lax.optimization_barrier((sent, right, pair))
    cols = exchange(sent, COL)
    right = [right[0]] + [from_peer(right[dz], "zl", dz) for dz in (1, 2, 3)]
    (part,) = call(right_kernel, "right", [((256, 256), f32)], [], 8, small, w2, *right)
    grad, weight = call(
        finish_kernel,
        "finish",
        [((256, 256), f32), ((4, 128), f32)],
        [((2, 256, 128), f32)],
        8,
        small,
        x,
        scale,
        w1,
        part,
        cols,
    )
    return pair, grad.reshape(4, 64, 256), weight


def solution(mesh):
    fine = Mesh(mesh.devices.reshape(SIZES), NAMES)
    tile = P(ROW, COL, None)
    return jax.shard_map(
        local,
        mesh=fine,
        in_specs=(tile, P(), P(), P(), P(), P(), P(), P(), P(), tile),
        out_specs=(tile, tile, P(ROW + COL, None)),
        check_vma=False,
    )
```

```python
import jax
import jax.numpy as jnp
from jax import lax
from jax.experimental import pallas as pl
from jax.experimental.pallas import tpu as pltpu
from jax.sharding import Mesh, PartitionSpec as P

exact = lax.Precision.HIGHEST
f32 = jnp.float32
bf16 = jnp.bfloat16

SIZES = (4, 4, 2, 2, 4)
NAMES = ("zl", "x", "core", "zh", "y")
CHIP = ("zl", "x")
ROW = ("zl", "x", "core")
COL = ("zh", "y")
VMEM = pl.BlockSpec(memory_space=pltpu.VMEM)
HBM = pl.BlockSpec(memory_space=pltpu.HBM)

BWD = 32


def contract(a, b, dims):
    return lax.dot_general(a, b, (dims, ((), ())), precision=exact, preferred_element_type=f32)


def matmul(a, b):
    return lax.dot_general(a, b, (((1,), (0,)), ((), ())), preferred_element_type=f32)


def halves(v):
    high = v.astype(bf16)
    return high, (v - high.astype(f32)).astype(bf16)


def standardized(x):
    demeaned = x - jnp.mean(x, axis=-1, keepdims=True)
    variance = jnp.mean(demeaned * demeaned, axis=-1, keepdims=True)
    inverse = lax.rsqrt(variance + 1e-05)
    return demeaned * inverse, inverse


def project_kernel(
    x_ref, scale_ref, offset_ref, w1_ref, b1_ref, w2_ref, b2_ref, left_ref, right_ref, tmp
):
    normed = standardized(x_ref[...])[0] * scale_ref[...] + offset_ref[...]
    on = lax.broadcasted_iota(jnp.int32, (32, 32), 0) == lax.broadcasted_iota(jnp.int32, (32, 32), 1)
    b2 = jnp.sum(jnp.where(on, b2_ref[...], 0.0), axis=1, keepdims=True)
    right = contract(w2_ref[...], normed, ((1,), (1,))) + b2
    for s in range(4):
        cols = right[:, s * 64 : s * 64 + 64]
        right_ref[s * 16 : s * 16 + 16, :] = jnp.concatenate([cols[0:16], cols[16:32]], axis=1)
    tmp[:, 0:32] = contract(normed, w1_ref[...], ((1,), (1,))) + b1_ref[...]
    wide = jnp.concatenate([tmp[pl.ds(u, 64, stride=4), :][:, 0:32] for u in range(4)], axis=1)
    for q in range(4):
        part = jnp.concatenate([wide[s * 16 + q * 4 : s * 16 + q * 4 + 4] for s in range(4)], axis=0)
        for copy in range(8):
            left_ref[copy, q * 16 : q * 16 + 16, :] = part


def fetch(pairs, sems):
    copies = [pltpu.make_async_copy(a, b, sems.at[i]) for i, (a, b) in enumerate(pairs)]
    for copy in copies:
        copy.start()
    return copies


def pick(parts):
    chunk = lax.broadcasted_iota(jnp.int32, (64, 128), 1) // 32
    low = jnp.where(chunk == 0, parts[0], parts[1])
    return jnp.where(chunk < 2, low, jnp.where(chunk == 2, parts[2], parts[3]))


def chip_of(dz, dx):
    return jnp.bitwise_xor(lax.axis_index("zl"), dz) * 4 + jnp.bitwise_xor(lax.axis_index("x"), dx)


def left_rows(left_ref, quad):
    core = lax.axis_index("core")
    got = []
    for side in (core, 1 - core):
        for s in range(4):
            got.append(left_ref[pl.ds(side * 16 + s * 4 + quad, 16, stride=32), :])
    return jnp.concatenate(got, axis=0)


def gather_right(parts, right_all):
    for at, ref in enumerate(parts):
        for dz in range(4):
            start = (at // 4) * 1024 + chip_of(dz, at % 4) * 64
            right_all[pl.ds(pl.multiple_of(start, 64), 64), :] = ref[dz]


def right_rows(right_all, e):
    got = []
    for half in range(2):
        for s in range(4):
            got.append(right_all[pl.ds(half * 1024 + s * 16 + e, 16, stride=64), :])
    return jnp.concatenate(got, axis=0)


def left_turned(left_ref, lt):
    for quad in range(4):
        hi, lo = halves(left_rows(left_ref, quad).T)
        for p in range(4):
            for m in range(4):
                at = quad * 128 + ((p + m) % 4) * 32
                lt[m, at : at + 32, 0:128] = hi[p * 32 : p * 32 + 32]
                lt[m, at : at + 32, 128:256] = lo[p * 32 : p * 32 + 32]


def weights_by_class(w_ref, w_hl):
    for e in range(32):
        hi, lo = halves(w_ref[pl.ds(e, 32, stride=32), :])
        for d in range(4):
            at = (e // 4) * 128 + ((e % 4 + d) % 4) * 32
            w_hl[d, at : at + 32, 0:128] = hi
            w_hl[d, at : at + 32, 128:256] = lo


def cotangent_kernel(w_ref, cot_ref, g_hi, g_lo, cot_t, wide_t, w_hl, w_cat, cot_cat):
    weights_by_class(w_ref, w_hl)
    for d in range(4):
        for quad in range(4):
            hi, lo = halves(cot_ref[quad * 4 + d])
            cot_cat[d, quad * 64 : quad * 64 + 64, 0:128] = hi
            cot_cat[d, quad * 64 : quad * 64 + 64, 128:256] = hi
            cot_cat[d, quad * 64 : quad * 64 + 64, 256:384] = lo
    for d in range(4):
        hi, lo = halves(jnp.concatenate([cot_ref[quad * 4 + d] for quad in range(4)], axis=0).T)
        cot_t[d, 0:128, :] = hi
        cot_t[d, 128:256, :] = lo
    for d in range(4):
        w_cat[:, 0:256] = w_hl[d]
        w_cat[:, 256:384] = w_hl[d, :, 0:128]
        wide_t[d] = lax.dot_general(
            cot_cat[d], w_cat[...], (((1,), (1,)), ((), ())), preferred_element_type=f32
        )
    for block in range(8):
        h, g = block // 4, block % 4
        at = g * 128 + h * 64
        for quad in range(4):
            parts = [
                wide_t[d, quad * 64 : quad * 64 + 64, block * 128 : block * 128 + 128]
                for d in range(4)
            ]
            for m in range(4):
                hi, lo = halves(pick([parts[(p - m) % 4] for p in range(4)]))
                g_hi[m, at : at + 64, quad * 128 : quad * 128 + 128] = hi
                g_lo[m, at : at + 64, quad * 128 : quad * 128 + 128] = lo


def outer_product(left_ref, parts, right_all, outer, lcat, rt, a_hi, a_lo):
    gather_right(parts, right_all)
    for quad in range(4):
        v = left_rows(left_ref, quad)
        for m in range(4):
            hi, lo = halves(pltpu.roll(v, 32 * m, axis=1) if m else v)
            lcat[m, 0:128, quad * 128 : quad * 128 + 128] = hi
            lcat[m, 128:256, quad * 128 : quad * 128 + 128] = lo
            lcat[m, 256:384, quad * 128 : quad * 128 + 128] = hi
    for e in range(16):
        g, m = e // 4, e % 4
        hi, lo = halves(right_rows(right_all, e).T)
        rt[m, g * 128 : g * 128 + 128, 0:128] = hi
        rt[m, g * 128 : g * 128 + 128, 128:256] = hi
        rt[m, g * 128 : g * 128 + 128, 256:384] = lo
    for m in range(4):
        outer[m] = matmul(rt[m], lcat[m])
    for block in range(8):
        h, g = block // 4, block % 4
        at = g * 128 + h * 64
        for quad in range(4):
            parts = [outer[m, at : at + 64, quad * 128 : quad * 128 + 128] for m in range(4)]
            for d in range(4):
                hi, lo = halves(pick([parts[(p - d) % 4] for p in range(4)]))
                a_hi[d, quad * 64 : quad * 64 + 64, block * 128 : block * 128 + 128] = hi
                a_lo[d, quad * 64 : quad * 64 + 64, block * 128 : block * 128 + 128] = lo


def pair_kernel(left_ref, *refs):
    parts, (bias_ref, w_far, pair_ref, right_all, outer, lcat, rt, a_hi, a_lo) = refs[:8], refs[8:17]
    w_hl, w_ref, sems = refs[17:]
    (fetched,) = fetch([(w_far, w_ref)], sems)
    outer_product(left_ref, parts, right_all, outer, lcat, rt, a_hi, a_lo)
    fetched.wait()
    weights_by_class(w_ref, w_hl)
    for d in range(4):
        both = matmul(a_hi[d], w_hl[d])
        pair = both[:, 0:128] + both[:, 128:256] + matmul(a_lo[d], w_hl[d, :, 0:128])
        pair = pair * (1.0 / 128) + bias_ref[...]
        for quad in range(4):
            pair_ref[quad * 4 + d] = pair[quad * 64 : quad * 64 + 64]


def tile_kernel(left_ref, *refs):
    parts, (cot_far, own_out, other_out) = refs[:8], refs[8:11]
    right_all, outer, lcat, rt, a_hi, a_lo, dw, cot_t, sems = refs[11:]
    core = lax.axis_index("core")
    (fetched,) = fetch([(cot_far, cot_t)], sems)
    outer_product(left_ref, parts, right_all, outer, lcat, rt, a_hi, a_lo)
    fetched.wait()
    for d in range(4):
        both = matmul(cot_t[d], a_hi[d])
        part = both[0:128] + both[128:256] + matmul(cot_t[d, 0:128, :], a_lo[d])
        for block in range(8):
            v = part[:, block * 128 : block * 128 + 128]
            if d == 0:
                dw[block] = v
            else:
                dw[block] += pltpu.roll(v, 128 - 32 * d, axis=1)
    for block in range(8):
        dw[block] = dw[block].T
    for block in range(8):
        for p in range(4):
            for out, side in ((own_out, core), (other_out, 1 - core)):
                out[pl.ds(p * 8 + block, 16, stride=BWD), :] = dw[
                    block, pl.ds(p * 32 + side, 16, stride=2), :
                ]


def left_gradient_kernel(*refs):
    parts, (hi_far, lo_far, own_out, other_out, right_all, r_hl, g_hi, g_lo, sems) = refs[:8], refs[8:]
    copies = fetch([(hi_far, g_hi), (lo_far, g_lo)], sems)
    gather_right(parts, right_all)
    for e in range(16):
        g, m = e // 4, e % 4
        hi, lo = halves(right_rows(right_all, e))
        r_hl[m, 0:128, g * 128 : g * 128 + 128] = hi
        r_hl[m, 128:256, g * 128 : g * 128 + 128] = lo
    for copy in copies:
        copy.wait()
    total = [None] * 4
    for m in range(4):
        both = matmul(r_hl[m], g_hi[m])
        v = both[0:128] + both[128:256] + matmul(r_hl[m, 0:128, :], g_lo[m])
        for quad in range(4):
            part = v[:, quad * 128 : quad * 128 + 128]
            if m:
                part = pltpu.roll(part, 128 - 32 * m, axis=1)
            total[quad] = part if total[quad] is None else total[quad] + part
    for quad in range(4):
        t = total[quad] * (1.0 / 128)
        for half, out in ((0, own_out), (1, other_out)):
            for s in range(4):
                at = (half * 4 + s) * 16
                out[pl.ds(s * 4 + quad, 16, stride=16), :] = t[at : at + 16]


def right_gradient_kernel(left_ref, hi_far, lo_far, *refs):
    outs, (lt, total, g_hi, g_lo, sems) = refs[:8], refs[8:]
    copies = fetch([(hi_far, g_hi), (lo_far, g_lo)], sems)
    left_turned(left_ref, lt)
    for copy in copies:
        copy.wait()
    for m in range(4):
        both = matmul(g_hi[m], lt[m])
        v = both[:, 0:128] + both[:, 128:256] + matmul(g_lo[m], lt[m, :, 0:128])
        for g in range(4):
            t = v[g * 128 : g * 128 + 128].T * (1.0 / 128)
            for half in range(2):
                for s in range(4):
                    at = (half * 4 + s) * 16
                    row = half * 1024 + s * 16 + g * 4 + m
                    total[pl.ds(row, 16, stride=64), :] = t[at : at + 16]
    for at, ref in enumerate(outs):
        for dz in range(4):
            start = (at // 4) * 1024 + chip_of(dz, at % 4) * 64
            ref[dz] = total[pl.ds(pl.multiple_of(start, 64), 64), :]


def right_kernel(w2_ref, a_ref, b_ref, c_ref, d_ref, out_ref):
    total = (a_ref[...] + b_ref[...]) + (c_ref[...] + d_ref[...])
    for s in range(4):
        part = total[s * 16 : s * 16 + 16, :]
        entries = jnp.concatenate([part[:, 0:64], part[:, 64:128]], axis=0)
        out_ref[s * 64 : s * 64 + 64, :] = contract(entries, w2_ref[...], ((0,), (0,)))


def finish_kernel(x_ref, scale_ref, w1_ref, part_ref, col_ref, out_ref, weight_ref, tmp):
    core = lax.axis_index("core")
    left = col_ref[0]
    for c in range(1, 8):
        left = left + col_ref[c]
    weight_ref[...] = left[64:68] * (1.0 / 512)
    for u in range(4):
        part = contract(left[0:64, u * 32 : u * 32 + 32], w1_ref[...], ((1,), (0,)))
        for q in range(4):
            side = lax.rem(q % 2 + core, 2)
            for s in range(4):
                at = s * 64 + 32 * (q // 2) + 16 * side + u
                block = (q * 4 + s) * 4
                for k in range(2):
                    tmp[k, pl.ds(at, 4, stride=4), :] = part[block : block + 4, k * 128 : k * 128 + 128]
    unit, inverse = standardized(x_ref[...])
    grad = (part_ref[...] + jnp.concatenate([tmp[0], tmp[1]], axis=1)) * scale_ref[...]
    mean = jnp.mean(grad, axis=-1, keepdims=True)
    along = jnp.mean(grad * unit, axis=-1, keepdims=True)
    out_ref[...] = inverse * (grad - mean - unit * along)


def call(kernel, name, outs, scratch, mib, flops, *args, far=(), copies=0):
    shapes = tuple(jax.ShapeDtypeStruct(*out) for out in outs)
    moved = sum(a.size * a.dtype.itemsize for a in args + tuple(far) + shapes)
    return pl.pallas_call(
        kernel,
        out_shape=shapes,
        in_specs=[VMEM] * len(args) + [HBM] * len(far),
        out_specs=(VMEM,) * len(outs),
        scratch_shapes=[pltpu.VMEM(*s) for s in scratch]
        + ([pltpu.SemaphoreType.DMA((copies,))] if copies else []),
        compiler_params=pltpu.CompilerParams(
            vmem_limit_bytes=mib * 1024 * 1024 if mib else None
        ),
        cost_estimate=pl.CostEstimate(flops=flops, bytes_accessed=moved, transcendentals=0),
        name=name,
    )(*args, *far)


def swap_cores(array):
    return lax.ppermute(array, "core", [(0, 1), (1, 0)])


def from_peer(array, axis, apart):
    return lax.ppermute(array, axis, [(i, i ^ apart) for i in range(4)])


def exchange(array, axes):
    return lax.all_to_all(array, axes, 0, 0, tiled=True)


def local(
    sequence_embedding,
    standardize_scale,
    standardize_offset,
    first_operand_matrix,
    first_operand_intercept,
    second_operand_matrix,
    second_operand_intercept,
    result_matrix,
    result_intercept,
    edge_incoming_sensitivity,
):
    x = sequence_embedding.reshape(256, 256)
    scale = standardize_scale.reshape(1, 256)
    w1 = first_operand_matrix.T
    w2 = second_operand_matrix.T
    small = 2 * 256 * 256 * 32 * 6
    step = 2 * 1024 * 1024 * 128 * 3
    offset = standardize_offset.reshape(1, 256)
    left, right = call(
        project_kernel,
        "project",
        [((8, 64, 128), f32), ((64, 128), f32)],
        [((256, 128), f32)],
        None,
        2 * small,
        x,
        scale,
        offset,
        w1,
        first_operand_intercept.reshape(1, 32),
        w2,
        second_operand_intercept.reshape(1, 32),
    )
    g_hi, g_lo, cot_t = call(
        cotangent_kernel,
        "cotangent",
        [((4, 512, 512), bf16), ((4, 512, 512), bf16), ((4, 256, 256), bf16)],
        [
            ((4, 256, 1024), f32),
            ((4, 1024, 256), bf16),
            ((1024, 384), bf16),
            ((4, 256, 384), bf16),
        ],
        None,
        step,
        result_matrix,
        edge_incoming_sensitivity,
    )
    left = exchange(left, COL).reshape(32, 16, 128)
    right = jnp.stack([right] + [from_peer(right, "zl", dz) for dz in (1, 2, 3)])
    parts = [right] + [from_peer(right, "x", dx) for dx in (1, 2, 3)]
    left, parts, g_hi, g_lo, cot_t = lax.optimization_barrier((left, parts, g_hi, g_lo, cot_t))
    left = exchange(left, ROW).reshape(512, 128)
    parts = parts + [swap_cores(part) for part in parts]
    own_left, other_left = call(
        left_gradient_kernel,
        "left_gradient",
        [((256, 128), f32), ((256, 128), f32)],
        [((2048, 128), f32), ((4, 256, 512), bf16)] + [((4, 512, 512), bf16)] * 2,
        14,
        step,
        *parts,
        far=(g_hi, g_lo),
        copies=2,
    )
    got_left = swap_cores(other_left)
    left, own_left, got_left = lax.optimization_barrier((left, own_left, got_left))
    working = [
        ((2048, 128), f32),
        ((4, 512, 512), f32),
        ((4, 384, 512), bf16),
        ((4, 512, 384), bf16),
        ((4, 256, 1024), bf16),
        ((4, 256, 1024), bf16),
    ]
    own, other = call(
        tile_kernel,
        "tile",
        [((16 * BWD, 128), f32)] * 2,
        working + [((8, 128, 128), f32), ((4, 256, 256), bf16)],
        22,
        2 * step,
        left,
        *parts,
        far=(cot_t,),
        copies=1,
    )
    got = swap_cores(other)
    sums = call(
        right_gradient_kernel,
        "right_gradient",
        [((4, 64, 128), f32)] * 8,
        [((4, 512, 256), bf16), ((2048, 128), f32)] + [((4, 512, 512), bf16)] * 2,
        None,
        step,
        left,
        far=(g_hi, g_lo),
        copies=2,
    )
    weight = (own + got).reshape(16, BWD, 128)
    sent = [weight, own_left.reshape(16, 16, 128), got_left.reshape(16, 16, 128)]
    back = exchange(jnp.concatenate(sent, axis=1), CHIP)
    sums = [a + swap_cores(b) for a, b in zip(sums[:4], sums[4:])]
    right = sums[0] + sum(from_peer(sums[dx], "x", dx) for dx in (1, 2, 3))
    (pair,) = call(
        pair_kernel,
        "pair",
        [((16, 64, 128), f32)],
        working + [((4, 1024, 256), bf16), ((1024, 128), f32)],
        24,
        2 * step,
        left,
        *parts,
        result_intercept.reshape(1, 128),
        far=(result_matrix,),
        copies=1,
    )
    weight = back[:, :32].sum(axis=0).reshape(4, 8, 128).transpose(1, 0, 2)
    sent = jnp.concatenate(
        [back[:, 32:].reshape(8, 64, 128), jnp.pad(weight, ((0, 0), (0, 4), (0, 0)))], axis=1
    )
    sent, right = lax.optimization_barrier((sent, right))
    cols = exchange(sent, COL)
    right = [right[0]] + [from_peer(right[dz], "zl", dz) for dz in (1, 2, 3)]
    (part,) = call(right_kernel, "right", [((256, 256), f32)], [], 8, small, w2, *right)
    grad, weight = call(
        finish_kernel,
        "finish",
        [((256, 256), f32), ((4, 128), f32)],
        [((2, 256, 128), f32)],
        8,
        small,
        x,
        scale,
        w1,
        part,
        cols,
    )
    return pair, grad.reshape(4, 64, 256), weight


def solution(mesh):
    fine = Mesh(mesh.devices.reshape(SIZES), NAMES)
    tile = P(ROW, COL, None)
    return jax.shard_map(
        local,
        mesh=fine,
        in_specs=(tile, P(), P(), P(), P(), P(), P(), P(), P(), tile),
        out_specs=(tile, tile, P(ROW + COL, None)),
        check_vma=False,
    )
```

```python
import jax
import jax.numpy as jnp
from jax import lax
from jax.experimental import pallas as pl
from jax.experimental.pallas import tpu as pltpu
from jax.sharding import Mesh, PartitionSpec as P

exact = lax.Precision.HIGHEST
f32 = jnp.float32
bf16 = jnp.bfloat16

SIZES = (4, 4, 2, 2, 4)
NAMES = ("zl", "x", "core", "zh", "y")
CHIP = ("zl", "x")
ROW = ("zl", "x", "core")
COL = ("zh", "y")
VMEM = pl.BlockSpec(memory_space=pltpu.VMEM)
HBM = pl.BlockSpec(memory_space=pltpu.HBM)

BWD = 32


def contract(a, b, dims):
    return lax.dot_general(a, b, (dims, ((), ())), precision=exact, preferred_element_type=f32)


def matmul(a, b):
    return lax.dot_general(a, b, (((1,), (0,)), ((), ())), preferred_element_type=f32)


def halves(v):
    high = v.astype(bf16)
    return high, (v - high.astype(f32)).astype(bf16)


def standardized(x):
    demeaned = x - jnp.mean(x, axis=-1, keepdims=True)
    variance = jnp.mean(demeaned * demeaned, axis=-1, keepdims=True)
    inverse = lax.rsqrt(variance + 1e-05)
    return demeaned * inverse, inverse


def project_right_kernel(x_ref, scale_ref, offset_ref, w2_ref, b2_ref, right_ref):
    normed = standardized(x_ref[...])[0] * scale_ref[...] + offset_ref[...]
    on = lax.broadcasted_iota(jnp.int32, (32, 32), 0) == lax.broadcasted_iota(jnp.int32, (32, 32), 1)
    b2 = jnp.sum(jnp.where(on, b2_ref[...], 0.0), axis=1, keepdims=True)
    right = contract(w2_ref[...], normed, ((1,), (1,))) + b2
    for s in range(4):
        cols = right[:, s * 64 : s * 64 + 64]
        right_ref[s * 16 : s * 16 + 16, :] = jnp.concatenate([cols[0:16], cols[16:32]], axis=1)


def project_left_kernel(x_ref, scale_ref, offset_ref, w1_ref, b1_ref, left_ref, tmp):
    normed = standardized(x_ref[...])[0] * scale_ref[...] + offset_ref[...]
    tmp[:, 0:32] = contract(normed, w1_ref[...], ((1,), (1,))) + b1_ref[...]
    wide = jnp.concatenate([tmp[pl.ds(u, 64, stride=4), :][:, 0:32] for u in range(4)], axis=1)
    for q in range(4):
        part = jnp.concatenate([wide[s * 16 + q * 4 : s * 16 + q * 4 + 4] for s in range(4)], axis=0)
        for copy in range(8):
            left_ref[copy, q * 16 : q * 16 + 16, :] = part


def fetch(pairs, sems):
    copies = [pltpu.make_async_copy(a, b, sems.at[i]) for i, (a, b) in enumerate(pairs)]
    for copy in copies:
        copy.start()
    return copies


def pick(parts):
    chunk = lax.broadcasted_iota(jnp.int32, (64, 128), 1) // 32
    low = jnp.where(chunk == 0, parts[0], parts[1])
    return jnp.where(chunk < 2, low, jnp.where(chunk == 2, parts[2], parts[3]))


def chip_of(dz, dx):
    return jnp.bitwise_xor(lax.axis_index("zl"), dz) * 4 + jnp.bitwise_xor(lax.axis_index("x"), dx)


def left_rows(left_ref, quad):
    core = lax.axis_index("core")
    got = []
    for side in (core, 1 - core):
        for s in range(4):
            got.append(left_ref[pl.ds(side * 16 + s * 4 + quad, 16, stride=32), :])
    return jnp.concatenate(got, axis=0)


def gather_right(parts, right_all):
    for at, ref in enumerate(parts):
        for dz in range(4):
            start = (at // 4) * 1024 + chip_of(dz, at % 4) * 64
            right_all[pl.ds(pl.multiple_of(start, 64), 64), :] = ref[dz]


def right_rows(right_all, e):
    got = []
    for half in range(2):
        for s in range(4):
            got.append(right_all[pl.ds(half * 1024 + s * 16 + e, 16, stride=64), :])
    return jnp.concatenate(got, axis=0)


def left_turned(left_ref, lt):
    for quad in range(4):
        hi, lo = halves(left_rows(left_ref, quad).T)
        for p in range(4):
            for m in range(4):
                at = quad * 128 + ((p + m) % 4) * 32
                lt[m, at : at + 32, 0:128] = hi[p * 32 : p * 32 + 32]
                lt[m, at : at + 32, 128:256] = lo[p * 32 : p * 32 + 32]


def weights_by_class(w_ref, w_hl):
    for e in range(32):
        hi, lo = halves(w_ref[pl.ds(e, 32, stride=32), :])
        for d in range(4):
            at = (e // 4) * 128 + ((e % 4 + d) % 4) * 32
            w_hl[d, at : at + 32, 0:128] = hi
            w_hl[d, at : at + 32, 128:256] = lo


def cotangent_kernel(w_ref, cot_ref, g_hi, g_lo, cot_t, wide_t, w_hl, w_cat, cot_cat):
    weights_by_class(w_ref, w_hl)
    for d in range(4):
        for quad in range(4):
            hi, lo = halves(cot_ref[quad * 4 + d])
            cot_cat[d, quad * 64 : quad * 64 + 64, 0:128] = hi
            cot_cat[d, quad * 64 : quad * 64 + 64, 128:256] = hi
            cot_cat[d, quad * 64 : quad * 64 + 64, 256:384] = lo
    for d in range(4):
        hi, lo = halves(jnp.concatenate([cot_ref[quad * 4 + d] for quad in range(4)], axis=0).T)
        cot_t[d, 0:128, :] = hi
        cot_t[d, 128:256, :] = lo
    for d in range(4):
        w_cat[:, 0:256] = w_hl[d]
        w_cat[:, 256:384] = w_hl[d, :, 0:128]
        wide_t[d] = lax.dot_general(
            cot_cat[d], w_cat[...], (((1,), (1,)), ((), ())), preferred_element_type=f32
        )
    for block in range(8):
        h, g = block // 4, block % 4
        at = g * 128 + h * 64
        for quad in range(4):
            parts = [
                wide_t[d, quad * 64 : quad * 64 + 64, block * 128 : block * 128 + 128]
                for d in range(4)
            ]
            for m in range(4):
                hi, lo = halves(pick([parts[(p - m) % 4] for p in range(4)]))
                g_hi[m, at : at + 64, quad * 128 : quad * 128 + 128] = hi
                g_lo[m, at : at + 64, quad * 128 : quad * 128 + 128] = lo


def outer_product(left_ref, parts, right_all, outer, lcat, rt, a_hi, a_lo):
    gather_right(parts, right_all)
    for quad in range(4):
        v = left_rows(left_ref, quad)
        for m in range(4):
            hi, lo = halves(pltpu.roll(v, 32 * m, axis=1) if m else v)
            lcat[m, 0:128, quad * 128 : quad * 128 + 128] = hi
            lcat[m, 128:256, quad * 128 : quad * 128 + 128] = lo
            lcat[m, 256:384, quad * 128 : quad * 128 + 128] = hi
    for e in range(16):
        g, m = e // 4, e % 4
        hi, lo = halves(right_rows(right_all, e).T)
        rt[m, g * 128 : g * 128 + 128, 0:128] = hi
        rt[m, g * 128 : g * 128 + 128, 128:256] = hi
        rt[m, g * 128 : g * 128 + 128, 256:384] = lo
    for m in range(4):
        outer[m] = matmul(rt[m], lcat[m])
    for block in range(8):
        h, g = block // 4, block % 4
        at = g * 128 + h * 64
        for quad in range(4):
            parts = [outer[m, at : at + 64, quad * 128 : quad * 128 + 128] for m in range(4)]
            for d in range(4):
                hi, lo = halves(pick([parts[(p - d) % 4] for p in range(4)]))
                a_hi[d, quad * 64 : quad * 64 + 64, block * 128 : block * 128 + 128] = hi
                a_lo[d, quad * 64 : quad * 64 + 64, block * 128 : block * 128 + 128] = lo


def pair_kernel(left_ref, *refs):
    parts, (bias_ref, w_far, pair_ref, right_all, outer, lcat, rt, a_hi, a_lo) = refs[:8], refs[8:17]
    w_hl, w_ref, sems = refs[17:]
    (fetched,) = fetch([(w_far, w_ref)], sems)
    outer_product(left_ref, parts, right_all, outer, lcat, rt, a_hi, a_lo)
    fetched.wait()
    weights_by_class(w_ref, w_hl)
    for d in range(4):
        both = matmul(a_hi[d], w_hl[d])
        pair = both[:, 0:128] + both[:, 128:256] + matmul(a_lo[d], w_hl[d, :, 0:128])
        pair = pair * (1.0 / 128) + bias_ref[...]
        for quad in range(4):
            pair_ref[quad * 4 + d] = pair[quad * 64 : quad * 64 + 64]


def tile_kernel(left_ref, *refs):
    parts, (cot_far, own_out, other_out) = refs[:8], refs[8:11]
    right_all, outer, lcat, rt, a_hi, a_lo, dw, cot_t, sems = refs[11:]
    core = lax.axis_index("core")
    (fetched,) = fetch([(cot_far, cot_t)], sems)
    outer_product(left_ref, parts, right_all, outer, lcat, rt, a_hi, a_lo)
    fetched.wait()
    for d in range(4):
        both = matmul(cot_t[d], a_hi[d])
        part = both[0:128] + both[128:256] + matmul(cot_t[d, 0:128, :], a_lo[d])
        for block in range(8):
            v = part[:, block * 128 : block * 128 + 128]
            if d == 0:
                dw[block] = v
            else:
                dw[block] += pltpu.roll(v, 128 - 32 * d, axis=1)
    for block in range(8):
        dw[block] = dw[block].T
    for block in range(8):
        for p in range(4):
            for out, side in ((own_out, core), (other_out, 1 - core)):
                out[pl.ds(p * 8 + block, 16, stride=BWD), :] = dw[
                    block, pl.ds(p * 32 + side, 16, stride=2), :
                ]


def left_gradient_kernel(*refs):
    parts, (g_hi, g_lo, own_out, other_out, right_all, r_hl) = refs[:8], refs[8:]
    gather_right(parts, right_all)
    for e in range(16):
        g, m = e // 4, e % 4
        hi, lo = halves(right_rows(right_all, e))
        r_hl[m, 0:128, g * 128 : g * 128 + 128] = hi
        r_hl[m, 128:256, g * 128 : g * 128 + 128] = lo
    total = [None] * 4
    for m in range(4):
        both = matmul(r_hl[m], g_hi[m])
        v = both[0:128] + both[128:256] + matmul(r_hl[m, 0:128, :], g_lo[m])
        for quad in range(4):
            part = v[:, quad * 128 : quad * 128 + 128]
            if m:
                part = pltpu.roll(part, 128 - 32 * m, axis=1)
            total[quad] = part if total[quad] is None else total[quad] + part
    for quad in range(4):
        t = total[quad] * (1.0 / 128)
        for half, out in ((0, own_out), (1, other_out)):
            for s in range(4):
                at = (half * 4 + s) * 16
                out[pl.ds(s * 4 + quad, 16, stride=16), :] = t[at : at + 16]


def right_gradient_kernel(left_ref, g_hi, g_lo, *refs):
    outs, (lt, total) = refs[:8], refs[8:]
    left_turned(left_ref, lt)
    for m in range(4):
        both = matmul(g_hi[m], lt[m])
        v = both[:, 0:128] + both[:, 128:256] + matmul(g_lo[m], lt[m, :, 0:128])
        for g in range(4):
            t = v[g * 128 : g * 128 + 128].T * (1.0 / 128)
            for half in range(2):
                for s in range(4):
                    at = (half * 4 + s) * 16
                    row = half * 1024 + s * 16 + g * 4 + m
                    total[pl.ds(row, 16, stride=64), :] = t[at : at + 16]
    for at, ref in enumerate(outs):
        for dz in range(4):
            start = (at // 4) * 1024 + chip_of(dz, at % 4) * 64
            ref[dz] = total[pl.ds(pl.multiple_of(start, 64), 64), :]


def right_kernel(w2_ref, a_ref, b_ref, c_ref, d_ref, out_ref):
    total = (a_ref[...] + b_ref[...]) + (c_ref[...] + d_ref[...])
    for s in range(4):
        part = total[s * 16 : s * 16 + 16, :]
        entries = jnp.concatenate([part[:, 0:64], part[:, 64:128]], axis=0)
        out_ref[s * 64 : s * 64 + 64, :] = contract(entries, w2_ref[...], ((0,), (0,)))


def finish_kernel(x_ref, scale_ref, w1_ref, part_ref, col_ref, out_ref, weight_ref, tmp):
    core = lax.axis_index("core")
    left = col_ref[0]
    for c in range(1, 8):
        left = left + col_ref[c]
    weight_ref[...] = left[64:68] * (1.0 / 512)
    for u in range(4):
        part = contract(left[0:64, u * 32 : u * 32 + 32], w1_ref[...], ((1,), (0,)))
        for q in range(4):
            side = lax.rem(q % 2 + core, 2)
            for s in range(4):
                at = s * 64 + 32 * (q // 2) + 16 * side + u
                block = (q * 4 + s) * 4
                for k in range(2):
                    tmp[k, pl.ds(at, 4, stride=4), :] = part[block : block + 4, k * 128 : k * 128 + 128]
    unit, inverse = standardized(x_ref[...])
    grad = (part_ref[...] + jnp.concatenate([tmp[0], tmp[1]], axis=1)) * scale_ref[...]
    mean = jnp.mean(grad, axis=-1, keepdims=True)
    along = jnp.mean(grad * unit, axis=-1, keepdims=True)
    out_ref[...] = inverse * (grad - mean - unit * along)


def call(kernel, name, outs, scratch, mib, flops, *args, far=(), copies=0):
    shapes = tuple(jax.ShapeDtypeStruct(*out) for out in outs)
    moved = sum(a.size * a.dtype.itemsize for a in args + tuple(far) + shapes)
    return pl.pallas_call(
        kernel,
        out_shape=shapes,
        in_specs=[VMEM] * len(args) + [HBM] * len(far),
        out_specs=(VMEM,) * len(outs),
        scratch_shapes=[pltpu.VMEM(*s) for s in scratch]
        + ([pltpu.SemaphoreType.DMA((copies,))] if copies else []),
        compiler_params=pltpu.CompilerParams(
            vmem_limit_bytes=mib * 1024 * 1024 if mib else None
        ),
        cost_estimate=pl.CostEstimate(flops=flops, bytes_accessed=moved, transcendentals=0),
        name=name,
    )(*args, *far)


def swap_cores(array):
    return lax.ppermute(array, "core", [(0, 1), (1, 0)])


def from_peer(array, axis, apart):
    return lax.ppermute(array, axis, [(i, i ^ apart) for i in range(4)])


def exchange(array, axes):
    return lax.all_to_all(array, axes, 0, 0, tiled=True)


def local(
    sequence_embedding,
    standardize_scale,
    standardize_offset,
    first_operand_matrix,
    first_operand_intercept,
    second_operand_matrix,
    second_operand_intercept,
    result_matrix,
    result_intercept,
    edge_incoming_sensitivity,
):
    x = sequence_embedding.reshape(256, 256)
    scale = standardize_scale.reshape(1, 256)
    w1 = first_operand_matrix.T
    w2 = second_operand_matrix.T
    small = 2 * 256 * 256 * 32 * 6
    step = 2 * 1024 * 1024 * 128 * 3
    offset = standardize_offset.reshape(1, 256)
    (right,) = call(
        project_right_kernel,
        "project_right",
        [((64, 128), f32)],
        [],
        None,
        small,
        x,
        scale,
        offset,
        w2,
        second_operand_intercept.reshape(1, 32),
    )
    (left,) = call(
        project_left_kernel,
        "project_left",
        [((8, 64, 128), f32)],
        [((256, 128), f32)],
        None,
        small,
        x,
        scale,
        offset,
        w1,
        first_operand_intercept.reshape(1, 32),
    )
    right = [right] + [from_peer(right, "zl", dz) for dz in (1, 2, 3)]
    left, right = lax.optimization_barrier((left, right))
    g_hi, g_lo, cot_t = call(
        cotangent_kernel,
        "cotangent",
        [((4, 512, 512), bf16), ((4, 512, 512), bf16), ((4, 256, 256), bf16)],
        [
            ((4, 256, 1024), f32),
            ((4, 1024, 256), bf16),
            ((1024, 384), bf16),
            ((4, 256, 384), bf16),
        ],
        24,
        step,
        result_matrix,
        edge_incoming_sensitivity,
    )
    left = exchange(left, COL).reshape(32, 16, 128)
    right = jnp.stack(right)
    parts = [right] + [from_peer(right, "x", dx) for dx in (1, 2, 3)]
    left, parts, g_hi, g_lo, cot_t = lax.optimization_barrier((left, parts, g_hi, g_lo, cot_t))
    left = exchange(left, ROW).reshape(512, 128)
    parts = parts + [swap_cores(part) for part in parts]
    own_left, other_left = call(
        left_gradient_kernel,
        "left_gradient",
        [((256, 128), f32), ((256, 128), f32)],
        [((2048, 128), f32), ((4, 256, 512), bf16)],
        14,
        step,
        *parts,
        g_hi,
        g_lo,
    )
    got_left = swap_cores(other_left)
    left, own_left, got_left = lax.optimization_barrier((left, own_left, got_left))
    working = [
        ((2048, 128), f32),
        ((4, 512, 512), f32),
        ((4, 384, 512), bf16),
        ((4, 512, 384), bf16),
        ((4, 256, 1024), bf16),
        ((4, 256, 1024), bf16),
    ]
    own, other = call(
        tile_kernel,
        "tile",
        [((16 * BWD, 128), f32)] * 2,
        working + [((8, 128, 128), f32), ((4, 256, 256), bf16)],
        22,
        2 * step,
        left,
        *parts,
        far=(cot_t,),
        copies=1,
    )
    got = swap_cores(other)
    sums = call(
        right_gradient_kernel,
        "right_gradient",
        [((4, 64, 128), f32)] * 8,
        [((4, 512, 256), bf16), ((2048, 128), f32)],
        16,
        step,
        left,
        g_hi,
        g_lo,
    )
    weight = (own + got).reshape(16, BWD, 128)
    sent = [weight, own_left.reshape(16, 16, 128), got_left.reshape(16, 16, 128)]
    back = exchange(jnp.concatenate(sent, axis=1), CHIP)
    sums = [a + swap_cores(b) for a, b in zip(sums[:4], sums[4:])]
    right = sums[0] + sum(from_peer(sums[dx], "x", dx) for dx in (1, 2, 3))
    (pair,) = call(
        pair_kernel,
        "pair",
        [((16, 64, 128), f32)],
        working + [((4, 1024, 256), bf16), ((1024, 128), f32)],
        24,
        2 * step,
        left,
        *parts,
        result_intercept.reshape(1, 128),
        far=(result_matrix,),
        copies=1,
    )
    weight = back[:, :32].sum(axis=0).reshape(4, 8, 128).transpose(1, 0, 2)
    sent = jnp.concatenate(
        [back[:, 32:].reshape(8, 64, 128), jnp.pad(weight, ((0, 0), (0, 4), (0, 0)))], axis=1
    )
    sent, right = lax.optimization_barrier((sent, right))
    cols = exchange(sent, COL)
    right = [right[0]] + [from_peer(right[dz], "zl", dz) for dz in (1, 2, 3)]
    (part,) = call(right_kernel, "right", [((256, 256), f32)], [], 8, small, w2, *right)
    grad, weight = call(
        finish_kernel,
        "finish",
        [((256, 256), f32), ((4, 128), f32)],
        [((2, 256, 128), f32)],
        8,
        small,
        x,
        scale,
        w1,
        part,
        cols,
    )
    return pair, grad.reshape(4, 64, 256), weight


def solution(mesh):
    fine = Mesh(mesh.devices.reshape(SIZES), NAMES)
    tile = P(ROW, COL, None)
    return jax.shard_map(
        local,
        mesh=fine,
        in_specs=(tile, P(), P(), P(), P(), P(), P(), P(), P(), tile),
        out_specs=(tile, tile, P(ROW + COL, None)),
        check_vma=False,
    )
```

```python
import jax
import jax.numpy as jnp
from jax import lax
from jax.experimental import pallas as pl
from jax.experimental.pallas import tpu as pltpu
from jax.sharding import Mesh, PartitionSpec as P

exact = lax.Precision.HIGHEST
f32 = jnp.float32
bf16 = jnp.bfloat16

SIZES = (4, 4, 2, 2, 4)
NAMES = ("zl", "x", "core", "zh", "y")
CHIP = ("zl", "x")
ROW = ("zl", "x", "core")
COL = ("zh", "y")
VMEM = pl.BlockSpec(memory_space=pltpu.VMEM)
HBM = pl.BlockSpec(memory_space=pltpu.HBM)

BWD = 32


def contract(a, b, dims):
    return lax.dot_general(a, b, (dims, ((), ())), precision=exact, preferred_element_type=f32)


def matmul(a, b):
    return lax.dot_general(a, b, (((1,), (0,)), ((), ())), preferred_element_type=f32)


def halves(v):
    high = v.astype(bf16)
    return high, (v - high.astype(f32)).astype(bf16)


def standardized(x):
    demeaned = x - jnp.mean(x, axis=-1, keepdims=True)
    variance = jnp.mean(demeaned * demeaned, axis=-1, keepdims=True)
    inverse = lax.rsqrt(variance + 1e-05)
    return demeaned * inverse, inverse


def project_right_kernel(x_ref, scale_ref, offset_ref, w2_ref, b2_ref, right_ref):
    normed = standardized(x_ref[...])[0] * scale_ref[...] + offset_ref[...]
    on = lax.broadcasted_iota(jnp.int32, (32, 32), 0) == lax.broadcasted_iota(jnp.int32, (32, 32), 1)
    b2 = jnp.sum(jnp.where(on, b2_ref[...], 0.0), axis=1, keepdims=True)
    right = contract(w2_ref[...], normed, ((1,), (1,))) + b2
    for s in range(4):
        cols = right[:, s * 64 : s * 64 + 64]
        right_ref[s * 16 : s * 16 + 16, :] = jnp.concatenate([cols[0:16], cols[16:32]], axis=1)


def project_left_kernel(x_ref, scale_ref, offset_ref, w1_ref, b1_ref, left_ref, tmp):
    normed = standardized(x_ref[...])[0] * scale_ref[...] + offset_ref[...]
    tmp[:, 0:32] = contract(normed, w1_ref[...], ((1,), (1,))) + b1_ref[...]
    wide = jnp.concatenate([tmp[pl.ds(u, 64, stride=4), :][:, 0:32] for u in range(4)], axis=1)
    for q in range(4):
        part = jnp.concatenate([wide[s * 16 + q * 4 : s * 16 + q * 4 + 4] for s in range(4)], axis=0)
        for copy in range(8):
            left_ref[copy, q * 16 : q * 16 + 16, :] = part


def fetch(pairs, sems):
    copies = [pltpu.make_async_copy(a, b, sems.at[i]) for i, (a, b) in enumerate(pairs)]
    for copy in copies:
        copy.start()
    return copies


def pick(parts):
    chunk = lax.broadcasted_iota(jnp.int32, (64, 128), 1) // 32
    low = jnp.where(chunk == 0, parts[0], parts[1])
    return jnp.where(chunk < 2, low, jnp.where(chunk == 2, parts[2], parts[3]))


def chip_of(dz, dx):
    return jnp.bitwise_xor(lax.axis_index("zl"), dz) * 4 + jnp.bitwise_xor(lax.axis_index("x"), dx)


def left_rows(left_ref, quad):
    core = lax.axis_index("core")
    got = []
    for side in (core, 1 - core):
        for s in range(4):
            got.append(left_ref[pl.ds(side * 16 + s * 4 + quad, 16, stride=32), :])
    return jnp.concatenate(got, axis=0)


def gather_right(parts, right_all):
    for at, ref in enumerate(parts):
        for dz in range(4):
            start = (at // 4) * 1024 + chip_of(dz, at % 4) * 64
            right_all[pl.ds(pl.multiple_of(start, 64), 64), :] = ref[dz]


def right_rows(right_all, e):
    got = []
    for half in range(2):
        for s in range(4):
            got.append(right_all[pl.ds(half * 1024 + s * 16 + e, 16, stride=64), :])
    return jnp.concatenate(got, axis=0)


def left_turned(left_ref, lt):
    for quad in range(4):
        hi, lo = halves(left_rows(left_ref, quad).T)
        for p in range(4):
            for m in range(4):
                at = quad * 128 + ((p + m) % 4) * 32
                lt[m, at : at + 32, 0:128] = hi[p * 32 : p * 32 + 32]
                lt[m, at : at + 32, 128:256] = lo[p * 32 : p * 32 + 32]


def weights_by_class(w_ref, w_hl):
    for e in range(32):
        hi, lo = halves(w_ref[pl.ds(e, 32, stride=32), :])
        for d in range(4):
            at = (e // 4) * 128 + ((e % 4 + d) % 4) * 32
            w_hl[d, at : at + 32, 0:128] = hi
            w_hl[d, at : at + 32, 128:256] = lo


def cotangent_kernel(w_far, cot_far, g_hi, g_lo, wide_t, w_hl, w_cat, cot_cat, w_ref, cot_ref, sems):
    copies = fetch([(w_far, w_ref), (cot_far, cot_ref)], sems)
    copies[0].wait()
    weights_by_class(w_ref, w_hl)
    copies[1].wait()
    for d in range(4):
        for quad in range(4):
            hi, lo = halves(cot_ref[quad * 4 + d])
            cot_cat[d, quad * 64 : quad * 64 + 64, 0:128] = hi
            cot_cat[d, quad * 64 : quad * 64 + 64, 128:256] = hi
            cot_cat[d, quad * 64 : quad * 64 + 64, 256:384] = lo
    for d in range(4):
        w_cat[:, 0:256] = w_hl[d]
        w_cat[:, 256:384] = w_hl[d, :, 0:128]
        wide_t[d] = lax.dot_general(
            cot_cat[d], w_cat[...], (((1,), (1,)), ((), ())), preferred_element_type=f32
        )
    for block in range(8):
        h, g = block // 4, block % 4
        at = g * 128 + h * 64
        for quad in range(4):
            parts = [
                wide_t[d, quad * 64 : quad * 64 + 64, block * 128 : block * 128 + 128]
                for d in range(4)
            ]
            for m in range(4):
                hi, lo = halves(pick([parts[(p - m) % 4] for p in range(4)]))
                g_hi[m, at : at + 64, quad * 128 : quad * 128 + 128] = hi
                g_lo[m, at : at + 64, quad * 128 : quad * 128 + 128] = lo


def outer_product(left_ref, parts, right_all, outer, lcat, rt, a_hi, a_lo):
    gather_right(parts, right_all)
    for quad in range(4):
        v = left_rows(left_ref, quad)
        for m in range(4):
            hi, lo = halves(pltpu.roll(v, 32 * m, axis=1) if m else v)
            lcat[m, 0:128, quad * 128 : quad * 128 + 128] = hi
            lcat[m, 128:256, quad * 128 : quad * 128 + 128] = lo
            lcat[m, 256:384, quad * 128 : quad * 128 + 128] = hi
    for e in range(16):
        g, m = e // 4, e % 4
        hi, lo = halves(right_rows(right_all, e).T)
        rt[m, g * 128 : g * 128 + 128, 0:128] = hi
        rt[m, g * 128 : g * 128 + 128, 128:256] = hi
        rt[m, g * 128 : g * 128 + 128, 256:384] = lo
    for m in range(4):
        outer[m] = matmul(rt[m], lcat[m])
    for block in range(8):
        h, g = block // 4, block % 4
        at = g * 128 + h * 64
        for quad in range(4):
            parts = [outer[m, at : at + 64, quad * 128 : quad * 128 + 128] for m in range(4)]
            for d in range(4):
                hi, lo = halves(pick([parts[(p - d) % 4] for p in range(4)]))
                a_hi[d, quad * 64 : quad * 64 + 64, block * 128 : block * 128 + 128] = hi
                a_lo[d, quad * 64 : quad * 64 + 64, block * 128 : block * 128 + 128] = lo


def pair_kernel(left_ref, *refs):
    parts, (bias_ref, w_far, pair_ref, right_all, outer, lcat, rt, a_hi, a_lo) = refs[:8], refs[8:17]
    w_hl, w_ref, sems = refs[17:]
    (fetched,) = fetch([(w_far, w_ref)], sems)
    outer_product(left_ref, parts, right_all, outer, lcat, rt, a_hi, a_lo)
    fetched.wait()
    weights_by_class(w_ref, w_hl)
    for d in range(4):
        both = matmul(a_hi[d], w_hl[d])
        pair = both[:, 0:128] + both[:, 128:256] + matmul(a_lo[d], w_hl[d, :, 0:128])
        pair = pair * (1.0 / 128) + bias_ref[...]
        for quad in range(4):
            pair_ref[quad * 4 + d] = pair[quad * 64 : quad * 64 + 64]


def tile_kernel(left_ref, *refs):
    parts, (cot_far, own_out, other_out) = refs[:8], refs[8:11]
    right_all, outer, lcat, rt, a_hi, a_lo, dw, cot_ref, sems = refs[11:]
    core = lax.axis_index("core")
    (fetched,) = fetch([(cot_far, cot_ref)], sems)
    outer_product(left_ref, parts, right_all, outer, lcat, rt, a_hi, a_lo)
    fetched.wait()
    for d in range(4):
        hi, lo = halves(jnp.concatenate([cot_ref[quad * 4 + d] for quad in range(4)], axis=0).T)
        both = matmul(jnp.concatenate([hi, lo], axis=0), a_hi[d])
        part = both[0:128] + both[128:256] + matmul(hi, a_lo[d])
        for block in range(8):
            v = part[:, block * 128 : block * 128 + 128]
            if d == 0:
                dw[block] = v
            else:
                dw[block] += pltpu.roll(v, 128 - 32 * d, axis=1)
    for block in range(8):
        dw[block] = dw[block].T
    for block in range(8):
        for p in range(4):
            for out, side in ((own_out, core), (other_out, 1 - core)):
                out[pl.ds(p * 8 + block, 16, stride=BWD), :] = dw[
                    block, pl.ds(p * 32 + side, 16, stride=2), :
                ]


def left_gradient_kernel(*refs):
    parts, (hi_far, lo_far, own_out, other_out, right_all, r_hl, g_hi, g_lo, sems) = refs[:8], refs[8:]
    copies = fetch([(hi_far, g_hi), (lo_far, g_lo)], sems)
    gather_right(parts, right_all)
    for e in range(16):
        g, m = e // 4, e % 4
        hi, lo = halves(right_rows(right_all, e))
        r_hl[m, 0:128, g * 128 : g * 128 + 128] = hi
        r_hl[m, 128:256, g * 128 : g * 128 + 128] = lo
    for copy in copies:
        copy.wait()
    total = [None] * 4
    for m in range(4):
        both = matmul(r_hl[m], g_hi[m])
        v = both[0:128] + both[128:256] + matmul(r_hl[m, 0:128, :], g_lo[m])
        for quad in range(4):
            part = v[:, quad * 128 : quad * 128 + 128]
            if m:
                part = pltpu.roll(part, 128 - 32 * m, axis=1)
            total[quad] = part if total[quad] is None else total[quad] + part
    for quad in range(4):
        t = total[quad] * (1.0 / 128)
        for half, out in ((0, own_out), (1, other_out)):
            for s in range(4):
                at = (half * 4 + s) * 16
                out[pl.ds(s * 4 + quad, 16, stride=16), :] = t[at : at + 16]


def right_gradient_kernel(left_ref, hi_far, lo_far, *refs):
    outs, (lt, total, g_hi, g_lo, sems) = refs[:8], refs[8:]
    copies = fetch([(hi_far, g_hi), (lo_far, g_lo)], sems)
    left_turned(left_ref, lt)
    for copy in copies:
        copy.wait()
    for m in range(4):
        both = matmul(g_hi[m], lt[m])
        v = both[:, 0:128] + both[:, 128:256] + matmul(g_lo[m], lt[m, :, 0:128])
        for g in range(4):
            t = v[g * 128 : g * 128 + 128].T * (1.0 / 128)
            for half in range(2):
                for s in range(4):
                    at = (half * 4 + s) * 16
                    row = half * 1024 + s * 16 + g * 4 + m
                    total[pl.ds(row, 16, stride=64), :] = t[at : at + 16]
    for at, ref in enumerate(outs):
        for dz in range(4):
            start = (at // 4) * 1024 + chip_of(dz, at % 4) * 64
            ref[dz] = total[pl.ds(pl.multiple_of(start, 64), 64), :]


def right_kernel(w2_ref, a_ref, b_ref, c_ref, d_ref, out_ref):
    total = (a_ref[...] + b_ref[...]) + (c_ref[...] + d_ref[...])
    for s in range(4):
        part = total[s * 16 : s * 16 + 16, :]
        entries = jnp.concatenate([part[:, 0:64], part[:, 64:128]], axis=0)
        out_ref[s * 64 : s * 64 + 64, :] = contract(entries, w2_ref[...], ((0,), (0,)))


def finish_kernel(x_ref, scale_ref, w1_ref, part_ref, col_ref, out_ref, weight_ref, tmp):
    core = lax.axis_index("core")
    left = col_ref[0]
    for c in range(1, 8):
        left = left + col_ref[c]
    weight_ref[...] = left[64:68] * (1.0 / 512)
    for u in range(4):
        part = contract(left[0:64, u * 32 : u * 32 + 32], w1_ref[...], ((1,), (0,)))
        for q in range(4):
            side = lax.rem(q % 2 + core, 2)
            for s in range(4):
                at = s * 64 + 32 * (q // 2) + 16 * side + u
                block = (q * 4 + s) * 4
                for k in range(2):
                    tmp[k, pl.ds(at, 4, stride=4), :] = part[block : block + 4, k * 128 : k * 128 + 128]
    unit, inverse = standardized(x_ref[...])
    grad = (part_ref[...] + jnp.concatenate([tmp[0], tmp[1]], axis=1)) * scale_ref[...]
    mean = jnp.mean(grad, axis=-1, keepdims=True)
    along = jnp.mean(grad * unit, axis=-1, keepdims=True)
    out_ref[...] = inverse * (grad - mean - unit * along)


def call(kernel, name, outs, scratch, mib, flops, *args, far=(), copies=0):
    shapes = tuple(jax.ShapeDtypeStruct(*out) for out in outs)
    moved = sum(a.size * a.dtype.itemsize for a in args + tuple(far) + shapes)
    return pl.pallas_call(
        kernel,
        out_shape=shapes,
        in_specs=[VMEM] * len(args) + [HBM] * len(far),
        out_specs=(VMEM,) * len(outs),
        scratch_shapes=[pltpu.VMEM(*s) for s in scratch]
        + ([pltpu.SemaphoreType.DMA((copies,))] if copies else []),
        compiler_params=pltpu.CompilerParams(
            vmem_limit_bytes=mib * 1024 * 1024 if mib else None
        ),
        cost_estimate=pl.CostEstimate(flops=flops, bytes_accessed=moved, transcendentals=0),
        name=name,
    )(*args, *far)


def swap_cores(array):
    return lax.ppermute(array, "core", [(0, 1), (1, 0)])


def from_peer(array, axis, apart):
    return lax.ppermute(array, axis, [(i, i ^ apart) for i in range(4)])


def exchange(array, axes):
    return lax.all_to_all(array, axes, 0, 0, tiled=True)


def local(
    sequence_embedding,
    standardize_scale,
    standardize_offset,
    first_operand_matrix,
    first_operand_intercept,
    second_operand_matrix,
    second_operand_intercept,
    result_matrix,
    result_intercept,
    edge_incoming_sensitivity,
):
    x = sequence_embedding.reshape(256, 256)
    scale = standardize_scale.reshape(1, 256)
    w1 = first_operand_matrix.T
    w2 = second_operand_matrix.T
    small = 2 * 256 * 256 * 32 * 6
    step = 2 * 1024 * 1024 * 128 * 3
    offset = standardize_offset.reshape(1, 256)
    (right,) = call(
        project_right_kernel,
        "project_right",
        [((64, 128), f32)],
        [],
        None,
        small,
        x,
        scale,
        offset,
        w2,
        second_operand_intercept.reshape(1, 32),
    )
    (left,) = call(
        project_left_kernel,
        "project_left",
        [((8, 64, 128), f32)],
        [((256, 128), f32)],
        None,
        small,
        x,
        scale,
        offset,
        w1,
        first_operand_intercept.reshape(1, 32),
    )
    right = [right] + [from_peer(right, "zl", dz) for dz in (1, 2, 3)]
    left, right = lax.optimization_barrier((left, right))
    g_hi, g_lo = call(
        cotangent_kernel,
        "cotangent",
        [((4, 512, 512), bf16), ((4, 512, 512), bf16)],
        [
            ((4, 256, 1024), f32),
            ((4, 1024, 256), bf16),
            ((1024, 384), bf16),
            ((4, 256, 384), bf16),
            ((1024, 128), f32),
            ((16, 64, 128), f32),
        ],
        None,
        step,
        far=(result_matrix, edge_incoming_sensitivity),
        copies=2,
    )
    left = exchange(left, COL).reshape(32, 16, 128)
    right = jnp.stack(right)
    parts = [right] + [from_peer(right, "x", dx) for dx in (1, 2, 3)]
    left, parts, g_hi, g_lo = lax.optimization_barrier((left, parts, g_hi, g_lo))
    left = exchange(left, ROW).reshape(512, 128)
    parts = parts + [swap_cores(part) for part in parts]
    own_left, other_left = call(
        left_gradient_kernel,
        "left_gradient",
        [((256, 128), f32), ((256, 128), f32)],
        [((2048, 128), f32), ((4, 256, 512), bf16)] + [((4, 512, 512), bf16)] * 2,
        52,
        step,
        *parts,
        far=(g_hi, g_lo),
        copies=2,
    )
    got_left = swap_cores(other_left)
    left, own_left, got_left = lax.optimization_barrier((left, own_left, got_left))
    working = [
        ((2048, 128), f32),
        ((4, 512, 512), f32),
        ((4, 384, 512), bf16),
        ((4, 512, 384), bf16),
        ((4, 256, 1024), bf16),
        ((4, 256, 1024), bf16),
    ]
    own, other = call(
        tile_kernel,
        "tile",
        [((16 * BWD, 128), f32)] * 2,
        working + [((8, 128, 128), f32), ((16, 64, 128), f32)],
        52,
        2 * step,
        left,
        *parts,
        far=(edge_incoming_sensitivity,),
        copies=1,
    )
    got = swap_cores(other)
    sums = call(
        right_gradient_kernel,
        "right_gradient",
        [((4, 64, 128), f32)] * 8,
        [((4, 512, 256), bf16), ((2048, 128), f32)] + [((4, 512, 512), bf16)] * 2,
        52,
        step,
        left,
        far=(g_hi, g_lo),
        copies=2,
    )
    weight = (own + got).reshape(16, BWD, 128)
    sent = [weight, own_left.reshape(16, 16, 128), got_left.reshape(16, 16, 128)]
    back = exchange(jnp.concatenate(sent, axis=1), CHIP)
    sums = [a + swap_cores(b) for a, b in zip(sums[:4], sums[4:])]
    right = sums[0] + sum(from_peer(sums[dx], "x", dx) for dx in (1, 2, 3))
    (pair,) = call(
        pair_kernel,
        "pair",
        [((16, 64, 128), f32)],
        working + [((4, 1024, 256), bf16), ((1024, 128), f32)],
        52,
        2 * step,
        left,
        *parts,
        result_intercept.reshape(1, 128),
        far=(result_matrix,),
        copies=1,
    )
    weight = back[:, :32].sum(axis=0).reshape(4, 8, 128).transpose(1, 0, 2)
    sent = jnp.concatenate(
        [back[:, 32:].reshape(8, 64, 128), jnp.pad(weight, ((0, 0), (0, 4), (0, 0)))], axis=1
    )
    sent, right, pair = lax.optimization_barrier((sent, right, pair))
    cols = exchange(sent, COL)
    right = [right[0]] + [from_peer(right[dz], "zl", dz) for dz in (1, 2, 3)]
    (part,) = call(right_kernel, "right", [((256, 256), f32)], [], 8, small, w2, *right)
    grad, weight = call(
        finish_kernel,
        "finish",
        [((256, 256), f32), ((4, 128), f32)],
        [((2, 256, 128), f32)],
        8,
        small,
        x,
        scale,
        w1,
        part,
        cols,
    )
    return pair, grad.reshape(4, 64, 256), weight


def solution(mesh):
    fine = Mesh(mesh.devices.reshape(SIZES), NAMES)
    tile = P(ROW, COL, None)
    return jax.shard_map(
        local,
        mesh=fine,
        in_specs=(tile, P(), P(), P(), P(), P(), P(), P(), P(), tile),
        out_specs=(tile, tile, P(ROW + COL, None)),
        check_vma=False,
    )
```

```python
import jax
import jax.numpy as jnp
from jax import lax
from jax.experimental import pallas as pl
from jax.experimental.pallas import tpu as pltpu
from jax.sharding import Mesh, PartitionSpec as P

exact = lax.Precision.HIGHEST
f32 = jnp.float32
bf16 = jnp.bfloat16

SIZES = (4, 4, 2, 2, 4)
NAMES = ("zl", "x", "core", "zh", "y")
CHIP = ("zl", "x")
ROW = ("zl", "x", "core")
COL = ("zh", "y")
VMEM = pl.BlockSpec(memory_space=pltpu.VMEM)
HBM = pl.BlockSpec(memory_space=pltpu.HBM)

BWD = 32


def contract(a, b, dims):
    return lax.dot_general(a, b, (dims, ((), ())), precision=exact, preferred_element_type=f32)


def matmul(a, b):
    return lax.dot_general(a, b, (((1,), (0,)), ((), ())), preferred_element_type=f32)


def halves(v):
    high = v.astype(bf16)
    return high, (v - high.astype(f32)).astype(bf16)


def standardized(x):
    demeaned = x - jnp.mean(x, axis=-1, keepdims=True)
    variance = jnp.mean(demeaned * demeaned, axis=-1, keepdims=True)
    inverse = lax.rsqrt(variance + 1e-05)
    return demeaned * inverse, inverse


def project_right_kernel(x_ref, scale_ref, offset_ref, w2_ref, b2_ref, right_ref):
    normed = standardized(x_ref[...])[0] * scale_ref[...] + offset_ref[...]
    on = lax.broadcasted_iota(jnp.int32, (32, 32), 0) == lax.broadcasted_iota(jnp.int32, (32, 32), 1)
    b2 = jnp.sum(jnp.where(on, b2_ref[...], 0.0), axis=1, keepdims=True)
    right = contract(w2_ref[...], normed, ((1,), (1,))) + b2
    for s in range(4):
        cols = right[:, s * 64 : s * 64 + 64]
        right_ref[s * 16 : s * 16 + 16, :] = jnp.concatenate([cols[0:16], cols[16:32]], axis=1)


def project_left_kernel(x_ref, scale_ref, offset_ref, w1_ref, b1_ref, left_ref, tmp):
    normed = standardized(x_ref[...])[0] * scale_ref[...] + offset_ref[...]
    tmp[:, 0:32] = contract(normed, w1_ref[...], ((1,), (1,))) + b1_ref[...]
    wide = jnp.concatenate([tmp[pl.ds(u, 64, stride=4), :][:, 0:32] for u in range(4)], axis=1)
    for q in range(4):
        part = jnp.concatenate([wide[s * 16 + q * 4 : s * 16 + q * 4 + 4] for s in range(4)], axis=0)
        for copy in range(8):
            left_ref[copy, q * 16 : q * 16 + 16, :] = part


def fetch(pairs, sems):
    copies = [pltpu.make_async_copy(a, b, sems.at[i]) for i, (a, b) in enumerate(pairs)]
    for copy in copies:
        copy.start()
    return copies


def fetch_classes(hi_far, lo_far, g_hi, g_lo, sems):
    pairs = []
    for m in range(4):
        pairs += [(hi_far.at[m], g_hi.at[m]), (lo_far.at[m], g_lo.at[m])]
    return fetch(pairs, sems)


def pick(parts):
    chunk = lax.broadcasted_iota(jnp.int32, (64, 128), 1) // 32
    low = jnp.where(chunk == 0, parts[0], parts[1])
    return jnp.where(chunk < 2, low, jnp.where(chunk == 2, parts[2], parts[3]))


def chip_of(dz, dx):
    return jnp.bitwise_xor(lax.axis_index("zl"), dz) * 4 + jnp.bitwise_xor(lax.axis_index("x"), dx)


def left_rows(left_ref, quad):
    core = lax.axis_index("core")
    got = []
    for side in (core, 1 - core):
        for s in range(4):
            got.append(left_ref[pl.ds(side * 16 + s * 4 + quad, 16, stride=32), :])
    return jnp.concatenate(got, axis=0)


def gather_right(parts, right_all):
    for at, ref in enumerate(parts):
        for dz in range(4):
            start = (at // 4) * 1024 + chip_of(dz, at % 4) * 64
            right_all[pl.ds(pl.multiple_of(start, 64), 64), :] = ref[dz]


def right_rows(right_all, e):
    got = []
    for half in range(2):
        for s in range(4):
            got.append(right_all[pl.ds(half * 1024 + s * 16 + e, 16, stride=64), :])
    return jnp.concatenate(got, axis=0)


def left_turned(left_ref, lt):
    for quad in range(4):
        hi, lo = halves(left_rows(left_ref, quad).T)
        for p in range(4):
            for m in range(4):
                at = quad * 128 + ((p + m) % 4) * 32
                lt[m, at : at + 32, 0:128] = hi[p * 32 : p * 32 + 32]
                lt[m, at : at + 32, 128:256] = lo[p * 32 : p * 32 + 32]


def weights_by_class(w_ref, w_hl):
    for e in range(32):
        hi, lo = halves(w_ref[pl.ds(e, 32, stride=32), :])
        for d in range(4):
            at = (e // 4) * 128 + ((e % 4 + d) % 4) * 32
            w_hl[d, at : at + 32, 0:128] = hi
            w_hl[d, at : at + 32, 128:256] = lo


def cotangent_kernel(
    w_far, cot_far, hi_far, lo_far, wide_t, w_hl, w_cat, cot_cat, w_ref, cot_ref, g_hi, g_lo, sems
):
    copies = fetch([(w_far, w_ref), (cot_far, cot_ref)], sems)
    copies[0].wait()
    weights_by_class(w_ref, w_hl)
    copies[1].wait()
    for d in range(4):
        for quad in range(4):
            hi, lo = halves(cot_ref[quad * 4 + d])
            cot_cat[d, quad * 64 : quad * 64 + 64, 0:128] = hi
            cot_cat[d, quad * 64 : quad * 64 + 64, 128:256] = hi
            cot_cat[d, quad * 64 : quad * 64 + 64, 256:384] = lo
    for d in range(4):
        w_cat[:, 0:256] = w_hl[d]
        w_cat[:, 256:384] = w_hl[d, :, 0:128]
        wide_t[d] = lax.dot_general(
            cot_cat[d], w_cat[...], (((1,), (1,)), ((), ())), preferred_element_type=f32
        )
    sent = []
    for g in range(4):
        for h in range(2):
            block = h * 4 + g
            at = g * 128 + h * 64
            for quad in range(4):
                parts = [
                    wide_t[d, quad * 64 : quad * 64 + 64, block * 128 : block * 128 + 128]
                    for d in range(4)
                ]
                for m in range(4):
                    hi, lo = halves(pick([parts[(p - m) % 4] for p in range(4)]))
                    g_hi[m, at : at + 64, quad * 128 : quad * 128 + 128] = hi
                    g_lo[m, at : at + 64, quad * 128 : quad * 128 + 128] = lo
        slab = (slice(None), pl.ds(g * 128, 128))
        pairs = [(g_hi.at[slab], hi_far.at[slab]), (g_lo.at[slab], lo_far.at[slab])]
        sent += fetch(pairs, sems.at[pl.ds(2 + 2 * g, 2)])
    for copy in sent:
        copy.wait()


def outer_product(left_ref, rt_far, outer, lcat, a_hi, a_lo, rt, sems):
    copies = fetch([(rt_far.at[m], rt.at[m]) for m in range(4)], sems)
    for quad in range(4):
        v = left_rows(left_ref, quad)
        for m in range(4):
            hi, lo = halves(pltpu.roll(v, 32 * m, axis=1) if m else v)
            lcat[m, 0:128, quad * 128 : quad * 128 + 128] = hi
            lcat[m, 128:256, quad * 128 : quad * 128 + 128] = lo
            lcat[m, 256:384, quad * 128 : quad * 128 + 128] = hi
    for m in range(4):
        copies[m].wait()
        outer[m] = matmul(rt[m], lcat[m])
    for block in range(8):
        h, g = block // 4, block % 4
        at = g * 128 + h * 64
        for quad in range(4):
            parts = [outer[m, at : at + 64, quad * 128 : quad * 128 + 128] for m in range(4)]
            for d in range(4):
                hi, lo = halves(pick([parts[(p - d) % 4] for p in range(4)]))
                a_hi[d, quad * 64 : quad * 64 + 64, block * 128 : block * 128 + 128] = hi
                a_lo[d, quad * 64 : quad * 64 + 64, block * 128 : block * 128 + 128] = lo


def pair_kernel(
    left_ref, bias_ref, rt_far, w_far, pair_ref, outer, lcat, a_hi, a_lo, rt, w_hl, w_ref, sems
):
    (fetched,) = fetch([(w_far, w_ref)], sems)
    outer_product(left_ref, rt_far, outer, lcat, a_hi, a_lo, rt, sems.at[pl.ds(1, 4)])
    fetched.wait()
    weights_by_class(w_ref, w_hl)
    for d in range(4):
        both = matmul(a_hi[d], w_hl[d])
        pair = both[:, 0:128] + both[:, 128:256] + matmul(a_lo[d], w_hl[d, :, 0:128])
        pair = pair * (1.0 / 128) + bias_ref[...]
        for quad in range(4):
            pair_ref[quad * 4 + d] = pair[quad * 64 : quad * 64 + 64]


def tile_kernel(
    left_ref, rt_far, cot_far, own_out, other_out, outer, lcat, a_hi, a_lo, rt, dw, cot_ref, sems
):
    core = lax.axis_index("core")
    (fetched,) = fetch([(cot_far, cot_ref)], sems)
    outer_product(left_ref, rt_far, outer, lcat, a_hi, a_lo, rt, sems.at[pl.ds(1, 4)])
    fetched.wait()
    for d in range(4):
        hi, lo = halves(jnp.concatenate([cot_ref[quad * 4 + d] for quad in range(4)], axis=0).T)
        both = matmul(jnp.concatenate([hi, lo], axis=0), a_hi[d])
        part = both[0:128] + both[128:256] + matmul(hi, a_lo[d])
        for block in range(8):
            v = part[:, block * 128 : block * 128 + 128]
            if d == 0:
                dw[block] = v
            else:
                dw[block] += pltpu.roll(v, 128 - 32 * d, axis=1)
    for block in range(8):
        dw[block] = dw[block].T
    for block in range(8):
        for p in range(4):
            for out, side in ((own_out, core), (other_out, 1 - core)):
                out[pl.ds(p * 8 + block, 16, stride=BWD), :] = dw[
                    block, pl.ds(p * 32 + side, 16, stride=2), :
                ]


def left_gradient_kernel(*refs):
    parts, (hi_far, lo_far, own_out, other_out, rt) = refs[:8], refs[8:13]
    right_all, r_hl, g_hi, g_lo, sems = refs[13:]
    copies = fetch_classes(hi_far, lo_far, g_hi, g_lo, sems)
    gather_right(parts, right_all)
    for e in range(16):
        g, m = e // 4, e % 4
        v = right_rows(right_all, e)
        hi, lo = halves(v)
        r_hl[m, 0:128, g * 128 : g * 128 + 128] = hi
        r_hl[m, 128:256, g * 128 : g * 128 + 128] = lo
        hi, lo = halves(v.T)
        rt[m, g * 128 : g * 128 + 128, 0:128] = hi
        rt[m, g * 128 : g * 128 + 128, 128:256] = hi
        rt[m, g * 128 : g * 128 + 128, 256:384] = lo
    total = [None] * 4
    for m in range(4):
        copies[2 * m].wait()
        copies[2 * m + 1].wait()
        both = matmul(r_hl[m], g_hi[m])
        v = both[0:128] + both[128:256] + matmul(r_hl[m, 0:128, :], g_lo[m])
        for quad in range(4):
            part = v[:, quad * 128 : quad * 128 + 128]
            if m:
                part = pltpu.roll(part, 128 - 32 * m, axis=1)
            total[quad] = part if total[quad] is None else total[quad] + part
    for quad in range(4):
        t = total[quad] * (1.0 / 128)
        for half, out in ((0, own_out), (1, other_out)):
            for s in range(4):
                at = (half * 4 + s) * 16
                out[pl.ds(s * 4 + quad, 16, stride=16), :] = t[at : at + 16]


def right_gradient_kernel(left_ref, hi_far, lo_far, *refs):
    outs, (lt, total, g_hi, g_lo, sems) = refs[:8], refs[8:]
    copies = fetch_classes(hi_far, lo_far, g_hi, g_lo, sems)
    left_turned(left_ref, lt)
    for m in range(4):
        copies[2 * m].wait()
        copies[2 * m + 1].wait()
        both = matmul(g_hi[m], lt[m])
        v = both[:, 0:128] + both[:, 128:256] + matmul(g_lo[m], lt[m, :, 0:128])
        for g in range(4):
            t = v[g * 128 : g * 128 + 128].T * (1.0 / 128)
            for half in range(2):
                for s in range(4):
                    at = (half * 4 + s) * 16
                    row = half * 1024 + s * 16 + g * 4 + m
                    total[pl.ds(row, 16, stride=64), :] = t[at : at + 16]
    for at, ref in enumerate(outs):
        for dz in range(4):
            start = (at // 4) * 1024 + chip_of(dz, at % 4) * 64
            ref[dz] = total[pl.ds(pl.multiple_of(start, 64), 64), :]


def right_kernel(w2_ref, a_ref, b_ref, c_ref, d_ref, out_ref):
    total = (a_ref[...] + b_ref[...]) + (c_ref[...] + d_ref[...])
    for s in range(4):
        part = total[s * 16 : s * 16 + 16, :]
        entries = jnp.concatenate([part[:, 0:64], part[:, 64:128]], axis=0)
        out_ref[s * 64 : s * 64 + 64, :] = contract(entries, w2_ref[...], ((0,), (0,)))


def finish_kernel(x_ref, scale_ref, w1_ref, part_ref, col_ref, out_ref, weight_ref, tmp):
    core = lax.axis_index("core")
    left = col_ref[0]
    for c in range(1, 8):
        left = left + col_ref[c]
    weight_ref[...] = left[64:68] * (1.0 / 512)
    for u in range(4):
        part = contract(left[0:64, u * 32 : u * 32 + 32], w1_ref[...], ((1,), (0,)))
        for q in range(4):
            side = lax.rem(q % 2 + core, 2)
            for s in range(4):
                at = s * 64 + 32 * (q // 2) + 16 * side + u
                block = (q * 4 + s) * 4
                for k in range(2):
                    tmp[k, pl.ds(at, 4, stride=4), :] = part[block : block + 4, k * 128 : k * 128 + 128]
    unit, inverse = standardized(x_ref[...])
    grad = (part_ref[...] + jnp.concatenate([tmp[0], tmp[1]], axis=1)) * scale_ref[...]
    mean = jnp.mean(grad, axis=-1, keepdims=True)
    along = jnp.mean(grad * unit, axis=-1, keepdims=True)
    out_ref[...] = inverse * (grad - mean - unit * along)


def call(kernel, name, outs, scratch, mib, flops, *args, far=(), far_outs=0, copies=0):
    shapes = tuple(jax.ShapeDtypeStruct(*out) for out in outs)
    moved = sum(a.size * a.dtype.itemsize for a in args + tuple(far) + shapes)
    return pl.pallas_call(
        kernel,
        out_shape=shapes,
        in_specs=[VMEM] * len(args) + [HBM] * len(far),
        out_specs=(VMEM,) * (len(outs) - far_outs) + (HBM,) * far_outs,
        scratch_shapes=[pltpu.VMEM(*s) for s in scratch]
        + ([pltpu.SemaphoreType.DMA((copies,))] if copies else []),
        compiler_params=pltpu.CompilerParams(
            vmem_limit_bytes=mib * 1024 * 1024 if mib else None
        ),
        cost_estimate=pl.CostEstimate(flops=flops, bytes_accessed=moved, transcendentals=0),
        name=name,
    )(*args, *far)


def swap_cores(array):
    return lax.ppermute(array, "core", [(0, 1), (1, 0)])


def from_peer(array, axis, apart):
    return lax.ppermute(array, axis, [(i, i ^ apart) for i in range(4)])


def exchange(array, axes):
    return lax.all_to_all(array, axes, 0, 0, tiled=True)


def local(
    sequence_embedding,
    standardize_scale,
    standardize_offset,
    first_operand_matrix,
    first_operand_intercept,
    second_operand_matrix,
    second_operand_intercept,
    result_matrix,
    result_intercept,
    edge_incoming_sensitivity,
):
    x = sequence_embedding.reshape(256, 256)
    scale = standardize_scale.reshape(1, 256)
    w1 = first_operand_matrix.T
    w2 = second_operand_matrix.T
    small = 2 * 256 * 256 * 32 * 6
    step = 2 * 1024 * 1024 * 128 * 3
    offset = standardize_offset.reshape(1, 256)
    (right,) = call(
        project_right_kernel,
        "project_right",
        [((64, 128), f32)],
        [],
        None,
        small,
        x,
        scale,
        offset,
        w2,
        second_operand_intercept.reshape(1, 32),
    )
    (left,) = call(
        project_left_kernel,
        "project_left",
        [((8, 64, 128), f32)],
        [((256, 128), f32)],
        None,
        small,
        x,
        scale,
        offset,
        w1,
        first_operand_intercept.reshape(1, 32),
    )
    right = [right] + [from_peer(right, "zl", dz) for dz in (1, 2, 3)]
    left, right = lax.optimization_barrier((left, right))
    g_hi, g_lo = call(
        cotangent_kernel,
        "cotangent",
        [((4, 512, 512), bf16), ((4, 512, 512), bf16)],
        [
            ((4, 256, 1024), f32),
            ((4, 1024, 256), bf16),
            ((1024, 384), bf16),
            ((4, 256, 384), bf16),
            ((1024, 128), f32),
            ((16, 64, 128), f32),
        ]
        + [((4, 512, 512), bf16)] * 2,
        None,
        step,
        far=(result_matrix, edge_incoming_sensitivity),
        far_outs=2,
        copies=10,
    )
    left = exchange(left, COL).reshape(32, 16, 128)
    right = jnp.stack(right)
    parts = [right] + [from_peer(right, "x", dx) for dx in (1, 2, 3)]
    left, parts, g_hi, g_lo = lax.optimization_barrier((left, parts, g_hi, g_lo))
    left = exchange(left, ROW).reshape(512, 128)
    parts = parts + [swap_cores(part) for part in parts]
    own_left, other_left, turned = call(
        left_gradient_kernel,
        "left_gradient",
        [((256, 128), f32), ((256, 128), f32), ((4, 512, 384), bf16)],
        [((2048, 128), f32), ((4, 256, 512), bf16)] + [((4, 512, 512), bf16)] * 2,
        52,
        step,
        *parts,
        far=(g_hi, g_lo),
        copies=8,
    )
    got_left = swap_cores(other_left)
    left, own_left, got_left = lax.optimization_barrier((left, own_left, got_left))
    working = [
        ((4, 512, 512), f32),
        ((4, 384, 512), bf16),
        ((4, 256, 1024), bf16),
        ((4, 256, 1024), bf16),
        ((4, 512, 384), bf16),
    ]
    own, other = call(
        tile_kernel,
        "tile",
        [((16 * BWD, 128), f32)] * 2,
        working + [((8, 128, 128), f32), ((16, 64, 128), f32)],
        53,
        2 * step,
        left,
        far=(turned, edge_incoming_sensitivity),
        copies=5,
    )
    got = swap_cores(other)
    sums = call(
        right_gradient_kernel,
        "right_gradient",
        [((4, 64, 128), f32)] * 8,
        [((4, 512, 256), bf16), ((2048, 128), f32)] + [((4, 512, 512), bf16)] * 2,
        52,
        step,
        left,
        far=(g_hi, g_lo),
        copies=8,
    )
    weight = (own + got).reshape(16, BWD, 128)
    sent = [weight, own_left.reshape(16, 16, 128), got_left.reshape(16, 16, 128)]
    back = exchange(jnp.concatenate(sent, axis=1), CHIP)
    sums = [a + swap_cores(b) for a, b in zip(sums[:4], sums[4:])]
    right = sums[0] + sum(from_peer(sums[dx], "x", dx) for dx in (1, 2, 3))
    (pair,) = call(
        pair_kernel,
        "pair",
        [((16, 64, 128), f32)],
        working + [((4, 1024, 256), bf16), ((1024, 128), f32)],
        52,
        2 * step,
        left,
        result_intercept.reshape(1, 128),
        far=(turned, result_matrix),
        copies=5,
    )
    weight = back[:, :32].sum(axis=0).reshape(4, 8, 128).transpose(1, 0, 2)
    sent = jnp.concatenate(
        [back[:, 32:].reshape(8, 64, 128), jnp.pad(weight, ((0, 0), (0, 4), (0, 0)))], axis=1
    )
    sent, right, pair = lax.optimization_barrier((sent, right, pair))
    cols = exchange(sent, COL)
    right = [right[0]] + [from_peer(right[dz], "zl", dz) for dz in (1, 2, 3)]
    (part,) = call(right_kernel, "right", [((256, 256), f32)], [], 8, small, w2, *right)
    grad, weight = call(
        finish_kernel,
        "finish",
        [((256, 256), f32), ((4, 128), f32)],
        [((2, 256, 128), f32)],
        8,
        small,
        x,
        scale,
        w1,
        part,
        cols,
    )
    return pair, grad.reshape(4, 64, 256), weight


def solution(mesh):
    fine = Mesh(mesh.devices.reshape(SIZES), NAMES)
    tile = P(ROW, COL, None)
    return jax.shard_map(
        local,
        mesh=fine,
        in_specs=(tile, P(), P(), P(), P(), P(), P(), P(), P(), tile),
        out_specs=(tile, tile, P(ROW + COL, None)),
        check_vma=False,
    )
```

```python
import jax
import jax.numpy as jnp
from jax import lax
from jax.experimental import pallas as pl
from jax.experimental.pallas import tpu as pltpu
from jax.sharding import Mesh, PartitionSpec as P

exact = lax.Precision.HIGHEST
f32 = jnp.float32
bf16 = jnp.bfloat16

SIZES = (4, 4, 2, 2, 4)
NAMES = ("zl", "x", "core", "zh", "y")
CHIP = ("zl", "x")
ROW = ("zl", "x", "core")
COL = ("zh", "y")
VMEM = pl.BlockSpec(memory_space=pltpu.VMEM)
HBM = pl.BlockSpec(memory_space=pltpu.HBM)

BWD = 48


def contract(a, b, dims):
    return lax.dot_general(a, b, (dims, ((), ())), precision=exact, preferred_element_type=f32)


def matmul(a, b):
    return lax.dot_general(a, b, (((1,), (0,)), ((), ())), preferred_element_type=f32)


def halves(v):
    high = v.astype(bf16)
    return high, (v - high.astype(f32)).astype(bf16)


def standardized(x):
    demeaned = x - jnp.mean(x, axis=-1, keepdims=True)
    variance = jnp.mean(demeaned * demeaned, axis=-1, keepdims=True)
    inverse = lax.rsqrt(variance + 1e-05)
    return demeaned * inverse, inverse


def project_kernel(x_ref, scale_ref, offset_ref, w1_ref, b1_ref, w2_ref, b2_ref, left_ref, right_ref, tmp):
    normed = standardized(x_ref[...])[0] * scale_ref[...] + offset_ref[...]
    tmp[:, 0:32] = contract(normed, w1_ref[...], ((1,), (1,))) + b1_ref[...]
    wide = jnp.concatenate([tmp[pl.ds(u, 64, stride=4), :][:, 0:32] for u in range(4)], axis=1)
    for q in range(4):
        part = jnp.concatenate([wide[s * 16 + q * 4 : s * 16 + q * 4 + 4] for s in range(4)], axis=0)
        for copy in range(8):
            left_ref[copy, q * 16 : q * 16 + 16, :] = part
    on = lax.broadcasted_iota(jnp.int32, (32, 32), 0) == lax.broadcasted_iota(jnp.int32, (32, 32), 1)
    b2 = jnp.sum(jnp.where(on, b2_ref[...], 0.0), axis=1, keepdims=True)
    right = contract(w2_ref[...], normed, ((1,), (1,))) + b2
    for s in range(4):
        cols = right[:, s * 64 : s * 64 + 64]
        right_ref[s * 16 : s * 16 + 16, :] = jnp.concatenate([cols[0:16], cols[16:32]], axis=1)


def fetch(pairs, sems):
    copies = [pltpu.make_async_copy(a, b, sems.at[i]) for i, (a, b) in enumerate(pairs)]
    for copy in copies:
        copy.start()
    return copies


def pick(parts):
    chunk = lax.broadcasted_iota(jnp.int32, (64, 128), 1) // 32
    low = jnp.where(chunk == 0, parts[0], parts[1])
    return jnp.where(chunk < 2, low, jnp.where(chunk == 2, parts[2], parts[3]))


def chip_of(dz, dx):
    return jnp.bitwise_xor(lax.axis_index("zl"), dz) * 4 + jnp.bitwise_xor(lax.axis_index("x"), dx)


def left_rows(left_ref, quad):
    core = lax.axis_index("core")
    got = []
    for side in (core, 1 - core):
        for s in range(4):
            got.append(left_ref[pl.ds(side * 16 + s * 4 + quad, 16, stride=32), :])
    return jnp.concatenate(got, axis=0)


def gather_right(parts, right_all):
    for at, ref in enumerate(parts):
        for dz in range(4):
            start = (at // 4) * 1024 + chip_of(dz, at % 4) * 64
            right_all[pl.ds(pl.multiple_of(start, 64), 64), :] = ref[dz]


def right_rows(right_all, e):
    got = []
    for half in range(2):
        for s in range(4):
            got.append(right_all[pl.ds(half * 1024 + s * 16 + e, 16, stride=64), :])
    return jnp.concatenate(got, axis=0)


def left_turned(left_ref, lt):
    for quad in range(4):
        hi, lo = halves(left_rows(left_ref, quad).T)
        for p in range(4):
            for m in range(4):
                at = quad * 128 + ((p + m) % 4) * 32
                lt[m, at : at + 32, 0:128] = hi[p * 32 : p * 32 + 32]
                lt[m, at : at + 32, 128:256] = lo[p * 32 : p * 32 + 32]


def weights_by_class(w_ref, w_hl):
    for e in range(32):
        hi, lo = halves(w_ref[pl.ds(e, 32, stride=32), :])
        for d in range(4):
            at = (e // 4) * 128 + ((e % 4 + d) % 4) * 32
            w_hl[d, at : at + 32, 0:128] = hi
            w_hl[d, at : at + 32, 128:256] = lo


def cotangent_kernel(w_far, cot_far, g_hi, g_lo, wide_t, w_hl, w_cat, cot_cat, w_ref, cot_ref, sems):
    copies = fetch([(w_far, w_ref), (cot_far, cot_ref)], sems)
    copies[0].wait()
    weights_by_class(w_ref, w_hl)
    copies[1].wait()
    for d in range(4):
        for quad in range(4):
            hi, lo = halves(cot_ref[quad * 4 + d])
            cot_cat[d, quad * 64 : quad * 64 + 64, 0:128] = hi
            cot_cat[d, quad * 64 : quad * 64 + 64, 128:256] = hi
            cot_cat[d, quad * 64 : quad * 64 + 64, 256:384] = lo
    for d in range(4):
        w_cat[:, 0:256] = w_hl[d]
        w_cat[:, 256:384] = w_hl[d, :, 0:128]
        wide_t[d] = lax.dot_general(
            cot_cat[d], w_cat[...], (((1,), (1,)), ((), ())), preferred_element_type=f32
        )
    for block in range(8):
        h, g = block // 4, block % 4
        at = g * 128 + h * 64
        for quad in range(4):
            parts = [
                wide_t[d, quad * 64 : quad * 64 + 64, block * 128 : block * 128 + 128]
                for d in range(4)
            ]
            for m in range(4):
                hi, lo = halves(pick([parts[(p - m) % 4] for p in range(4)]))
                g_hi[m, at : at + 64, quad * 128 : quad * 128 + 128] = hi
                g_lo[m, at : at + 64, quad * 128 : quad * 128 + 128] = lo


def outer_product(left_ref, parts, right_all, outer, lcat, rt, a_hi, a_lo, r_hl=None, lt=None):
    gather_right(parts, right_all)
    for quad in range(4):
        v = left_rows(left_ref, quad)
        for m in range(4):
            hi, lo = halves(pltpu.roll(v, 32 * m, axis=1) if m else v)
            lcat[m, 0:128, quad * 128 : quad * 128 + 128] = hi
            lcat[m, 128:256, quad * 128 : quad * 128 + 128] = lo
            lcat[m, 256:384, quad * 128 : quad * 128 + 128] = hi
    if lt is not None:
        left_turned(left_ref, lt)
    for e in range(16):
        g, m = e // 4, e % 4
        v = right_rows(right_all, e)
        if r_hl is not None:
            hi, lo = halves(v)
            r_hl[m, 0:128, g * 128 : g * 128 + 128] = hi
            r_hl[m, 128:256, g * 128 : g * 128 + 128] = lo
        hi, lo = halves(v.T)
        rt[m, g * 128 : g * 128 + 128, 0:128] = hi
        rt[m, g * 128 : g * 128 + 128, 128:256] = hi
        rt[m, g * 128 : g * 128 + 128, 256:384] = lo
    for m in range(4):
        outer[m] = matmul(rt[m], lcat[m])
    for block in range(8):
        h, g = block // 4, block % 4
        at = g * 128 + h * 64
        for quad in range(4):
            parts = [outer[m, at : at + 64, quad * 128 : quad * 128 + 128] for m in range(4)]
            for d in range(4):
                hi, lo = halves(pick([parts[(p - d) % 4] for p in range(4)]))
                a_hi[d, quad * 64 : quad * 64 + 64, block * 128 : block * 128 + 128] = hi
                a_lo[d, quad * 64 : quad * 64 + 64, block * 128 : block * 128 + 128] = lo


def pair_kernel(left_ref, *refs):
    parts, (bias_ref, w_far, pair_ref, right_all, outer, lcat, rt, a_hi, a_lo) = refs[:8], refs[8:17]
    w_hl, w_ref, sems = refs[17:]
    (fetched,) = fetch([(w_far, w_ref)], sems)
    outer_product(left_ref, parts, right_all, outer, lcat, rt, a_hi, a_lo)
    fetched.wait()
    weights_by_class(w_ref, w_hl)
    for d in range(4):
        both = matmul(a_hi[d], w_hl[d])
        pair = both[:, 0:128] + both[:, 128:256] + matmul(a_lo[d], w_hl[d, :, 0:128])
        pair = pair * (1.0 / 128) + bias_ref[...]
        for quad in range(4):
            pair_ref[quad * 4 + d] = pair[quad * 64 : quad * 64 + 64]


def tile_kernel(left_ref, *refs):
    parts, (hi_far, lo_far, cot_far, own_out, other_out) = refs[:8], refs[8:13]
    sums, (right_all, outer, lcat, rt, a_hi, a_lo) = refs[13:21], refs[21:27]
    r_hl, lt, g_hi, g_lo, dw, cot_ref, sems = refs[27:]
    core = lax.axis_index("core")
    (fetched,) = fetch([(cot_far, cot_ref)], sems)
    pairs = []
    for m in range(4):
        pairs += [(hi_far.at[m], g_hi.at[m]), (lo_far.at[m], g_lo.at[m])]
    copies = fetch(pairs, sems.at[pl.ds(1, 8)])
    outer_product(left_ref, parts, right_all, outer, lcat, rt, a_hi, a_lo, r_hl, lt)
    fetched.wait()
    for d in range(4):
        hi, lo = halves(jnp.concatenate([cot_ref[quad * 4 + d] for quad in range(4)], axis=0).T)
        both = matmul(jnp.concatenate([hi, lo], axis=0), a_hi[d])
        part = both[0:128] + both[128:256] + matmul(hi, a_lo[d])
        for block in range(8):
            v = part[:, block * 128 : block * 128 + 128]
            if d == 0:
                dw[block] = v
            else:
                dw[block] += pltpu.roll(v, 128 - 32 * d, axis=1)
    for block in range(8):
        dw[block] = dw[block].T
    for block in range(8):
        for p in range(4):
            for out, side in ((own_out, core), (other_out, 1 - core)):
                out[pl.ds(p * 8 + block, 16, stride=BWD), :] = dw[
                    block, pl.ds(p * 32 + side, 16, stride=2), :
                ]
    for m in range(4):
        copies[2 * m].wait()
        copies[2 * m + 1].wait()
        both = matmul(g_hi[m], lt[m])
        v = both[:, 0:128] + both[:, 128:256] + matmul(g_lo[m], lt[m, :, 0:128])
        for g in range(4):
            t = v[g * 128 : g * 128 + 128].T * (1.0 / 128)
            for half in range(2):
                for s in range(4):
                    at = (half * 4 + s) * 16
                    row = half * 1024 + s * 16 + g * 4 + m
                    right_all[pl.ds(row, 16, stride=64), :] = t[at : at + 16]
    for at, ref in enumerate(sums):
        for dz in range(4):
            start = (at // 4) * 1024 + chip_of(dz, at % 4) * 64
            ref[dz] = right_all[pl.ds(pl.multiple_of(start, 64), 64), :]
    total = [None] * 4
    for m in range(4):
        both = matmul(r_hl[m], g_hi[m])
        v = both[0:128] + both[128:256] + matmul(r_hl[m, 0:128, :], g_lo[m])
        for quad in range(4):
            part = v[:, quad * 128 : quad * 128 + 128]
            if m:
                part = pltpu.roll(part, 128 - 32 * m, axis=1)
            total[quad] = part if total[quad] is None else total[quad] + part
    for quad in range(4):
        t = total[quad] * (1.0 / 128)
        for half, out in ((0, own_out), (1, other_out)):
            for s in range(4):
                at = (half * 4 + s) * 16
                out[pl.ds(32 + s * 4 + quad, 16, stride=BWD), :] = t[at : at + 16]


def right_kernel(w2_ref, a_ref, b_ref, c_ref, d_ref, out_ref):
    total = (a_ref[...] + b_ref[...]) + (c_ref[...] + d_ref[...])
    for s in range(4):
        part = total[s * 16 : s * 16 + 16, :]
        entries = jnp.concatenate([part[:, 0:64], part[:, 64:128]], axis=0)
        out_ref[s * 64 : s * 64 + 64, :] = contract(entries, w2_ref[...], ((0,), (0,)))


def finish_kernel(x_ref, scale_ref, w1_ref, part_ref, col_ref, out_ref, weight_ref, tmp):
    core = lax.axis_index("core")
    left = col_ref[0]
    for c in range(1, 8):
        left = left + col_ref[c]
    weight_ref[...] = left[64:68] * (1.0 / 512)
    for u in range(4):
        part = contract(left[0:64, u * 32 : u * 32 + 32], w1_ref[...], ((1,), (0,)))
        for q in range(4):
            side = lax.rem(q % 2 + core, 2)
            for s in range(4):
                at = s * 64 + 32 * (q // 2) + 16 * side + u
                block = (q * 4 + s) * 4
                for k in range(2):
                    tmp[k, pl.ds(at, 4, stride=4), :] = part[block : block + 4, k * 128 : k * 128 + 128]
    unit, inverse = standardized(x_ref[...])
    grad = (part_ref[...] + jnp.concatenate([tmp[0], tmp[1]], axis=1)) * scale_ref[...]
    mean = jnp.mean(grad, axis=-1, keepdims=True)
    along = jnp.mean(grad * unit, axis=-1, keepdims=True)
    out_ref[...] = inverse * (grad - mean - unit * along)


def call(kernel, name, outs, scratch, mib, flops, *args, far=(), copies=0):
    shapes = tuple(jax.ShapeDtypeStruct(*out) for out in outs)
    moved = sum(a.size * a.dtype.itemsize for a in args + tuple(far) + shapes)
    return pl.pallas_call(
        kernel,
        out_shape=shapes,
        in_specs=[VMEM] * len(args) + [HBM] * len(far),
        out_specs=(VMEM,) * len(outs),
        scratch_shapes=[pltpu.VMEM(*s) for s in scratch]
        + ([pltpu.SemaphoreType.DMA((copies,))] if copies else []),
        compiler_params=pltpu.CompilerParams(
            vmem_limit_bytes=mib * 1024 * 1024 if mib else None
        ),
        cost_estimate=pl.CostEstimate(flops=flops, bytes_accessed=moved, transcendentals=0),
        name=name,
    )(*args, *far)


def swap_cores(array):
    return lax.ppermute(array, "core", [(0, 1), (1, 0)])


def from_peer(array, axis, apart):
    return lax.ppermute(array, axis, [(i, i ^ apart) for i in range(4)])


def exchange(array, axes):
    return lax.all_to_all(array, axes, 0, 0, tiled=True)


def local(
    sequence_embedding,
    standardize_scale,
    standardize_offset,
    first_operand_matrix,
    first_operand_intercept,
    second_operand_matrix,
    second_operand_intercept,
    result_matrix,
    result_intercept,
    edge_incoming_sensitivity,
):
    x = sequence_embedding.reshape(256, 256)
    scale = standardize_scale.reshape(1, 256)
    w1 = first_operand_matrix.T
    w2 = second_operand_matrix.T
    small = 2 * 256 * 256 * 32 * 6
    step = 2 * 1024 * 1024 * 128 * 3
    offset = standardize_offset.reshape(1, 256)
    left, right = call(
        project_kernel,
        "project",
        [((8, 64, 128), f32), ((64, 128), f32)],
        [((256, 128), f32)],
        None,
        2 * small,
        x,
        scale,
        offset,
        w1,
        first_operand_intercept.reshape(1, 32),
        w2,
        second_operand_intercept.reshape(1, 32),
    )
    g_hi, g_lo = call(
        cotangent_kernel,
        "cotangent",
        [((4, 512, 512), bf16), ((4, 512, 512), bf16)],
        [
            ((4, 256, 1024), f32),
            ((4, 1024, 256), bf16),
            ((1024, 384), bf16),
            ((4, 256, 384), bf16),
            ((1024, 128), f32),
            ((16, 64, 128), f32),
        ],
        None,
        step,
        far=(result_matrix, edge_incoming_sensitivity),
        copies=2,
    )
    left = exchange(left, COL).reshape(32, 16, 128)
    right = [right] + [from_peer(right, "zl", dz) for dz in (1, 2, 3)]
    right, g_hi, g_lo = lax.optimization_barrier((right, g_hi, g_lo))
    left, right = lax.optimization_barrier((left, jnp.stack(right)))
    left = exchange(left, ROW).reshape(512, 128)
    parts = [right] + [from_peer(right, "x", dx) for dx in (1, 2, 3)]
    parts = parts + [swap_cores(part) for part in parts]
    working = [
        ((2048, 128), f32),
        ((4, 512, 512), f32),
        ((4, 384, 512), bf16),
        ((4, 512, 384), bf16),
        ((4, 256, 1024), bf16),
        ((4, 256, 1024), bf16),
    ]
    own, other, *sums = call(
        tile_kernel,
        "tile",
        [((16 * BWD, 128), f32)] * 2 + [((4, 64, 128), f32)] * 8,
        working
        + [((4, 256, 512), bf16), ((4, 512, 256), bf16)]
        + [((4, 512, 512), bf16)] * 2
        + [((8, 128, 128), f32), ((16, 64, 128), f32)],
        51,
        4 * step,
        left,
        *parts,
        far=(g_hi, g_lo, edge_incoming_sensitivity),
        copies=9,
    )
    own = own.reshape(16, BWD, 128)
    got = swap_cores(other.reshape(16, BWD, 128))
    sent = jnp.concatenate([own[:, :32] + got[:, :32], own[:, 32:], got[:, 32:]], axis=1)
    back = exchange(sent, CHIP)
    sums = [a + swap_cores(b) for a, b in zip(sums[:4], sums[4:])]
    right = sums[0] + sum(from_peer(sums[dx], "x", dx) for dx in (1, 2, 3))
    (pair,) = call(
        pair_kernel,
        "pair",
        [((16, 64, 128), f32)],
        working + [((4, 1024, 256), bf16), ((1024, 128), f32)],
        52,
        2 * step,
        left,
        *parts,
        result_intercept.reshape(1, 128),
        far=(result_matrix,),
        copies=1,
    )
    weight = back[:, :32].sum(axis=0).reshape(4, 8, 128).transpose(1, 0, 2)
    sent = jnp.concatenate(
        [back[:, 32:].reshape(8, 64, 128), jnp.pad(weight, ((0, 0), (0, 4), (0, 0)))], axis=1
    )
    sent, right, pair = lax.optimization_barrier((sent, right, pair))
    cols = exchange(sent, COL)
    right = [right[0]] + [from_peer(right[dz], "zl", dz) for dz in (1, 2, 3)]
    (part,) = call(right_kernel, "right", [((256, 256), f32)], [], 8, small, w2, *right)
    grad, weight = call(
        finish_kernel,
        "finish",
        [((256, 256), f32), ((4, 128), f32)],
        [((2, 256, 128), f32)],
        8,
        small,
        x,
        scale,
        w1,
        part,
        cols,
    )
    return pair, grad.reshape(4, 64, 256), weight


def solution(mesh):
    fine = Mesh(mesh.devices.reshape(SIZES), NAMES)
    tile = P(ROW, COL, None)
    return jax.shard_map(
        local,
        mesh=fine,
        in_specs=(tile, P(), P(), P(), P(), P(), P(), P(), P(), tile),
        out_specs=(tile, tile, P(ROW + COL, None)),
        check_vma=False,
    )
```

```python
import jax
import jax.numpy as jnp
from jax import lax
from jax.experimental import pallas as pl
from jax.experimental.pallas import tpu as pltpu
from jax.sharding import Mesh, PartitionSpec as P

exact = lax.Precision.HIGHEST
f32 = jnp.float32
bf16 = jnp.bfloat16

SIZES = (4, 4, 2, 2, 4)
NAMES = ("zl", "x", "core", "zh", "y")
CHIP = ("zl", "x")
ROW = ("zl", "x", "core")
COL = ("zh", "y")
VMEM = pl.BlockSpec(memory_space=pltpu.VMEM)
HBM = pl.BlockSpec(memory_space=pltpu.HBM)

BWD = 32


def contract(a, b, dims):
    return lax.dot_general(a, b, (dims, ((), ())), precision=exact, preferred_element_type=f32)


def matmul(a, b):
    return lax.dot_general(a, b, (((1,), (0,)), ((), ())), preferred_element_type=f32)


def halves(v):
    high = v.astype(bf16)
    return high, (v - high.astype(f32)).astype(bf16)


def standardized(x):
    demeaned = x - jnp.mean(x, axis=-1, keepdims=True)
    variance = jnp.mean(demeaned * demeaned, axis=-1, keepdims=True)
    inverse = lax.rsqrt(variance + 1e-05)
    return demeaned * inverse, inverse


def project_right_kernel(x_ref, scale_ref, offset_ref, w2_ref, b2_ref, right_ref):
    normed = standardized(x_ref[...])[0] * scale_ref[...] + offset_ref[...]
    on = lax.broadcasted_iota(jnp.int32, (32, 32), 0) == lax.broadcasted_iota(jnp.int32, (32, 32), 1)
    b2 = jnp.sum(jnp.where(on, b2_ref[...], 0.0), axis=1, keepdims=True)
    right = contract(w2_ref[...], normed, ((1,), (1,))) + b2
    for s in range(4):
        cols = right[:, s * 64 : s * 64 + 64]
        right_ref[s * 16 : s * 16 + 16, :] = jnp.concatenate([cols[0:16], cols[16:32]], axis=1)


def project_left_kernel(x_ref, scale_ref, offset_ref, w1_ref, b1_ref, left_ref, tmp):
    normed = standardized(x_ref[...])[0] * scale_ref[...] + offset_ref[...]
    tmp[:, 0:32] = contract(normed, w1_ref[...], ((1,), (1,))) + b1_ref[...]
    wide = jnp.concatenate([tmp[pl.ds(u, 64, stride=4), :][:, 0:32] for u in range(4)], axis=1)
    for q in range(4):
        part = jnp.concatenate([wide[s * 16 + q * 4 : s * 16 + q * 4 + 4] for s in range(4)], axis=0)
        for copy in range(8):
            left_ref[copy, q * 16 : q * 16 + 16, :] = part


def fetch(pairs, sems):
    copies = [pltpu.make_async_copy(a, b, sems.at[i]) for i, (a, b) in enumerate(pairs)]
    for copy in copies:
        copy.start()
    return copies


def fetch_classes(hi_far, lo_far, g_hi, g_lo, sems):
    pairs = []
    for m in range(4):
        pairs += [(hi_far.at[m], g_hi.at[m]), (lo_far.at[m], g_lo.at[m])]
    return fetch(pairs, sems)


def pick(parts):
    chunk = lax.broadcasted_iota(jnp.int32, (64, 128), 1) // 32
    low = jnp.where(chunk == 0, parts[0], parts[1])
    return jnp.where(chunk < 2, low, jnp.where(chunk == 2, parts[2], parts[3]))


def chip_of(dz, dx):
    return jnp.bitwise_xor(lax.axis_index("zl"), dz) * 4 + jnp.bitwise_xor(lax.axis_index("x"), dx)


def left_rows(left_ref, quad):
    core = lax.axis_index("core")
    got = []
    for side in (core, 1 - core):
        for s in range(4):
            got.append(left_ref[pl.ds(side * 16 + s * 4 + quad, 16, stride=32), :])
    return jnp.concatenate(got, axis=0)


def gather_right(parts, right_all):
    for at, ref in enumerate(parts):
        for dz in range(4):
            start = (at // 4) * 1024 + chip_of(dz, at % 4) * 64
            right_all[pl.ds(pl.multiple_of(start, 64), 64), :] = ref[dz]


def right_rows(right_all, e):
    got = []
    for half in range(2):
        for s in range(4):
            got.append(right_all[pl.ds(half * 1024 + s * 16 + e, 16, stride=64), :])
    return jnp.concatenate(got, axis=0)


def left_turned(left_ref, lt):
    for quad in range(4):
        hi, lo = halves(left_rows(left_ref, quad).T)
        for p in range(4):
            for m in range(4):
                at = quad * 128 + ((p + m) % 4) * 32
                lt[m, at : at + 32, 0:128] = hi[p * 32 : p * 32 + 32]
                lt[m, at : at + 32, 128:256] = lo[p * 32 : p * 32 + 32]


def weights_by_class(w_ref, w_hl):
    for e in range(32):
        hi, lo = halves(w_ref[pl.ds(e, 32, stride=32), :])
        for d in range(4):
            at = (e // 4) * 128 + ((e % 4 + d) % 4) * 32
            w_hl[d, at : at + 32, 0:128] = hi
            w_hl[d, at : at + 32, 128:256] = lo


def cotangent_kernel(w_far, cot_far, g_hi, g_lo, wide_t, w_hl, w_cat, cot_cat, w_ref, cot_ref, sems):
    copies = fetch([(w_far, w_ref), (cot_far, cot_ref)], sems)
    copies[0].wait()
    weights_by_class(w_ref, w_hl)
    copies[1].wait()
    for d in range(4):
        for quad in range(4):
            hi, lo = halves(cot_ref[quad * 4 + d])
            cot_cat[d, quad * 64 : quad * 64 + 64, 0:128] = hi
            cot_cat[d, quad * 64 : quad * 64 + 64, 128:256] = hi
            cot_cat[d, quad * 64 : quad * 64 + 64, 256:384] = lo
    for d in range(4):
        w_cat[:, 0:256] = w_hl[d]
        w_cat[:, 256:384] = w_hl[d, :, 0:128]
        wide_t[d] = lax.dot_general(
            cot_cat[d], w_cat[...], (((1,), (1,)), ((), ())), preferred_element_type=f32
        )
    for block in range(8):
        h, g = block // 4, block % 4
        at = g * 128 + h * 64
        for quad in range(4):
            parts = [
                wide_t[d, quad * 64 : quad * 64 + 64, block * 128 : block * 128 + 128]
                for d in range(4)
            ]
            for m in range(4):
                hi, lo = halves(pick([parts[(p - m) % 4] for p in range(4)]))
                g_hi[m, at : at + 64, quad * 128 : quad * 128 + 128] = hi
                g_lo[m, at : at + 64, quad * 128 : quad * 128 + 128] = lo


def outer_product(left_ref, parts, right_all, outer, lcat, rt, a_hi, a_lo, lt=None):
    gather_right(parts, right_all)
    for quad in range(4):
        v = left_rows(left_ref, quad)
        for m in range(4):
            hi, lo = halves(pltpu.roll(v, 32 * m, axis=1) if m else v)
            lcat[m, 0:128, quad * 128 : quad * 128 + 128] = hi
            lcat[m, 128:256, quad * 128 : quad * 128 + 128] = lo
            lcat[m, 256:384, quad * 128 : quad * 128 + 128] = hi
    if lt is not None:
        left_turned(left_ref, lt)
    for e in range(16):
        g, m = e // 4, e % 4
        hi, lo = halves(right_rows(right_all, e).T)
        rt[m, g * 128 : g * 128 + 128, 0:128] = hi
        rt[m, g * 128 : g * 128 + 128, 128:256] = hi
        rt[m, g * 128 : g * 128 + 128, 256:384] = lo
    for m in range(4):
        outer[m] = matmul(rt[m], lcat[m])
    for block in range(8):
        h, g = block // 4, block % 4
        at = g * 128 + h * 64
        for quad in range(4):
            parts = [outer[m, at : at + 64, quad * 128 : quad * 128 + 128] for m in range(4)]
            for d in range(4):
                hi, lo = halves(pick([parts[(p - d) % 4] for p in range(4)]))
                a_hi[d, quad * 64 : quad * 64 + 64, block * 128 : block * 128 + 128] = hi
                a_lo[d, quad * 64 : quad * 64 + 64, block * 128 : block * 128 + 128] = lo


def pair_kernel(left_ref, *refs):
    parts, (bias_ref, w_far, pair_ref, right_all, outer, lcat, rt, a_hi, a_lo) = refs[:8], refs[8:17]
    w_hl, w_ref, sems = refs[17:]
    (fetched,) = fetch([(w_far, w_ref)], sems)
    outer_product(left_ref, parts, right_all, outer, lcat, rt, a_hi, a_lo)
    fetched.wait()
    weights_by_class(w_ref, w_hl)
    for d in range(4):
        both = matmul(a_hi[d], w_hl[d])
        pair = both[:, 0:128] + both[:, 128:256] + matmul(a_lo[d], w_hl[d, :, 0:128])
        pair = pair * (1.0 / 128) + bias_ref[...]
        for quad in range(4):
            pair_ref[quad * 4 + d] = pair[quad * 64 : quad * 64 + 64]


def tile_kernel(left_ref, *refs):
    parts, (hi_far, lo_far, cot_far, own_out, other_out) = refs[:8], refs[8:13]
    sums, (right_all, outer, lcat, rt, a_hi, a_lo) = refs[13:21], refs[21:27]
    lt, g_hi, g_lo, dw, cot_ref, sems = refs[27:]
    core = lax.axis_index("core")
    (fetched,) = fetch([(cot_far, cot_ref)], sems)
    copies = fetch_classes(hi_far, lo_far, g_hi, g_lo, sems.at[pl.ds(1, 8)])
    outer_product(left_ref, parts, right_all, outer, lcat, rt, a_hi, a_lo, lt)
    fetched.wait()
    for d in range(4):
        hi, lo = halves(jnp.concatenate([cot_ref[quad * 4 + d] for quad in range(4)], axis=0).T)
        both = matmul(jnp.concatenate([hi, lo], axis=0), a_hi[d])
        part = both[0:128] + both[128:256] + matmul(hi, a_lo[d])
        for block in range(8):
            v = part[:, block * 128 : block * 128 + 128]
            if d == 0:
                dw[block] = v
            else:
                dw[block] += pltpu.roll(v, 128 - 32 * d, axis=1)
    for block in range(8):
        dw[block] = dw[block].T
    for block in range(8):
        for p in range(4):
            for out, side in ((own_out, core), (other_out, 1 - core)):
                out[pl.ds(p * 8 + block, 16, stride=BWD), :] = dw[
                    block, pl.ds(p * 32 + side, 16, stride=2), :
                ]
    for m in range(4):
        copies[2 * m].wait()
        copies[2 * m + 1].wait()
        both = matmul(g_hi[m], lt[m])
        v = both[:, 0:128] + both[:, 128:256] + matmul(g_lo[m], lt[m, :, 0:128])
        for g in range(4):
            t = v[g * 128 : g * 128 + 128].T * (1.0 / 128)
            for half in range(2):
                for s in range(4):
                    at = (half * 4 + s) * 16
                    row = half * 1024 + s * 16 + g * 4 + m
                    right_all[pl.ds(row, 16, stride=64), :] = t[at : at + 16]
    for at, ref in enumerate(sums):
        for dz in range(4):
            start = (at // 4) * 1024 + chip_of(dz, at % 4) * 64
            ref[dz] = right_all[pl.ds(pl.multiple_of(start, 64), 64), :]


def left_gradient_kernel(*refs):
    parts, (hi_far, lo_far, own_out, other_out, right_all, r_hl, g_hi, g_lo, sems) = refs[:8], refs[8:]
    copies = fetch_classes(hi_far, lo_far, g_hi, g_lo, sems)
    gather_right(parts, right_all)
    for e in range(16):
        g, m = e // 4, e % 4
        hi, lo = halves(right_rows(right_all, e))
        r_hl[m, 0:128, g * 128 : g * 128 + 128] = hi
        r_hl[m, 128:256, g * 128 : g * 128 + 128] = lo
    total = [None] * 4
    for m in range(4):
        copies[2 * m].wait()
        copies[2 * m + 1].wait()
        both = matmul(r_hl[m], g_hi[m])
        v = both[0:128] + both[128:256] + matmul(r_hl[m, 0:128, :], g_lo[m])
        for quad in range(4):
            part = v[:, quad * 128 : quad * 128 + 128]
            if m:
                part = pltpu.roll(part, 128 - 32 * m, axis=1)
            total[quad] = part if total[quad] is None else total[quad] + part
    for quad in range(4):
        t = total[quad] * (1.0 / 128)
        for half, out in ((0, own_out), (1, other_out)):
            for s in range(4):
                at = (half * 4 + s) * 16
                out[pl.ds(s * 4 + quad, 16, stride=16), :] = t[at : at + 16]


def right_kernel(w2_ref, a_ref, b_ref, c_ref, d_ref, out_ref):
    total = (a_ref[...] + b_ref[...]) + (c_ref[...] + d_ref[...])
    for s in range(4):
        part = total[s * 16 : s * 16 + 16, :]
        entries = jnp.concatenate([part[:, 0:64], part[:, 64:128]], axis=0)
        out_ref[s * 64 : s * 64 + 64, :] = contract(entries, w2_ref[...], ((0,), (0,)))


def finish_kernel(x_ref, scale_ref, w1_ref, part_ref, col_ref, out_ref, weight_ref, tmp):
    core = lax.axis_index("core")
    left = col_ref[0]
    for c in range(1, 8):
        left = left + col_ref[c]
    weight_ref[...] = left[64:68] * (1.0 / 512)
    for u in range(4):
        part = contract(left[0:64, u * 32 : u * 32 + 32], w1_ref[...], ((1,), (0,)))
        for q in range(4):
            side = lax.rem(q % 2 + core, 2)
            for s in range(4):
                at = s * 64 + 32 * (q // 2) + 16 * side + u
                block = (q * 4 + s) * 4
                for k in range(2):
                    tmp[k, pl.ds(at, 4, stride=4), :] = part[block : block + 4, k * 128 : k * 128 + 128]
    unit, inverse = standardized(x_ref[...])
    grad = (part_ref[...] + jnp.concatenate([tmp[0], tmp[1]], axis=1)) * scale_ref[...]
    mean = jnp.mean(grad, axis=-1, keepdims=True)
    along = jnp.mean(grad * unit, axis=-1, keepdims=True)
    out_ref[...] = inverse * (grad - mean - unit * along)


def call(kernel, name, outs, scratch, mib, flops, *args, far=(), copies=0):
    shapes = tuple(jax.ShapeDtypeStruct(*out) for out in outs)
    moved = sum(a.size * a.dtype.itemsize for a in args + tuple(far) + shapes)
    return pl.pallas_call(
        kernel,
        out_shape=shapes,
        in_specs=[VMEM] * len(args) + [HBM] * len(far),
        out_specs=(VMEM,) * len(outs),
        scratch_shapes=[pltpu.VMEM(*s) for s in scratch]
        + ([pltpu.SemaphoreType.DMA((copies,))] if copies else []),
        compiler_params=pltpu.CompilerParams(
            vmem_limit_bytes=mib * 1024 * 1024 if mib else None
        ),
        cost_estimate=pl.CostEstimate(flops=flops, bytes_accessed=moved, transcendentals=0),
        name=name,
    )(*args, *far)


def swap_cores(array):
    return lax.ppermute(array, "core", [(0, 1), (1, 0)])


def from_peer(array, axis, apart):
    return lax.ppermute(array, axis, [(i, i ^ apart) for i in range(4)])


def exchange(array, axes):
    return lax.all_to_all(array, axes, 0, 0, tiled=True)


def local(
    sequence_embedding,
    standardize_scale,
    standardize_offset,
    first_operand_matrix,
    first_operand_intercept,
    second_operand_matrix,
    second_operand_intercept,
    result_matrix,
    result_intercept,
    edge_incoming_sensitivity,
):
    x = sequence_embedding.reshape(256, 256)
    scale = standardize_scale.reshape(1, 256)
    w1 = first_operand_matrix.T
    w2 = second_operand_matrix.T
    small = 2 * 256 * 256 * 32 * 6
    step = 2 * 1024 * 1024 * 128 * 3
    offset = standardize_offset.reshape(1, 256)
    (right,) = call(
        project_right_kernel,
        "project_right",
        [((64, 128), f32)],
        [],
        None,
        small,
        x,
        scale,
        offset,
        w2,
        second_operand_intercept.reshape(1, 32),
    )
    (left,) = call(
        project_left_kernel,
        "project_left",
        [((8, 64, 128), f32)],
        [((256, 128), f32)],
        None,
        small,
        x,
        scale,
        offset,
        w1,
        first_operand_intercept.reshape(1, 32),
    )
    right = [right] + [from_peer(right, "zl", dz) for dz in (1, 2, 3)]
    left, right = lax.optimization_barrier((left, right))
    g_hi, g_lo = call(
        cotangent_kernel,
        "cotangent",
        [((4, 512, 512), bf16), ((4, 512, 512), bf16)],
        [
            ((4, 256, 1024), f32),
            ((4, 1024, 256), bf16),
            ((1024, 384), bf16),
            ((4, 256, 384), bf16),
            ((1024, 128), f32),
            ((16, 64, 128), f32),
        ],
        None,
        step,
        far=(result_matrix, edge_incoming_sensitivity),
        copies=2,
    )
    left = exchange(left, COL).reshape(32, 16, 128)
    right = jnp.stack(right)
    parts = [right] + [from_peer(right, "x", dx) for dx in (1, 2, 3)]
    left, parts, g_hi, g_lo = lax.optimization_barrier((left, parts, g_hi, g_lo))
    left = exchange(left, ROW).reshape(512, 128)
    parts = parts + [swap_cores(part) for part in parts]
    own_left, other_left = call(
        left_gradient_kernel,
        "left_gradient",
        [((256, 128), f32), ((256, 128), f32)],
        [((2048, 128), f32), ((4, 256, 512), bf16)] + [((4, 512, 512), bf16)] * 2,
        52,
        step,
        *parts,
        far=(g_hi, g_lo),
        copies=8,
    )
    got_left = swap_cores(other_left)
    left, own_left, got_left = lax.optimization_barrier((left, own_left, got_left))
    working = [
        ((2048, 128), f32),
        ((4, 512, 512), f32),
        ((4, 384, 512), bf16),
        ((4, 512, 384), bf16),
        ((4, 256, 1024), bf16),
        ((4, 256, 1024), bf16),
    ]
    own, other, *sums = call(
        tile_kernel,
        "tile",
        [((16 * BWD, 128), f32)] * 2 + [((4, 64, 128), f32)] * 8,
        working
        + [((4, 512, 256), bf16)]
        + [((4, 512, 512), bf16)] * 2
        + [((8, 128, 128), f32), ((16, 64, 128), f32)],
        51,
        3 * step,
        left,
        *parts,
        far=(g_hi, g_lo, edge_incoming_sensitivity),
        copies=9,
    )
    got = swap_cores(other)
    weight = (own + got).reshape(16, BWD, 128)
    sent = [weight, own_left.reshape(16, 16, 128), got_left.reshape(16, 16, 128)]
    back = exchange(jnp.concatenate(sent, axis=1), CHIP)
    sums = [a + swap_cores(b) for a, b in zip(sums[:4], sums[4:])]
    right = sums[0] + sum(from_peer(sums[dx], "x", dx) for dx in (1, 2, 3))
    (pair,) = call(
        pair_kernel,
        "pair",
        [((16, 64, 128), f32)],
        working + [((4, 1024, 256), bf16), ((1024, 128), f32)],
        52,
        2 * step,
        left,
        *parts,
        result_intercept.reshape(1, 128),
        far=(result_matrix,),
        copies=1,
    )
    weight = back[:, :32].sum(axis=0).reshape(4, 8, 128).transpose(1, 0, 2)
    sent = jnp.concatenate(
        [back[:, 32:].reshape(8, 64, 128), jnp.pad(weight, ((0, 0), (0, 4), (0, 0)))], axis=1
    )
    sent, right, pair = lax.optimization_barrier((sent, right, pair))
    cols = exchange(sent, COL)
    right = [right[0]] + [from_peer(right[dz], "zl", dz) for dz in (1, 2, 3)]
    (part,) = call(right_kernel, "right", [((256, 256), f32)], [], 8, small, w2, *right)
    grad, weight = call(
        finish_kernel,
        "finish",
        [((256, 256), f32), ((4, 128), f32)],
        [((2, 256, 128), f32)],
        8,
        small,
        x,
        scale,
        w1,
        part,
        cols,
    )
    return pair, grad.reshape(4, 64, 256), weight


def solution(mesh):
    fine = Mesh(mesh.devices.reshape(SIZES), NAMES)
    tile = P(ROW, COL, None)
    return jax.shard_map(
        local,
        mesh=fine,
        in_specs=(tile, P(), P(), P(), P(), P(), P(), P(), P(), tile),
        out_specs=(tile, tile, P(ROW + COL, None)),
        check_vma=False,
    )
```

```python
import jax
import jax.numpy as jnp
from jax import lax
from jax.experimental import pallas as pl
from jax.experimental.pallas import tpu as pltpu
from jax.sharding import Mesh, PartitionSpec as P

exact = lax.Precision.HIGHEST
f32 = jnp.float32
bf16 = jnp.bfloat16

SIZES = (4, 4, 2, 2, 4)
NAMES = ("zl", "x", "core", "zh", "y")
CHIP = ("zl", "x")
ROW = ("zl", "x", "core")
COL = ("zh", "y")
VMEM = pl.BlockSpec(memory_space=pltpu.VMEM)
HBM = pl.BlockSpec(memory_space=pltpu.HBM)

BWD = 32


def contract(a, b, dims):
    return lax.dot_general(a, b, (dims, ((), ())), precision=exact, preferred_element_type=f32)


def matmul(a, b):
    return lax.dot_general(a, b, (((1,), (0,)), ((), ())), preferred_element_type=f32)


def halves(v):
    high = v.astype(bf16)
    return high, (v - high.astype(f32)).astype(bf16)


def standardized(x):
    demeaned = x - jnp.mean(x, axis=-1, keepdims=True)
    variance = jnp.mean(demeaned * demeaned, axis=-1, keepdims=True)
    inverse = lax.rsqrt(variance + 1e-05)
    return demeaned * inverse, inverse


def project_right_kernel(x_ref, scale_ref, offset_ref, w2_ref, b2_ref, right_ref):
    normed = standardized(x_ref[...])[0] * scale_ref[...] + offset_ref[...]
    on = lax.broadcasted_iota(jnp.int32, (32, 32), 0) == lax.broadcasted_iota(jnp.int32, (32, 32), 1)
    b2 = jnp.sum(jnp.where(on, b2_ref[...], 0.0), axis=1, keepdims=True)
    right = contract(w2_ref[...], normed, ((1,), (1,))) + b2
    for s in range(4):
        cols = right[:, s * 64 : s * 64 + 64]
        right_ref[s * 16 : s * 16 + 16, :] = jnp.concatenate([cols[0:16], cols[16:32]], axis=1)


def project_left_kernel(x_ref, scale_ref, offset_ref, w1_ref, b1_ref, left_ref, tmp):
    normed = standardized(x_ref[...])[0] * scale_ref[...] + offset_ref[...]
    tmp[:, 0:32] = contract(normed, w1_ref[...], ((1,), (1,))) + b1_ref[...]
    wide = jnp.concatenate([tmp[pl.ds(u, 64, stride=4), :][:, 0:32] for u in range(4)], axis=1)
    for q in range(4):
        part = jnp.concatenate([wide[s * 16 + q * 4 : s * 16 + q * 4 + 4] for s in range(4)], axis=0)
        for copy in range(8):
            left_ref[copy, q * 16 : q * 16 + 16, :] = part


def fetch(pairs, sems):
    copies = [pltpu.make_async_copy(a, b, sems.at[i]) for i, (a, b) in enumerate(pairs)]
    for copy in copies:
        copy.start()
    return copies


def fetch_classes(hi_far, lo_far, g_hi, g_lo, sems):
    pairs = []
    for m in range(4):
        pairs += [(hi_far.at[m], g_hi.at[m]), (lo_far.at[m], g_lo.at[m])]
    return fetch(pairs, sems)


def pick(parts):
    chunk = lax.broadcasted_iota(jnp.int32, (64, 128), 1) // 32
    low = jnp.where(chunk == 0, parts[0], parts[1])
    return jnp.where(chunk < 2, low, jnp.where(chunk == 2, parts[2], parts[3]))


def chip_of(dz, dx):
    return jnp.bitwise_xor(lax.axis_index("zl"), dz) * 4 + jnp.bitwise_xor(lax.axis_index("x"), dx)


def left_rows(left_ref, quad):
    core = lax.axis_index("core")
    got = []
    for side in (core, 1 - core):
        for s in range(4):
            got.append(left_ref[pl.ds(side * 16 + s * 4 + quad, 16, stride=32), :])
    return jnp.concatenate(got, axis=0)


def gather_right(parts, right_all):
    for at, ref in enumerate(parts):
        for dz in range(4):
            start = (at // 4) * 1024 + chip_of(dz, at % 4) * 64
            right_all[pl.ds(pl.multiple_of(start, 64), 64), :] = ref[dz]


def right_rows(right_all, e):
    got = []
    for half in range(2):
        for s in range(4):
            got.append(right_all[pl.ds(half * 1024 + s * 16 + e, 16, stride=64), :])
    return jnp.concatenate(got, axis=0)


def left_turned(left_ref, lt):
    for quad in range(4):
        hi, lo = halves(left_rows(left_ref, quad).T)
        for p in range(4):
            for m in range(4):
                at = quad * 128 + ((p + m) % 4) * 32
                lt[m, at : at + 32, 0:128] = hi[p * 32 : p * 32 + 32]
                lt[m, at : at + 32, 128:256] = lo[p * 32 : p * 32 + 32]


def weights_by_class(w_ref, w_hl):
    for e in range(32):
        hi, lo = halves(w_ref[pl.ds(e, 32, stride=32), :])
        for d in range(4):
            at = (e // 4) * 128 + ((e % 4 + d) % 4) * 32
            w_hl[d, at : at + 32, 0:128] = hi
            w_hl[d, at : at + 32, 128:256] = lo


def cotangent_kernel(w_far, cot_far, g_hi, g_lo, wide_t, w_hl, w_cat, cot_cat, w_ref, cot_ref, sems):
    copies = fetch([(w_far, w_ref), (cot_far, cot_ref)], sems)
    copies[0].wait()
    weights_by_class(w_ref, w_hl)
    copies[1].wait()
    for d in range(4):
        for quad in range(4):
            hi, lo = halves(cot_ref[quad * 4 + d])
            cot_cat[d, quad * 64 : quad * 64 + 64, 0:128] = hi
            cot_cat[d, quad * 64 : quad * 64 + 64, 128:256] = hi
            cot_cat[d, quad * 64 : quad * 64 + 64, 256:384] = lo
    for d in range(4):
        w_cat[:, 0:256] = w_hl[d]
        w_cat[:, 256:384] = w_hl[d, :, 0:128]
        wide_t[d] = lax.dot_general(
            cot_cat[d], w_cat[...], (((1,), (1,)), ((), ())), preferred_element_type=f32
        )
    for block in range(8):
        h, g = block // 4, block % 4
        at = g * 128 + h * 64
        for quad in range(4):
            parts = [
                wide_t[d, quad * 64 : quad * 64 + 64, block * 128 : block * 128 + 128]
                for d in range(4)
            ]
            for m in range(4):
                hi, lo = halves(pick([parts[(p - m) % 4] for p in range(4)]))
                g_hi[m, at : at + 64, quad * 128 : quad * 128 + 128] = hi
                g_lo[m, at : at + 64, quad * 128 : quad * 128 + 128] = lo


def outer_product(left_ref, parts, right_all, outer, lcat, rt, a_hi, a_lo, lt=None):
    gather_right(parts, right_all)
    for quad in range(4):
        v = left_rows(left_ref, quad)
        for m in range(4):
            hi, lo = halves(pltpu.roll(v, 32 * m, axis=1) if m else v)
            lcat[m, 0:128, quad * 128 : quad * 128 + 128] = hi
            lcat[m, 128:256, quad * 128 : quad * 128 + 128] = lo
            lcat[m, 256:384, quad * 128 : quad * 128 + 128] = hi
    if lt is not None:
        left_turned(left_ref, lt)
    for e in range(16):
        g, m = e // 4, e % 4
        hi, lo = halves(right_rows(right_all, e).T)
        rt[m, g * 128 : g * 128 + 128, 0:128] = hi
        rt[m, g * 128 : g * 128 + 128, 128:256] = hi
        rt[m, g * 128 : g * 128 + 128, 256:384] = lo
    for m in range(4):
        outer[m] = matmul(rt[m], lcat[m])
    for block in range(8):
        h, g = block // 4, block % 4
        at = g * 128 + h * 64
        for quad in range(4):
            parts = [outer[m, at : at + 64, quad * 128 : quad * 128 + 128] for m in range(4)]
            for d in range(4):
                hi, lo = halves(pick([parts[(p - d) % 4] for p in range(4)]))
                a_hi[d, quad * 64 : quad * 64 + 64, block * 128 : block * 128 + 128] = hi
                a_lo[d, quad * 64 : quad * 64 + 64, block * 128 : block * 128 + 128] = lo


def pair_kernel(left_ref, *refs):
    parts, (bias_ref, w_far, pair_ref, right_all, outer, lcat, rt, a_hi, a_lo) = refs[:8], refs[8:17]
    w_hl, w_ref, sems = refs[17:]
    (fetched,) = fetch([(w_far, w_ref)], sems)
    outer_product(left_ref, parts, right_all, outer, lcat, rt, a_hi, a_lo)
    fetched.wait()
    weights_by_class(w_ref, w_hl)
    for d in range(4):
        both = matmul(a_hi[d], w_hl[d])
        pair = both[:, 0:128] + both[:, 128:256] + matmul(a_lo[d], w_hl[d, :, 0:128])
        pair = pair * (1.0 / 128) + bias_ref[...]
        for quad in range(4):
            pair_ref[quad * 4 + d] = pair[quad * 64 : quad * 64 + 64]


def tile_kernel(left_ref, *refs):
    parts, (hi_far, lo_far, cot_far, own_out, other_out) = refs[:8], refs[8:13]
    sums, (right_all, outer, lcat, rt, a_hi, a_lo) = refs[13:21], refs[21:27]
    lt, g_hi, g_lo, dw, cot_ref, sems = refs[27:]
    core = lax.axis_index("core")
    (fetched,) = fetch([(cot_far, cot_ref)], sems)
    copies = fetch_classes(hi_far, lo_far, g_hi, g_lo, sems.at[pl.ds(1, 8)])
    outer_product(left_ref, parts, right_all, outer, lcat, rt, a_hi, a_lo, lt)
    fetched.wait()
    for d in range(4):
        hi, lo = halves(jnp.concatenate([cot_ref[quad * 4 + d] for quad in range(4)], axis=0).T)
        both = matmul(jnp.concatenate([hi, lo], axis=0), a_hi[d])
        part = both[0:128] + both[128:256] + matmul(hi, a_lo[d])
        for block in range(8):
            v = part[:, block * 128 : block * 128 + 128]
            if d == 0:
                dw[block] = v
            else:
                dw[block] += pltpu.roll(v, 128 - 32 * d, axis=1)
    for block in range(8):
        dw[block] = dw[block].T
    for block in range(8):
        for p in range(4):
            for out, side in ((own_out, core), (other_out, 1 - core)):
                out[pl.ds(p * 8 + block, 16, stride=BWD), :] = dw[
                    block, pl.ds(p * 32 + side, 16, stride=2), :
                ]
    for m in range(4):
        copies[2 * m].wait()
        copies[2 * m + 1].wait()
        both = matmul(g_hi[m], lt[m])
        v = both[:, 0:128] + both[:, 128:256] + matmul(g_lo[m], lt[m, :, 0:128])
        for g in range(4):
            t = v[g * 128 : g * 128 + 128].T * (1.0 / 128)
            for half in range(2):
                for s in range(4):
                    at = (half * 4 + s) * 16
                    row = half * 1024 + s * 16 + g * 4 + m
                    right_all[pl.ds(row, 16, stride=64), :] = t[at : at + 16]
    for at, ref in enumerate(sums):
        for dz in range(4):
            start = (at // 4) * 1024 + chip_of(dz, at % 4) * 64
            ref[dz] = right_all[pl.ds(pl.multiple_of(start, 64), 64), :]


def left_gradient_kernel(*refs):
    parts, (hi_far, lo_far, own_out, other_out, right_all, r_hl, g_hi, g_lo, sems) = refs[:8], refs[8:]
    copies = fetch_classes(hi_far, lo_far, g_hi, g_lo, sems)
    gather_right(parts, right_all)
    for e in range(16):
        g, m = e // 4, e % 4
        hi, lo = halves(right_rows(right_all, e))
        r_hl[m, 0:128, g * 128 : g * 128 + 128] = hi
        r_hl[m, 128:256, g * 128 : g * 128 + 128] = lo
    total = [None] * 4
    for m in range(4):
        copies[2 * m].wait()
        copies[2 * m + 1].wait()
        both = matmul(r_hl[m], g_hi[m])
        v = both[0:128] + both[128:256] + matmul(r_hl[m, 0:128, :], g_lo[m])
        for quad in range(4):
            part = v[:, quad * 128 : quad * 128 + 128]
            if m:
                part = pltpu.roll(part, 128 - 32 * m, axis=1)
            total[quad] = part if total[quad] is None else total[quad] + part
    for quad in range(4):
        t = total[quad] * (1.0 / 128)
        for half, out in ((0, own_out), (1, other_out)):
            for s in range(4):
                at = (half * 4 + s) * 16
                out[pl.ds(s * 4 + quad, 16, stride=16), :] = t[at : at + 16]


def right_kernel(w2_ref, a_ref, b_ref, c_ref, d_ref, out_ref):
    total = (a_ref[...] + b_ref[...]) + (c_ref[...] + d_ref[...])
    for s in range(4):
        part = total[s * 16 : s * 16 + 16, :]
        entries = jnp.concatenate([part[:, 0:64], part[:, 64:128]], axis=0)
        out_ref[s * 64 : s * 64 + 64, :] = contract(entries, w2_ref[...], ((0,), (0,)))


def finish_kernel(x_ref, scale_ref, w1_ref, part_ref, col_ref, out_ref, weight_ref, tmp):
    core = lax.axis_index("core")
    left = col_ref[0]
    for c in range(1, 8):
        left = left + col_ref[c]
    weight_ref[...] = left[64:68] * (1.0 / 512)
    for u in range(4):
        part = contract(left[0:64, u * 32 : u * 32 + 32], w1_ref[...], ((1,), (0,)))
        for q in range(4):
            side = lax.rem(q % 2 + core, 2)
            for s in range(4):
                at = s * 64 + 32 * (q // 2) + 16 * side + u
                block = (q * 4 + s) * 4
                for k in range(2):
                    tmp[k, pl.ds(at, 4, stride=4), :] = part[block : block + 4, k * 128 : k * 128 + 128]
    unit, inverse = standardized(x_ref[...])
    grad = (part_ref[...] + jnp.concatenate([tmp[0], tmp[1]], axis=1)) * scale_ref[...]
    mean = jnp.mean(grad, axis=-1, keepdims=True)
    along = jnp.mean(grad * unit, axis=-1, keepdims=True)
    out_ref[...] = inverse * (grad - mean - unit * along)


def call(kernel, name, outs, scratch, mib, flops, *args, far=(), copies=0):
    shapes = tuple(jax.ShapeDtypeStruct(*out) for out in outs)
    moved = sum(a.size * a.dtype.itemsize for a in args + tuple(far) + shapes)
    return pl.pallas_call(
        kernel,
        out_shape=shapes,
        in_specs=[VMEM] * len(args) + [HBM] * len(far),
        out_specs=(VMEM,) * len(outs),
        scratch_shapes=[pltpu.VMEM(*s) for s in scratch]
        + ([pltpu.SemaphoreType.DMA((copies,))] if copies else []),
        compiler_params=pltpu.CompilerParams(
            vmem_limit_bytes=mib * 1024 * 1024 if mib else None
        ),
        cost_estimate=pl.CostEstimate(flops=flops, bytes_accessed=moved, transcendentals=0),
        name=name,
    )(*args, *far)


def swap_cores(array):
    return lax.ppermute(array, "core", [(0, 1), (1, 0)])


def from_peer(array, axis, apart):
    return lax.ppermute(array, axis, [(i, i ^ apart) for i in range(4)])


def exchange(array, axes):
    return lax.all_to_all(array, axes, 0, 0, tiled=True)


def local(
    sequence_embedding,
    standardize_scale,
    standardize_offset,
    first_operand_matrix,
    first_operand_intercept,
    second_operand_matrix,
    second_operand_intercept,
    result_matrix,
    result_intercept,
    edge_incoming_sensitivity,
):
    x = sequence_embedding.reshape(256, 256)
    scale = standardize_scale.reshape(1, 256)
    w1 = first_operand_matrix.T
    w2 = second_operand_matrix.T
    small = 2 * 256 * 256 * 32 * 6
    step = 2 * 1024 * 1024 * 128 * 3
    offset = standardize_offset.reshape(1, 256)
    (right,) = call(
        project_right_kernel,
        "project_right",
        [((64, 128), f32)],
        [],
        None,
        small,
        x,
        scale,
        offset,
        w2,
        second_operand_intercept.reshape(1, 32),
    )
    (left,) = call(
        project_left_kernel,
        "project_left",
        [((8, 64, 128), f32)],
        [((256, 128), f32)],
        None,
        small,
        x,
        scale,
        offset,
        w1,
        first_operand_intercept.reshape(1, 32),
    )
    right = [right] + [from_peer(right, "zl", dz) for dz in (1, 2, 3)]
    left, right = lax.optimization_barrier((left, right))
    g_hi, g_lo = call(
        cotangent_kernel,
        "cotangent",
        [((4, 512, 512), bf16), ((4, 512, 512), bf16)],
        [
            ((4, 256, 1024), f32),
            ((4, 1024, 256), bf16),
            ((1024, 384), bf16),
            ((4, 256, 384), bf16),
            ((1024, 128), f32),
            ((16, 64, 128), f32),
        ],
        None,
        step,
        far=(result_matrix, edge_incoming_sensitivity),
        copies=2,
    )
    left = exchange(left, COL).reshape(32, 16, 128)
    right = jnp.stack(right)
    parts = [right] + [from_peer(right, "x", dx) for dx in (1, 2, 3)]
    left, parts, g_hi, g_lo = lax.optimization_barrier((left, parts, g_hi, g_lo))
    left = exchange(left, ROW).reshape(512, 128)
    parts = parts + [swap_cores(part) for part in parts]
    own_left, other_left = call(
        left_gradient_kernel,
        "left_gradient",
        [((256, 128), f32), ((256, 128), f32)],
        [((2048, 128), f32), ((4, 256, 512), bf16)] + [((4, 512, 512), bf16)] * 2,
        52,
        step,
        *parts,
        far=(g_hi, g_lo),
        copies=8,
    )
    got_left = swap_cores(other_left)
    left, own_left, got_left = lax.optimization_barrier((left, own_left, got_left))
    working = [
        ((2048, 128), f32),
        ((4, 512, 512), f32),
        ((4, 384, 512), bf16),
        ((4, 512, 384), bf16),
        ((4, 256, 1024), bf16),
        ((4, 256, 1024), bf16),
    ]
    own, other, *sums = call(
        tile_kernel,
        "tile",
        [((16 * BWD, 128), f32)] * 2 + [((4, 64, 128), f32)] * 8,
        working
        + [((4, 512, 256), bf16)]
        + [((4, 512, 512), bf16)] * 2
        + [((8, 128, 128), f32), ((16, 64, 128), f32)],
        51,
        3 * step,
        left,
        *parts,
        far=(g_hi, g_lo, edge_incoming_sensitivity),
        copies=9,
    )
    got = swap_cores(other)
    weight = (own + got).reshape(16, BWD, 128)
    sent = [weight, own_left.reshape(16, 16, 128), got_left.reshape(16, 16, 128)]
    back = exchange(jnp.concatenate(sent, axis=1), CHIP)
    order = (0, 2, 3, 1)
    sums = [sums[dx] + swap_cores(sums[4 + dx]) for dx in order]
    right = sums[0] + sum(from_peer(sums[k], "x", order[k]) for k in (1, 2, 3))
    (pair,) = call(
        pair_kernel,
        "pair",
        [((16, 64, 128), f32)],
        working + [((4, 1024, 256), bf16), ((1024, 128), f32)],
        52,
        2 * step,
        left,
        *parts,
        result_intercept.reshape(1, 128),
        far=(result_matrix,),
        copies=1,
    )
    weight = back[:, :32].sum(axis=0).reshape(4, 8, 128).transpose(1, 0, 2)
    sent = jnp.concatenate(
        [back[:, 32:].reshape(8, 64, 128), jnp.pad(weight, ((0, 0), (0, 4), (0, 0)))], axis=1
    )
    sent, right, pair = lax.optimization_barrier((sent, right, pair))
    cols = exchange(sent, COL)
    right = [right[0]] + [from_peer(right[dz], "zl", dz) for dz in (3, 2, 1)]
    (part,) = call(right_kernel, "right", [((256, 256), f32)], [], 8, small, w2, *right)
    grad, weight = call(
        finish_kernel,
        "finish",
        [((256, 256), f32), ((4, 128), f32)],
        [((2, 256, 128), f32)],
        8,
        small,
        x,
        scale,
        w1,
        part,
        cols,
    )
    return pair, grad.reshape(4, 64, 256), weight


def solution(mesh):
    fine = Mesh(mesh.devices.reshape(SIZES), NAMES)
    tile = P(ROW, COL, None)
    return jax.shard_map(
        local,
        mesh=fine,
        in_specs=(tile, P(), P(), P(), P(), P(), P(), P(), P(), tile),
        out_specs=(tile, tile, P(ROW + COL, None)),
        check_vma=False,
    )
```

```python
import jax
import jax.numpy as jnp
from jax import lax
from jax.experimental import pallas as pl
from jax.experimental.pallas import tpu as pltpu
from jax.sharding import Mesh, PartitionSpec as P

exact = lax.Precision.HIGHEST
f32 = jnp.float32
bf16 = jnp.bfloat16

SIZES = (4, 4, 2, 2, 4)
NAMES = ("zl", "x", "core", "zh", "y")
CHIP = ("zl", "x")
ROW = ("zl", "x", "core")
COL = ("zh", "y")
VMEM = pl.BlockSpec(memory_space=pltpu.VMEM)
HBM = pl.BlockSpec(memory_space=pltpu.HBM)

BWD = 32


def contract(a, b, dims):
    return lax.dot_general(a, b, (dims, ((), ())), precision=exact, preferred_element_type=f32)


def matmul(a, b):
    return lax.dot_general(a, b, (((1,), (0,)), ((), ())), preferred_element_type=f32)


def halves(v):
    high = v.astype(bf16)
    return high, (v - high.astype(f32)).astype(bf16)


def standardized(x):
    demeaned = x - jnp.mean(x, axis=-1, keepdims=True)
    variance = jnp.mean(demeaned * demeaned, axis=-1, keepdims=True)
    inverse = lax.rsqrt(variance + 1e-05)
    return demeaned * inverse, inverse


def project_right_kernel(x_ref, scale_ref, offset_ref, w2_ref, b2_ref, right_ref):
    normed = standardized(x_ref[...])[0] * scale_ref[...] + offset_ref[...]
    on = lax.broadcasted_iota(jnp.int32, (32, 32), 0) == lax.broadcasted_iota(jnp.int32, (32, 32), 1)
    b2 = jnp.sum(jnp.where(on, b2_ref[...], 0.0), axis=1, keepdims=True)
    right = contract(w2_ref[...], normed, ((1,), (1,))) + b2
    for s in range(4):
        cols = right[:, s * 64 : s * 64 + 64]
        right_ref[s * 16 : s * 16 + 16, :] = jnp.concatenate([cols[0:16], cols[16:32]], axis=1)


def project_left_kernel(x_ref, scale_ref, offset_ref, w1_ref, b1_ref, left_ref, tmp):
    normed = standardized(x_ref[...])[0] * scale_ref[...] + offset_ref[...]
    tmp[:, 0:32] = contract(normed, w1_ref[...], ((1,), (1,))) + b1_ref[...]
    wide = jnp.concatenate([tmp[pl.ds(u, 64, stride=4), :][:, 0:32] for u in range(4)], axis=1)
    for q in range(4):
        part = jnp.concatenate([wide[s * 16 + q * 4 : s * 16 + q * 4 + 4] for s in range(4)], axis=0)
        for copy in range(8):
            left_ref[copy, q * 16 : q * 16 + 16, :] = part


def fetch(pairs, sems):
    copies = [pltpu.make_async_copy(a, b, sems.at[i]) for i, (a, b) in enumerate(pairs)]
    for copy in copies:
        copy.start()
    return copies


def fetch_classes(hi_far, lo_far, g_hi, g_lo, sems):
    pairs = []
    for m in range(4):
        pairs += [(hi_far.at[m], g_hi.at[m]), (lo_far.at[m], g_lo.at[m])]
    return fetch(pairs, sems)


def pick(parts):
    chunk = lax.broadcasted_iota(jnp.int32, (64, 128), 1) // 32
    low = jnp.where(chunk == 0, parts[0], parts[1])
    return jnp.where(chunk < 2, low, jnp.where(chunk == 2, parts[2], parts[3]))


def chip_of(dz, dx):
    return jnp.bitwise_xor(lax.axis_index("zl"), dz) * 4 + jnp.bitwise_xor(lax.axis_index("x"), dx)


def left_rows(left_ref, quad):
    core = lax.axis_index("core")
    got = []
    for side in (core, 1 - core):
        for s in range(4):
            got.append(left_ref[pl.ds(side * 16 + s * 4 + quad, 16, stride=32), :])
    return jnp.concatenate(got, axis=0)


def gather_right(parts, right_all):
    for at, ref in enumerate(parts):
        for dz in range(4):
            start = (at // 4) * 1024 + chip_of(dz, at % 4) * 64
            right_all[pl.ds(pl.multiple_of(start, 64), 64), :] = ref[dz]


def right_rows(right_all, e):
    got = []
    for half in range(2):
        for s in range(4):
            got.append(right_all[pl.ds(half * 1024 + s * 16 + e, 16, stride=64), :])
    return jnp.concatenate(got, axis=0)


def left_turned(left_ref, lt):
    for quad in range(4):
        hi, lo = halves(left_rows(left_ref, quad).T)
        for p in range(4):
            for m in range(4):
                at = quad * 128 + ((p + m) % 4) * 32
                lt[m, at : at + 32, 0:128] = hi[p * 32 : p * 32 + 32]
                lt[m, at : at + 32, 128:256] = lo[p * 32 : p * 32 + 32]


def weights_by_class(w_ref, w_hl):
    for e in range(32):
        hi, lo = halves(w_ref[pl.ds(e, 32, stride=32), :])
        for d in range(4):
            at = (e // 4) * 128 + ((e % 4 + d) % 4) * 32
            w_hl[d, at : at + 32, 0:128] = hi
            w_hl[d, at : at + 32, 128:256] = lo


def cotangent_kernel(
    w_far, cot_far, hi_far, lo_far, wide_t, w_hl, w_cat, cot_cat, w_ref, cot_ref, g_hi, g_lo, sems
):
    copies = fetch([(w_far, w_ref), (cot_far, cot_ref)], sems)
    copies[0].wait()
    weights_by_class(w_ref, w_hl)
    copies[1].wait()
    for d in range(4):
        for quad in range(4):
            hi, lo = halves(cot_ref[quad * 4 + d])
            cot_cat[d, quad * 64 : quad * 64 + 64, 0:128] = hi
            cot_cat[d, quad * 64 : quad * 64 + 64, 128:256] = hi
            cot_cat[d, quad * 64 : quad * 64 + 64, 256:384] = lo
    for d in range(4):
        w_cat[:, 0:256] = w_hl[d]
        w_cat[:, 256:384] = w_hl[d, :, 0:128]
        wide_t[d] = lax.dot_general(
            cot_cat[d], w_cat[...], (((1,), (1,)), ((), ())), preferred_element_type=f32
        )
    sent = []
    for g in range(4):
        for h in range(2):
            block = h * 4 + g
            at = g * 128 + h * 64
            for quad in range(4):
                parts = [
                    wide_t[d, quad * 64 : quad * 64 + 64, block * 128 : block * 128 + 128]
                    for d in range(4)
                ]
                for m in range(4):
                    hi, lo = halves(pick([parts[(p - m) % 4] for p in range(4)]))
                    g_hi[m, at : at + 64, quad * 128 : quad * 128 + 128] = hi
                    g_lo[m, at : at + 64, quad * 128 : quad * 128 + 128] = lo
        slab = (slice(None), pl.ds(g * 128, 128))
        pairs = [(g_hi.at[slab], hi_far.at[slab]), (g_lo.at[slab], lo_far.at[slab])]
        sent += fetch(pairs, sems.at[pl.ds(2 + 2 * g, 2)])
    for copy in sent:
        copy.wait()


def outer_product(left_ref, parts, right_all, outer, lcat, rt, a_hi, a_lo):
    gather_right(parts, right_all)
    for quad in range(4):
        v = left_rows(left_ref, quad)
        for m in range(4):
            hi, lo = halves(pltpu.roll(v, 32 * m, axis=1) if m else v)
            lcat[m, 0:128, quad * 128 : quad * 128 + 128] = hi
            lcat[m, 128:256, quad * 128 : quad * 128 + 128] = lo
            lcat[m, 256:384, quad * 128 : quad * 128 + 128] = hi
    for e in range(16):
        g, m = e // 4, e % 4
        hi, lo = halves(right_rows(right_all, e).T)
        rt[m, g * 128 : g * 128 + 128, 0:128] = hi
        rt[m, g * 128 : g * 128 + 128, 128:256] = hi
        rt[m, g * 128 : g * 128 + 128, 256:384] = lo
    for m in range(4):
        outer[m] = matmul(rt[m], lcat[m])
    for block in range(8):
        h, g = block // 4, block % 4
        at = g * 128 + h * 64
        for quad in range(4):
            parts = [outer[m, at : at + 64, quad * 128 : quad * 128 + 128] for m in range(4)]
            for d in range(4):
                hi, lo = halves(pick([parts[(p - d) % 4] for p in range(4)]))
                a_hi[d, quad * 64 : quad * 64 + 64, block * 128 : block * 128 + 128] = hi
                a_lo[d, quad * 64 : quad * 64 + 64, block * 128 : block * 128 + 128] = lo


def pair_kernel(left_ref, *refs):
    parts, (bias_ref, w_far, pair_ref, right_all, outer, lcat, rt, a_hi, a_lo) = refs[:8], refs[8:17]
    w_hl, w_ref, sems = refs[17:]
    (fetched,) = fetch([(w_far, w_ref)], sems)
    outer_product(left_ref, parts, right_all, outer, lcat, rt, a_hi, a_lo)
    fetched.wait()
    weights_by_class(w_ref, w_hl)
    for d in range(4):
        both = matmul(a_hi[d], w_hl[d])
        pair = both[:, 0:128] + both[:, 128:256] + matmul(a_lo[d], w_hl[d, :, 0:128])
        pair = pair * (1.0 / 128) + bias_ref[...]
        for quad in range(4):
            pair_ref[quad * 4 + d] = pair[quad * 64 : quad * 64 + 64]


def tile_kernel(left_ref, *refs):
    parts, (cot_far, own_out, other_out) = refs[:8], refs[8:11]
    right_all, outer, lcat, rt, a_hi, a_lo, dw, cot_ref, sems = refs[11:]
    core = lax.axis_index("core")
    (fetched,) = fetch([(cot_far, cot_ref)], sems)
    outer_product(left_ref, parts, right_all, outer, lcat, rt, a_hi, a_lo)
    fetched.wait()
    for d in range(4):
        hi, lo = halves(jnp.concatenate([cot_ref[quad * 4 + d] for quad in range(4)], axis=0).T)
        both = matmul(jnp.concatenate([hi, lo], axis=0), a_hi[d])
        part = both[0:128] + both[128:256] + matmul(hi, a_lo[d])
        for block in range(8):
            v = part[:, block * 128 : block * 128 + 128]
            if d == 0:
                dw[block] = v
            else:
                dw[block] += pltpu.roll(v, 128 - 32 * d, axis=1)
    for block in range(8):
        dw[block] = dw[block].T
    for block in range(8):
        for p in range(4):
            for out, side in ((own_out, core), (other_out, 1 - core)):
                out[pl.ds(p * 8 + block, 16, stride=BWD), :] = dw[
                    block, pl.ds(p * 32 + side, 16, stride=2), :
                ]


def left_gradient_kernel(*refs):
    parts, (hi_far, lo_far, own_out, other_out, right_all, r_hl, g_hi, g_lo, sems) = refs[:8], refs[8:]
    copies = fetch_classes(hi_far, lo_far, g_hi, g_lo, sems)
    gather_right(parts, right_all)
    for e in range(16):
        g, m = e // 4, e % 4
        hi, lo = halves(right_rows(right_all, e))
        r_hl[m, 0:128, g * 128 : g * 128 + 128] = hi
        r_hl[m, 128:256, g * 128 : g * 128 + 128] = lo
    total = [None] * 4
    for m in range(4):
        copies[2 * m].wait()
        copies[2 * m + 1].wait()
        both = matmul(r_hl[m], g_hi[m])
        v = both[0:128] + both[128:256] + matmul(r_hl[m, 0:128, :], g_lo[m])
        for quad in range(4):
            part = v[:, quad * 128 : quad * 128 + 128]
            if m:
                part = pltpu.roll(part, 128 - 32 * m, axis=1)
            total[quad] = part if total[quad] is None else total[quad] + part
    for quad in range(4):
        t = total[quad] * (1.0 / 128)
        for half, out in ((0, own_out), (1, other_out)):
            for s in range(4):
                at = (half * 4 + s) * 16
                out[pl.ds(s * 4 + quad, 16, stride=16), :] = t[at : at + 16]


def right_gradient_kernel(left_ref, hi_far, lo_far, *refs):
    outs, (lt, total, g_hi, g_lo, sems) = refs[:8], refs[8:]
    copies = fetch_classes(hi_far, lo_far, g_hi, g_lo, sems)
    left_turned(left_ref, lt)
    for m in range(4):
        copies[2 * m].wait()
        copies[2 * m + 1].wait()
        both = matmul(g_hi[m], lt[m])
        v = both[:, 0:128] + both[:, 128:256] + matmul(g_lo[m], lt[m, :, 0:128])
        for g in range(4):
            t = v[g * 128 : g * 128 + 128].T * (1.0 / 128)
            for half in range(2):
                for s in range(4):
                    at = (half * 4 + s) * 16
                    row = half * 1024 + s * 16 + g * 4 + m
                    total[pl.ds(row, 16, stride=64), :] = t[at : at + 16]
    for at, ref in enumerate(outs):
        for dz in range(4):
            start = (at // 4) * 1024 + chip_of(dz, at % 4) * 64
            ref[dz] = total[pl.ds(pl.multiple_of(start, 64), 64), :]


def right_kernel(w2_ref, a_ref, b_ref, c_ref, d_ref, out_ref):
    total = (a_ref[...] + b_ref[...]) + (c_ref[...] + d_ref[...])
    for s in range(4):
        part = total[s * 16 : s * 16 + 16, :]
        entries = jnp.concatenate([part[:, 0:64], part[:, 64:128]], axis=0)
        out_ref[s * 64 : s * 64 + 64, :] = contract(entries, w2_ref[...], ((0,), (0,)))


def finish_kernel(x_ref, scale_ref, w1_ref, part_ref, col_ref, out_ref, weight_ref, tmp):
    core = lax.axis_index("core")
    left = col_ref[0]
    for c in range(1, 8):
        left = left + col_ref[c]
    weight_ref[...] = left[64:68] * (1.0 / 512)
    for u in range(4):
        part = contract(left[0:64, u * 32 : u * 32 + 32], w1_ref[...], ((1,), (0,)))
        for q in range(4):
            side = lax.rem(q % 2 + core, 2)
            for s in range(4):
                at = s * 64 + 32 * (q // 2) + 16 * side + u
                block = (q * 4 + s) * 4
                for k in range(2):
                    tmp[k, pl.ds(at, 4, stride=4), :] = part[block : block + 4, k * 128 : k * 128 + 128]
    unit, inverse = standardized(x_ref[...])
    grad = (part_ref[...] + jnp.concatenate([tmp[0], tmp[1]], axis=1)) * scale_ref[...]
    mean = jnp.mean(grad, axis=-1, keepdims=True)
    along = jnp.mean(grad * unit, axis=-1, keepdims=True)
    out_ref[...] = inverse * (grad - mean - unit * along)


def call(kernel, name, outs, scratch, mib, flops, *args, far=(), far_outs=0, copies=0):
    shapes = tuple(jax.ShapeDtypeStruct(*out) for out in outs)
    moved = sum(a.size * a.dtype.itemsize for a in args + tuple(far) + shapes)
    return pl.pallas_call(
        kernel,
        out_shape=shapes,
        in_specs=[VMEM] * len(args) + [HBM] * len(far),
        out_specs=(VMEM,) * (len(outs) - far_outs) + (HBM,) * far_outs,
        scratch_shapes=[pltpu.VMEM(*s) for s in scratch]
        + ([pltpu.SemaphoreType.DMA((copies,))] if copies else []),
        compiler_params=pltpu.CompilerParams(
            vmem_limit_bytes=mib * 1024 * 1024 if mib else None
        ),
        cost_estimate=pl.CostEstimate(flops=flops, bytes_accessed=moved, transcendentals=0),
        name=name,
    )(*args, *far)


def swap_cores(array):
    return lax.ppermute(array, "core", [(0, 1), (1, 0)])


def from_peer(array, axis, apart):
    return lax.ppermute(array, axis, [(i, i ^ apart) for i in range(4)])


def exchange(array, axes):
    return lax.all_to_all(array, axes, 0, 0, tiled=True)


def local(
    sequence_embedding,
    standardize_scale,
    standardize_offset,
    first_operand_matrix,
    first_operand_intercept,
    second_operand_matrix,
    second_operand_intercept,
    result_matrix,
    result_intercept,
    edge_incoming_sensitivity,
):
    x = sequence_embedding.reshape(256, 256)
    scale = standardize_scale.reshape(1, 256)
    w1 = first_operand_matrix.T
    w2 = second_operand_matrix.T
    small = 2 * 256 * 256 * 32 * 6
    step = 2 * 1024 * 1024 * 128 * 3
    offset = standardize_offset.reshape(1, 256)
    (right,) = call(
        project_right_kernel,
        "project_right",
        [((64, 128), f32)],
        [],
        None,
        small,
        x,
        scale,
        offset,
        w2,
        second_operand_intercept.reshape(1, 32),
    )
    (left,) = call(
        project_left_kernel,
        "project_left",
        [((8, 64, 128), f32)],
        [((256, 128), f32)],
        None,
        small,
        x,
        scale,
        offset,
        w1,
        first_operand_intercept.reshape(1, 32),
    )
    right = [right] + [from_peer(right, "zl", dz) for dz in (1, 2, 3)]
    left, right = lax.optimization_barrier((left, right))
    g_hi, g_lo = call(
        cotangent_kernel,
        "cotangent",
        [((4, 512, 512), bf16), ((4, 512, 512), bf16)],
        [
            ((4, 256, 1024), f32),
            ((4, 1024, 256), bf16),
            ((1024, 384), bf16),
            ((4, 256, 384), bf16),
            ((1024, 128), f32),
            ((16, 64, 128), f32),
        ]
        + [((4, 512, 512), bf16)] * 2,
        None,
        step,
        far=(result_matrix, edge_incoming_sensitivity),
        far_outs=2,
        copies=10,
    )
    left = exchange(left, COL).reshape(32, 16, 128)
    right = jnp.stack(right)
    parts = [right] + [from_peer(right, "x", dx) for dx in (1, 2, 3)]
    left, parts, g_hi, g_lo = lax.optimization_barrier((left, parts, g_hi, g_lo))
    left = exchange(left, ROW).reshape(512, 128)
    parts = parts + [swap_cores(part) for part in parts]
    own_left, other_left = call(
        left_gradient_kernel,
        "left_gradient",
        [((256, 128), f32), ((256, 128), f32)],
        [((2048, 128), f32), ((4, 256, 512), bf16)] + [((4, 512, 512), bf16)] * 2,
        52,
        step,
        *parts,
        far=(g_hi, g_lo),
        copies=8,
    )
    got_left = swap_cores(other_left)
    left, own_left, got_left = lax.optimization_barrier((left, own_left, got_left))
    working = [
        ((2048, 128), f32),
        ((4, 512, 512), f32),
        ((4, 384, 512), bf16),
        ((4, 512, 384), bf16),
        ((4, 256, 1024), bf16),
        ((4, 256, 1024), bf16),
    ]
    own, other = call(
        tile_kernel,
        "tile",
        [((16 * BWD, 128), f32)] * 2,
        working + [((8, 128, 128), f32), ((16, 64, 128), f32)],
        52,
        2 * step,
        left,
        *parts,
        far=(edge_incoming_sensitivity,),
        copies=1,
    )
    got = swap_cores(other)
    sums = call(
        right_gradient_kernel,
        "right_gradient",
        [((4, 64, 128), f32)] * 8,
        [((4, 512, 256), bf16), ((2048, 128), f32)] + [((4, 512, 512), bf16)] * 2,
        52,
        step,
        left,
        far=(g_hi, g_lo),
        copies=8,
    )
    weight = (own + got).reshape(16, BWD, 128)
    sent = [weight, own_left.reshape(16, 16, 128), got_left.reshape(16, 16, 128)]
    back = exchange(jnp.concatenate(sent, axis=1), CHIP)
    sums = [a + swap_cores(b) for a, b in zip(sums[:4], sums[4:])]
    right = sums[0] + sum(from_peer(sums[dx], "x", dx) for dx in (1, 2, 3))
    (pair,) = call(
        pair_kernel,
        "pair",
        [((16, 64, 128), f32)],
        working + [((4, 1024, 256), bf16), ((1024, 128), f32)],
        52,
        2 * step,
        left,
        *parts,
        result_intercept.reshape(1, 128),
        far=(result_matrix,),
        copies=1,
    )
    weight = back[:, :32].sum(axis=0).reshape(4, 8, 128).transpose(1, 0, 2)
    sent = jnp.concatenate(
        [back[:, 32:].reshape(8, 64, 128), jnp.pad(weight, ((0, 0), (0, 4), (0, 0)))], axis=1
    )
    sent, right, pair = lax.optimization_barrier((sent, right, pair))
    cols = exchange(sent, COL)
    right = [right[0]] + [from_peer(right[dz], "zl", dz) for dz in (1, 2, 3)]
    (part,) = call(right_kernel, "right", [((256, 256), f32)], [], 8, small, w2, *right)
    grad, weight = call(
        finish_kernel,
        "finish",
        [((256, 256), f32), ((4, 128), f32)],
        [((2, 256, 128), f32)],
        8,
        small,
        x,
        scale,
        w1,
        part,
        cols,
    )
    return pair, grad.reshape(4, 64, 256), weight


def solution(mesh):
    fine = Mesh(mesh.devices.reshape(SIZES), NAMES)
    tile = P(ROW, COL, None)
    return jax.shard_map(
        local,
        mesh=fine,
        in_specs=(tile, P(), P(), P(), P(), P(), P(), P(), P(), tile),
        out_specs=(tile, tile, P(ROW + COL, None)),
        check_vma=False,
    )
```
